32 devices in a mesh: mod: 8 (over z, y), dp: 4 (over x, core).
Axes of the slice: x: 2, y: 2, z: 4, core: 2. Of those that a mesh axis runs over, the one named last changes fastest.
Arguments:
- token_ids: int32 [2, 192, 32], P(None, 'mod'), may hold values from 0 to 31999
- targets: int32 [2, 192, 4], P(None, 'mod'), may hold values from 0 to 31999
- positions: int32 [2, 192, 4], P(None, 'mod'), may hold values from 0 to 31, as said below
- loss_mask: int32 [2, 192, 4], P(None, 'mod'), may hold values 0 or 1
- paths: int32 [2, 192], P(None, 'mod'), may hold values from 0 to 7, as said below
- attend: float32 [8, 896, 2688], P('mod', 'dp'), may hold values from -0.1875 to 0.1875
- output: float32 [8, 896, 896], P('mod', 'dp'), may hold values from -0.0625 to 0.0625
- widen: float32 [8, 896, 3584], P('mod', 'dp'), may hold values from -0.1875 to 0.1875
- narrow: float32 [8, 3584, 896], P('mod', 'dp'), may hold values from -0.009765625 to 0.009765625
- gains: float32 [8, 1792], P('mod', 'dp'), may hold values from 0.5 to 1.5
- table: float32 [32000, 896], P(('mod', 'dp')), may hold values from -0.2338536 to 0.2338536
- final_gain: float32 [896], P('mod'), may hold values from 0.5 to 1.5
- first_attend: float32 [8, 896, 2688], P('mod', 'dp'), may hold values from -7.6293945e-05 to 7.6293945e-05
- first_output: float32 [8, 896, 896], P('mod', 'dp'), may hold values from -7.6293945e-05 to 7.6293945e-05
- first_widen: float32 [8, 896, 3584], P('mod', 'dp'), may hold values from -2.3841858e-06 to 2.3841858e-06
- first_narrow: float32 [8, 3584, 896], P('mod', 'dp'), may hold values from -7.6293945e-05 to 7.6293945e-05
- first_gains: float32 [8, 1792], P('mod', 'dp'), may hold values from -7.6293945e-05 to 7.6293945e-05
- first_table: float32 [32000, 896], P(('mod', 'dp')), may hold values from -7.6293945e-05 to 7.6293945e-05
- first_final: float32 [896], P('mod'), may hold values from -7.6293945e-05 to 7.6293945e-05
- second_attend: float32 [8, 896, 2688], P('mod', 'dp'), may hold values from 2.3638971e-11 to 9.4555884e-11
- second_output: float32 [8, 896, 896], P('mod', 'dp'), may hold values from 2.3638971e-11 to 9.4555884e-11
- second_widen: float32 [8, 896, 3584], P('mod', 'dp'), may hold values from 6.08535e-14 to 2.4523054e-13
- second_narrow: float32 [8, 3584, 896], P('mod', 'dp'), may hold values from 2.3638971e-11 to 9.4555884e-11
- second_gains: float32 [8, 1792], P('mod', 'dp'), may hold values from 2.3638971e-11 to 9.4555884e-11
- second_table: float32 [32000, 896], P(('mod', 'dp')), may hold values from 2.3638971e-11 to 9.4555884e-11
- second_final: float32 [896], P('mod'), may hold values from 2.3638971e-11 to 9.4555884e-11
Outputs:
- loss: float32 [], replicated
- gradient_norm: float32 [], replicated
- new_attend: float32 [8, 896, 2688], P('mod', 'dp')
- new_output: float32 [8, 896, 896], P('mod', 'dp')
- new_widen: float32 [8, 896, 3584], P('mod', 'dp')
- new_narrow: float32 [8, 3584, 896], P('mod', 'dp')
- new_gains: float32 [8, 1792], P('mod', 'dp')
- new_table: float32 [32000, 896], P(('mod', 'dp'))
- new_final: float32 [896], P('mod')
- mean_attend: float32 [8, 896, 2688], P('mod', 'dp')
- mean_output: float32 [8, 896, 896], P('mod', 'dp')
- mean_widen: float32 [8, 896, 3584], P('mod', 'dp')
- mean_narrow: float32 [8, 3584, 896], P('mod', 'dp')
- mean_gains: float32 [8, 1792], P('mod', 'dp')
- mean_table: float32 [32000, 896], P(('mod', 'dp'))
- mean_final: float32 [896], P('mod')
- square_attend: float32 [8, 896, 2688], P('mod', 'dp')
- square_output: float32 [8, 896, 896], P('mod', 'dp')
- square_widen: float32 [8, 896, 3584], P('mod', 'dp')
- square_narrow: float32 [8, 3584, 896], P('mod', 'dp')
- square_gains: float32 [8, 1792], P('mod', 'dp')
- square_table: float32 [32000, 896], P(('mod', 'dp'))
- square_final: float32 [896], P('mod')
The draws below stay inside these ranges and needn't reach their ends.
Inputs may be any that keep to these rules, and one draw needn't show every extreme that they name: Within one sequence the 4 positions differ. `paths`: the 6 sequences of one device (aligned blocks of rows of a micro-batch) name 6 different modules.
All inputs are finite; a program needn't handle non-finite values. No bound on the sum of `loss_mask` on one device may be relied on, other than what follows from the above.
Results may differ from the reference program's by a relative error of at most 0.0095.
Values may be sent and summed in bfloat16 or wider, within the bound.
A program may use at most 384 MiB of HBM per device.

```python
import math
import jax
import jax.numpy as jnp
import numpy as np
from jax import lax

D = 896
HEADS = 14
HEAD_DIM = 64
FF = 3584
VOCAB = 32000
SEQ_LEN = 32
MB = 2
POS_SEQ = 4
MODULES = 8
SEQ_DEV = 6
SEQS = 192
PARAMS = 105757568
DEVICES = 32


def draw_paths(key, part):
    streams = jax.random.split(key, MB * DEVICES)
    orders = jax.vmap(lambda single: jax.random.permutation(single, MODULES))(streams)
    return orders[:, :SEQ_DEV].reshape(MB, SEQS).astype(jnp.int32)


def draw_positions(key, part):
    streams = jax.random.split(jax.random.fold_in(key, 7), MB * SEQS)
    orders = jax.vmap(lambda single: jax.random.permutation(single, SEQ_LEN))(streams)
    return orders[:, :POS_SEQ].reshape(MB, SEQS, POS_SEQ).astype(jnp.int32)


def draw_table(key, part):
    noise_key = jax.random.fold_in(key, 11)
    shift_key = jax.random.fold_in(key, 12)
    pick_key = jax.random.fold_in(key, 13)
    noise_part = jax.random.normal(noise_key, (VOCAB, D), jnp.float32) * (2.0 / D ** 0.5)
    shared_shift = jnp.clip(jax.random.normal(shift_key, (D,), jnp.float32), -2.0, 2.0) * (1.5 / D ** 0.5)
    cluster_rows = jax.random.permutation(pick_key, VOCAB)[:max(VOCAB // 128, 2)]
    tilt_scale = jnp.ones((VOCAB,), jnp.float32).at[cluster_rows].set(1.27)
    bound_value = 7.0 / D ** 0.5
    return jnp.clip(noise_part + tilt_scale[:, None] * shared_shift[None, :], -bound_value, bound_value)


def plant(values, rng, low, high):
    longest = values.shape.index(max(values.shape))
    spots = []
    for shift in (0, 1):
        where = [jax.random.randint(jax.random.fold_in(rng, axis), (), 0, length) for axis, length in enumerate(values.shape)]
        where[longest] = (where[longest] + shift) % values.shape[longest]
        spots.append(tuple(where))
    return values.at[spots[0]].set(low).at[spots[1]].set(high)


def shard_levels(own_key, shape, cuts, low, high):
    level = 1.0
    for dim, shards_of in cuts:
        steps = jax.random.uniform(jax.random.fold_in(jax.random.fold_in(own_key, 6), dim), (shards_of,), jnp.float32, low / len(cuts), high / len(cuts))
        level = level * jnp.repeat(jnp.exp(steps), shape[dim] // shards_of).reshape((-1,) + (1,) * (len(shape) - 1 - dim))
    return level


def cumulative_ranks(amount, skew):
    weights = [(1 << 20) // math.isqrt(grade ** skew) + 1 for grade in range(1, amount + 1)]
    scale = 1 + sum(weights) // (1 << 30)
    return np.cumsum(np.array([max(1, weight // scale) for weight in weights]))


def skewed_ids(own_key, shape, count, slope):
    table = cumulative_ranks(count, slope)
    lot = jax.random.randint(jax.random.fold_in(own_key, 1), shape, 0, int(table[count - 1]))
    grade = jnp.searchsorted(jnp.asarray(table, jnp.int32), lot, side="right")
    return jax.random.permutation(jax.random.fold_in(own_key, 2), count)[grade].astype(jnp.int32)


def bell_draw(key, extent, spread, bound, shards=(), held_as=jnp.bfloat16):
    array = jax.random.normal(key, extent, jnp.float32) * spread
    if len(shards) > 0:
        array = shard_levels(key, extent, shards, -0.22, 0.18) * array
    return jnp.clip(array, min=-bound, max=bound).astype(held_as)


def setup_inputs(seed: int = 0) -> dict:
    arg_keys = jax.random.split(jax.random.key(seed), 27)
    return {
        "token_ids": plant(skewed_ids(arg_keys[0], (MB, SEQS, SEQ_LEN), VOCAB, 2), jax.random.fold_in(arg_keys[0], 3), 0, VOCAB - 1).astype(jnp.int32),
        "targets": plant(skewed_ids(arg_keys[1], (MB, SEQS, POS_SEQ), VOCAB, 2), jax.random.fold_in(arg_keys[1], 3), 0, VOCAB - 1).astype(jnp.int32),
        "positions": draw_positions(jax.random.fold_in(arg_keys[26], 71), 0),
        "loss_mask": plant((jax.random.randint(arg_keys[3], (MB, SEQS, POS_SEQ), 0, 4) < 3).astype(jnp.int32), jax.random.fold_in(arg_keys[3], 1), 0, 1),
        "paths": draw_paths(jax.random.fold_in(arg_keys[26], 71), 0),
        "attend": bell_draw(arg_keys[5], (MODULES, D, 3 * D), D ** -0.5, 0.1875, ((0, 8), (1, 4)), jnp.float32),
        "output": bell_draw(arg_keys[6], (MODULES, D, D), (12 * D) ** -0.5, 0.0625, ((0, 8), (1, 4)), jnp.float32),
        "widen": bell_draw(arg_keys[7], (MODULES, D, FF), D ** -0.5, 0.1875, ((0, 8), (1, 4)), jnp.float32),
        "narrow": bell_draw(arg_keys[8], (MODULES, FF, D), (100 * FF) ** -0.5, 0.009765625, ((0, 8), (1, 4)), jnp.float32),
        "gains": jnp.clip(1.0 + 0.1 * jax.random.normal(arg_keys[9], (MODULES, 2 * D), jnp.float32), 0.5, 1.5),
        "table": draw_table(jax.random.fold_in(arg_keys[26], 71), 0),
        "final_gain": jnp.clip(1.0 + 0.1 * jax.random.normal(arg_keys[11], (D,), jnp.float32), 0.5, 1.5),
        "first_attend": bell_draw(arg_keys[12], (MODULES, D, 3 * D), (0.05 / PARAMS ** 0.5), 7.62939453125e-05, ((0, 8), (1, 4)), jnp.float32),
        "first_output": bell_draw(arg_keys[13], (MODULES, D, D), (0.05 / PARAMS ** 0.5), 7.62939453125e-05, ((0, 8), (1, 4)), jnp.float32),
        "first_widen": bell_draw(arg_keys[14], (MODULES, D, FF), (0.00058 / (MB * SEQS * POS_SEQ * MODULES * D) ** 0.5), 2.384185791015625e-06, ((0, 8), (1, 4)), jnp.float32),
        "first_narrow": bell_draw(arg_keys[15], (MODULES, FF, D), (0.05 / PARAMS ** 0.5), 7.62939453125e-05, ((0, 8), (1, 4)), jnp.float32),
        "first_gains": bell_draw(arg_keys[16], (MODULES, 2 * D), (0.05 / PARAMS ** 0.5), 7.62939453125e-05, ((0, 8), (1, 4)), jnp.float32),
        "first_table": bell_draw(arg_keys[17], (VOCAB, D), (0.05 / PARAMS ** 0.5), 7.62939453125e-05, ((0, 32),), jnp.float32),
        "first_final": bell_draw(arg_keys[18], (D,), (0.05 / PARAMS ** 0.5), 7.62939453125e-05, ((0, 8),), jnp.float32),
        "second_attend": jnp.clip(jnp.exp(math.log(9.455588395601566e-11) - 1.3862944 * jax.random.uniform(arg_keys[19], (MODULES, D, 3 * D), jnp.float32) ** shard_levels(arg_keys[19], (MODULES, D, 3 * D), ((0, 8), (1, 4)), -0.2, 0.2)), 2.3638970989003916e-11, 9.455588395601566e-11),
        "second_output": jnp.clip(jnp.exp(math.log(9.455588395601566e-11) - 1.3862944 * jax.random.uniform(arg_keys[20], (MODULES, D, D), jnp.float32) ** shard_levels(arg_keys[20], (MODULES, D, D), ((0, 8), (1, 4)), -0.2, 0.2)), 2.3638970989003916e-11, 9.455588395601566e-11),
        "second_widen": jnp.clip(jnp.exp(math.log(2.4523053943417694e-13) - 1.39372936 * jax.random.uniform(arg_keys[21], (MODULES, D, FF), jnp.float32) ** shard_levels(arg_keys[21], (MODULES, D, FF), ((0, 8), (1, 4)), -0.2, 0.2)), 6.085350322607153e-14, 2.4523053943417694e-13),
        "second_narrow": jnp.clip(jnp.exp(math.log(9.455588395601566e-11) - 1.3862944 * jax.random.uniform(arg_keys[22], (MODULES, FF, D), jnp.float32) ** shard_levels(arg_keys[22], (MODULES, FF, D), ((0, 8), (1, 4)), -0.2, 0.2)), 2.3638970989003916e-11, 9.455588395601566e-11),
        "second_gains": jnp.clip(jnp.exp(math.log(9.455588395601566e-11) - 1.3862944 * jax.random.uniform(arg_keys[23], (MODULES, 2 * D), jnp.float32) ** shard_levels(arg_keys[23], (MODULES, 2 * D), ((0, 8), (1, 4)), -0.2, 0.2)), 2.3638970989003916e-11, 9.455588395601566e-11),
        "second_table": jnp.clip(jnp.exp(math.log(9.455588395601566e-11) - 1.3862944 * jax.random.uniform(arg_keys[24], (VOCAB, D), jnp.float32) ** shard_levels(arg_keys[24], (VOCAB, D), ((0, 32),), -0.2, 0.2)), 2.3638970989003916e-11, 9.455588395601566e-11),
        "second_final": jnp.clip(jnp.exp(math.log(9.455588395601566e-11) - 1.3862944 * jax.random.uniform(arg_keys[25], (D,), jnp.float32) ** shard_levels(arg_keys[25], (D,), ((0, 8),), -0.2, 0.2)), 2.3638970989003916e-11, 9.455588395601566e-11),
    }


NORM_EPS = 1e-05
CLIP_LIMIT = 0.05
BETA_ONE = 0.5
BETA_TWO = 0.5
ADAM_STEP = 10.0
ADAM_EPS = 1e-08
RATE_MATRIX = 0.03
RATE_GAIN = 0.3
DECAY_MATRIX = 0.1
TOP_PRECISION = lax.Precision.HIGHEST

@jax.custom_vjp
def low(v):
    return lax.optimization_barrier(v.astype(jnp.bfloat16)).astype(jnp.float32)

@jax.custom_vjp
def lower_backward(v):
    return v

def low_keep(v):
    return (low(v), None)

def low_pass(kept, grad):
    return (grad,)

def back_keep(v):
    return (v, None)

def back_low(kept, grad):
    return (low(grad),)
low.defvjp(low_keep, low_pass)
lower_backward.defvjp(back_keep, back_low)

def rms_scale(values, gain):
    return values * lax.rsqrt(lax.optimization_barrier(jnp.mean(values * values, axis=-1, keepdims=True)) + NORM_EPS) * gain

def rotate(values):
    length = values.shape[-3]
    half = values.shape[-1] // 2
    inverse = 10000.0 ** (-jnp.arange(half, dtype=jnp.float32) / half)
    angle = jnp.arange(length, dtype=jnp.float32)[:, None] * inverse[None, :]
    cosine = jnp.cos(angle)[:, None, :]
    sine = jnp.sin(angle)[:, None, :]
    first, second = (values[..., :half], values[..., half:])
    return jnp.concatenate([first * cosine - second * sine, first * sine + second * cosine], axis=-1)

def module_apply(layer_input, attend, output, widen, narrow, gains):
    count, length, width = layer_input.shape
    normed_first = low(rms_scale(layer_input, gains[:width]))
    mixed_heads = lower_backward(jnp.einsum('qtb,bu->qtu', normed_first, attend, precision=TOP_PRECISION))
    shape = (count, length, HEADS, HEAD_DIM)
    queries = low(rotate(mixed_heads[..., :width].reshape(shape)))
    keys_in = low(rotate(mixed_heads[..., width:2 * width].reshape(shape)))
    values = low(mixed_heads[..., 2 * width:].reshape(shape))
    raw = lower_backward(jnp.einsum('sqhe,skhe->shqk', queries, keys_in, precision=TOP_PRECISION))
    causal = jnp.arange(length)[:, None] >= jnp.arange(length)[None, :]
    scores = jnp.where(causal, raw * HEAD_DIM ** (-0.5), -1e+30)
    weights = low(jax.nn.softmax(scores, axis=-1))
    head_outputs = jnp.einsum('shqk,skhe->sqhe', weights, values, precision=TOP_PRECISION).reshape(count, length, width)
    head_outputs = low(lower_backward(head_outputs))
    middle_hidden = layer_input + lower_backward(jnp.einsum('qtb,bu->qtu', head_outputs, output, precision=TOP_PRECISION))
    normed_second = low(rms_scale(middle_hidden, gains[width:]))
    upper_hidden = lower_backward(jnp.einsum('uvr,re->uve', normed_second, widen, precision=TOP_PRECISION))
    activation_output = low(jax.nn.gelu(upper_hidden, approximate=True))
    return middle_hidden + lower_backward(jnp.einsum('tnc,ci->tni', activation_output, narrow, precision=TOP_PRECISION))

def head_block(pack):
    picked, table_low, target_block, mask_block = pack
    logits = lower_backward(jnp.dot(picked, table_low.T, precision=TOP_PRECISION))
    log_total = jax.scipy.special.logsumexp(logits, axis=-1)
    chosen = jnp.take_along_axis(logits, target_block[:, None], axis=1)[:, 0]
    return jnp.sum(mask_block * (log_total - chosen))

def total_loss(params, token_ids, targets, positions, loss_mask, paths):
    attend, output, widen, narrow, gains, table, final_gain = [low(w) for w in params]
    summed = jnp.float32(0.0)
    module_fn = jax.checkpoint(lambda pack: module_apply(*pack))
    for batch in range(MB):
        token_embedding = jnp.take(table, token_ids[batch], axis=0)
        layer_input = low(lower_backward(token_embedding))
        order = jnp.arange(SEQS, dtype=jnp.int32)
        slots = paths[batch] * DEVICES + order // SEQ_DEV
        source = jnp.zeros((MODULES * DEVICES,), jnp.int32).at[slots].set(order)
        live = jnp.zeros((MODULES * DEVICES,), jnp.float32).at[slots].set(1.0)
        buffer = (jnp.take(layer_input, source, axis=0) * live[:, None, None]).reshape(MODULES, DEVICES, SEQ_LEN, D)
        results = lax.map(module_fn, (buffer, attend, output, widen, narrow, gains))
        returned_rows = jnp.take(results.reshape(MODULES * DEVICES, SEQ_LEN, D), slots, axis=0)
        returned_rows = low(lower_backward(returned_rows))
        final = rms_scale(returned_rows, final_gain)
        picked = low(jnp.take_along_axis(final, positions[batch][:, :, None], axis=1))
        picked = picked.reshape(DEVICES, -1, D)
        target_rows = targets[batch].reshape(DEVICES, -1)
        mask_rows = loss_mask[batch].reshape(DEVICES, -1).astype(jnp.float32)
        head_fn = jax.checkpoint(lambda pack: head_block((pack[0], table, pack[1], pack[2])))
        summed = summed + jnp.sum(lax.map(head_fn, (picked, target_rows, mask_rows)))
    return summed

def adam_step(weight, grad, first, second, rate, decay):
    mean = BETA_ONE * first + (1.0 - BETA_ONE) * grad
    square = BETA_TWO * second + (1.0 - BETA_TWO) * grad * grad
    mean_hat = mean / (1.0 - BETA_ONE ** ADAM_STEP)
    square_hat = square / (1.0 - BETA_TWO ** ADAM_STEP)
    return (weight - rate * (mean_hat / (jnp.sqrt(square_hat) + ADAM_EPS) + decay * weight), mean, square)

def reference(token_ids, targets, positions, loss_mask, paths, attend, output, widen, narrow, gains, table, final_gain, first_attend, first_output, first_widen, first_narrow, first_gains, first_table, first_final, second_attend, second_output, second_widen, second_narrow, second_gains, second_table, second_final):
    params = (attend, output, widen, narrow, gains, table, final_gain)
    summed, back_fn = jax.vjp(lambda p: total_loss(p, token_ids, targets, positions, loss_mask, paths), params)
    count = jnp.sum(loss_mask.astype(jnp.float32))
    grads = back_fn(jnp.float32(1.0))[0]
    grads = [g / count for g in grads]
    gradient_norm = jnp.sqrt(sum((jnp.sum(g * g) for g in grads)))
    factor = CLIP_LIMIT / jnp.maximum(gradient_norm, CLIP_LIMIT)
    firsts = (first_attend, first_output, first_widen, first_narrow, first_gains, first_table, first_final)
    seconds = (second_attend, second_output, second_widen, second_narrow, second_gains, second_table, second_final)
    rates = (RATE_MATRIX, RATE_MATRIX, RATE_MATRIX, RATE_MATRIX, RATE_GAIN, RATE_MATRIX, RATE_GAIN)
    decays = (DECAY_MATRIX, DECAY_MATRIX, DECAY_MATRIX, DECAY_MATRIX, 0.0, DECAY_MATRIX, 0.0)
    updated = [adam_step(w, g * factor, f, s, r, d) for w, g, f, s, r, d in zip(params, grads, firsts, seconds, rates, decays)]
    loss = summed / count
    return (loss, gradient_norm, updated[0][0], updated[1][0], updated[2][0], updated[3][0], updated[4][0], updated[5][0], updated[6][0], updated[0][1], updated[1][1], updated[2][1], updated[3][1], updated[4][1], updated[5][1], updated[6][1], updated[0][2], updated[1][2], updated[2][2], updated[3][2], updated[4][2], updated[5][2], updated[6][2])
```

```python
import jax
import jax.numpy as jnp
from jax import lax
from jax.sharding import PartitionSpec as P

HEAD_DIM = 64


NORM_EPS = 1e-05
CLIP_LIMIT = 0.05
BETA_ONE = 0.5
BETA_TWO = 0.5
ADAM_STEP = 10.0
ADAM_EPS = 1e-08
RATE_MATRIX = 0.03
RATE_GAIN = 0.3
DECAY_MATRIX = 0.1


def rms_scale(values, gain):
    return values * lax.rsqrt(jnp.mean(values * values, axis=-1, keepdims=True) + NORM_EPS) * gain


def rotary_tables(length):
    half = HEAD_DIM // 2
    inverse = 10000.0 ** (-jnp.arange(half, dtype=jnp.float32) / half)
    angle = jnp.arange(length, dtype=jnp.float32)[:, None] * inverse[None, :]
    return jnp.cos(angle), jnp.sin(angle)


def rotate(values, cosine, sine):
    half = values.shape[-1] // 2
    first, second = (values[..., :half], values[..., half:])
    return jnp.concatenate(
        [first * cosine - second * sine, first * sine + second * cosine], axis=-1
    )


def product(left, right):
    return jnp.dot(left, right, preferred_element_type=jnp.float32)


def left_product(left, right):
    return lax.dot_general(
        left, right, (((0,), (0,)), ((), ())), preferred_element_type=jnp.float32
    )


def right_product(left, right):
    return lax.dot_general(
        left, right, (((1,), (1,)), ((), ())), preferred_element_type=jnp.float32
    )


def adam_step(weight, grad, first, second, rate, decay):
    mean = BETA_ONE * first + (1.0 - BETA_ONE) * grad
    square = BETA_TWO * second + (1.0 - BETA_TWO) * grad * grad
    mean_hat = mean / (1.0 - BETA_ONE**ADAM_STEP)
    square_hat = square / (1.0 - BETA_TWO**ADAM_STEP)
    return (
        weight - rate * (mean_hat / (jnp.sqrt(square_hat) + ADAM_EPS) + decay * weight),
        mean,
        square,
    )


def one_hot(index, extent):
    return (index[..., None] == jnp.arange(extent, dtype=jnp.int32)).astype(jnp.bfloat16)


def distinct_ranks(shard, row, counted, shard_rows):
    key = jnp.where(counted, shard * shard_rows + row, -1)
    place = jnp.arange(key.shape[0], dtype=jnp.int32)
    repeated = jnp.any(
        (key[:, None] == key[None, :]) & (place[None, :] < place[:, None]), axis=1
    )
    leading = counted & ~repeated
    rank = jnp.sum(
        (
            leading[None, :]
            & (shard[None, :] == shard[:, None])
            & (key[None, :] < key[:, None])
        ).astype(jnp.int32),
        axis=1,
    )
    return leading, rank


def on_device(
    token_ids,
    targets,
    positions,
    loss_mask,
    paths,
    attend,
    output,
    widen,
    narrow,
    gains,
    table,
    final_gain,
    first_attend,
    first_output,
    first_widen,
    first_narrow,
    first_gains,
    first_table,
    first_final,
    second_attend,
    second_output,
    second_widen,
    second_narrow,
    second_gains,
    second_table,
    second_final,
):
    group_dp = lax.axis_size("dp")
    group_mod = lax.axis_size("mod")
    dp_place = lax.axis_index("dp")
    mod_place = lax.axis_index("mod")
    sources = group_mod * group_dp
    micro, per_mod, length = token_ids.shape
    spots_seq = positions.shape[2]
    seq_dev = per_mod // group_dp
    shard_rows, width = table.shape
    heads = width // HEAD_DIM
    slots = micro * sources
    slots_local = slots // group_dp
    low = jnp.bfloat16

    mixing = lax.all_gather(
        jnp.concatenate([attend[0], output[0]], axis=1).astype(low), "dp", axis=0, tiled=True
    )
    attend_low, output_low = mixing[:, : 3 * width], mixing[:, 3 * width :]
    widen_low = lax.all_to_all(
        widen[0].astype(low), "dp", split_axis=1, concat_axis=0, tiled=True
    )
    narrow_low = narrow[0].astype(low)
    table_low = table.astype(low)
    gain_rows = lax.all_gather(
        jnp.concatenate([gains[0], final_gain]).astype(low), ("mod", "dp"), axis=0, tiled=False
    ).reshape(group_mod, group_dp, -1)
    gain_part = gains.shape[1]
    own_gains = lax.dynamic_index_in_dim(gain_rows, mod_place, 0, keepdims=False)
    own_gains = own_gains[:, :gain_part].reshape(-1).astype(jnp.float32)
    gain_one, gain_two = own_gains[:width], own_gains[width:]
    gain_final = gain_rows[:, 0, gain_part:].reshape(-1).astype(jnp.float32)

    fields = jnp.concatenate(
        [token_ids, positions, targets, loss_mask, paths[..., None]], axis=-1
    )
    fields = lax.all_gather(fields, "mod", axis=1, tiled=True)
    fields = fields.reshape(micro, sources, seq_dev, -1)
    routes = fields[..., -1]
    own_match = routes == mod_place
    own = jnp.sum(jnp.where(own_match[..., None], fields[..., : length + spots_seq], 0), axis=2)
    own_tokens = own[..., :length].reshape(-1)
    own_spots = own[..., length:].reshape(slots, spots_seq)
    own_live = jnp.any(own_match, axis=2).reshape(slots)
    match = routes[None] == jnp.arange(group_mod, dtype=jnp.int32)[:, None, None, None]
    scoring = jnp.sum(
        jnp.where(match[..., None], fields[None, ..., length + spots_seq : -1], 0), axis=3
    )
    wanted = scoring[..., :spots_seq].reshape(-1)
    counted = scoring[..., spots_seq:].reshape(-1).astype(jnp.float32)
    count_total = jnp.sum(counted)

    owner = own_tokens // shard_rows
    row = own_tokens % shard_rows
    shard = owner // group_dp
    held = jnp.repeat(own_live, length) & (owner % group_dp == dp_place)
    leading, rank = distinct_ranks(shard, row, held, shard_rows)
    expected = -(-slots * seq_dev * length // (group_mod * sources))
    cap = min(-(-2 * expected // 16) * 16, -(-shard_rows // 16) * 16)
    rounds = lax.pmax(jnp.max(jnp.where(leading, rank // cap, 0)) + 1, ("mod", "dp"))

    def exchange_plan(turn):
        slot = rank - turn * cap
        inside = held & (slot >= 0) & (slot < cap)
        slot = jnp.where(inside, shard * cap + slot, -1)
        asked = jnp.sum(
            jnp.where(
                leading[None, :]
                & (slot[None, :] == jnp.arange(group_mod * cap, dtype=jnp.int32)[:, None]),
                row[None, :] + 1,
                0,
            ),
            axis=1,
        )
        asked = lax.all_to_all(
            asked.reshape(group_mod, cap), "mod", split_axis=0, concat_axis=0, tiled=True
        )
        return one_hot(slot, group_mod * cap), one_hot(asked.reshape(-1) - 1, shard_rows)

    def fetch(plan):
        spread, pick = plan
        sent = product(pick, table_low).astype(low).reshape(group_mod, cap, width)
        got = lax.all_to_all(sent, "mod", split_axis=0, concat_axis=0, tiled=True)
        return product(spread, got.reshape(-1, width)).astype(low)

    def give(plan, gradient):
        spread, pick = plan
        sent = left_product(spread, gradient).astype(low).reshape(group_mod, cap, width)
        got = lax.all_to_all(sent, "mod", split_axis=0, concat_axis=0, tiled=True)
        return left_product(pick, got.reshape(-1, width))

    plan = exchange_plan(0)
    rows = fetch(plan)
    rows = lax.while_loop(
        lambda state: state[0] < rounds,
        lambda state: (state[0] + 1, state[1] + fetch(exchange_plan(state[0]))),
        (jnp.int32(1), rows),
    )[1]
    inputs = lax.psum_scatter(rows, "dp", scatter_dimension=0, tiled=True)

    spots = lax.dynamic_slice_in_dim(own_spots, dp_place * slots_local, slots_local)
    cosine, sine = rotary_tables(length)
    here = spots[:, :, None] == jnp.arange(length, dtype=jnp.int32)
    chosen = here.astype(low)
    inputs_wide = inputs.astype(jnp.float32)
    normed_one = rms_scale(inputs_wide, gain_one).astype(low)
    mixed = product(normed_one, attend_low)
    shape = (slots_local, length, heads, HEAD_DIM)
    around = (cosine[:, None, :], sine[:, None, :])
    queries = rotate(mixed[:, :width].reshape(shape), *around).astype(low)
    queries = jnp.einsum(
        "skt,sthe->skhe", chosen, queries, preferred_element_type=jnp.float32
    ).astype(low)
    keys_in = rotate(mixed[:, width : 2 * width].reshape(shape), *around).astype(low)
    values = mixed[:, 2 * width :].reshape(shape).astype(low)
    scale = HEAD_DIM ** (-0.5)
    raw = jnp.einsum("skhe,sthe->shkt", queries, keys_in, preferred_element_type=jnp.float32)
    causal = jnp.arange(length, dtype=jnp.int32) <= spots[:, None, :, None]
    scores = jnp.where(causal, raw * scale, -1e30)
    log_weight = jax.scipy.special.logsumexp(scores, axis=-1)
    chances = jnp.exp(scores - log_weight[..., None])
    heads_out = jnp.einsum(
        "shkt,sthe->skhe", chances.astype(low), values, preferred_element_type=jnp.float32
    )
    heads_out = heads_out.reshape(-1, width).astype(low)
    picked_inputs = jnp.einsum(
        "skt,stw->skw",
        chosen,
        inputs.reshape(slots_local, length, width),
        preferred_element_type=jnp.float32,
    ).reshape(-1, width)
    middle = picked_inputs + product(heads_out, output_low)

    normed_two = rms_scale(middle, gain_two).astype(low)
    normed_all = lax.all_gather(normed_two, "dp", axis=0, tiled=True)
    upper = product(normed_all, widen_low)
    gelu = lambda value: jax.nn.gelu(value, approximate=True)
    activated = gelu(upper).astype(low)
    lifted = lax.psum_scatter(
        product(activated, narrow_low), "dp", scatter_dimension=0, tiled=True
    )
    returned = (middle + lifted).astype(low).astype(jnp.float32)

    final, final_back = jax.vjp(rms_scale, returned, gain_final)
    scored = lax.all_gather(final.astype(low), ("mod", "dp"), axis=0, tiled=True)
    logits = right_product(scored, table_low)
    target_row = wanted - (mod_place * group_dp + dp_place) * shard_rows
    hits = target_row[:, None] == jnp.arange(shard_rows, dtype=jnp.int32)
    local_top = jnp.max(logits, axis=1)
    local_total = jnp.sum(jnp.exp(logits - local_top[:, None]), axis=1)
    local_target = jnp.sum(jnp.where(hits, logits, 0.0), axis=1)
    stats = lax.all_gather(
        jnp.stack([local_top, local_total, local_target]), ("mod", "dp"), axis=0, tiled=False
    )
    top = jnp.max(stats[:, 0], axis=0)
    total = jnp.sum(stats[:, 1] * jnp.exp(stats[:, 0] - top), axis=0)
    log_total = top + jnp.log(total)
    loss_total = jnp.sum(counted * (log_total - jnp.sum(stats[:, 2], axis=0)))
    grad_logits = (
        counted[:, None] * (jnp.exp(logits - log_total[:, None]) - hits.astype(jnp.float32))
    ).astype(low)
    table_grad = left_product(grad_logits, scored)
    grad_picked = lax.psum_scatter(
        product(grad_logits, table_low), ("mod", "dp"), scatter_dimension=0, tiled=True
    )

    grad_returned, grad_final = final_back(grad_picked)
    incoming = grad_returned.astype(low)
    incoming_all = lax.all_gather(incoming, "dp", axis=0, tiled=True)
    grad_narrow = left_product(activated, incoming_all)
    grad_act = right_product(incoming_all, narrow_low)
    grad_upper = jax.vjp(gelu, upper)[1](grad_act)[0].astype(low)
    grad_widen = left_product(normed_all, grad_upper)
    grad_widen = lax.all_to_all(grad_widen, "dp", split_axis=0, concat_axis=1, tiled=True)
    grad_normed_two = lax.psum_scatter(
        right_product(grad_upper, widen_low), "dp", scatter_dimension=0, tiled=True
    )
    grad_middle, grad_gain_two = jax.vjp(rms_scale, middle, gain_two)[1](grad_normed_two)
    grad_middle = grad_middle + incoming.astype(jnp.float32)

    branch_grad = grad_middle.astype(low)
    grad_output = left_product(heads_out, branch_grad)
    grad_heads = right_product(branch_grad, output_low).astype(low).reshape(queries.shape)
    grad_values = jnp.einsum(
        "shkt,skhe->sthe", chances.astype(low), grad_heads, preferred_element_type=jnp.float32
    )
    grad_chances = jnp.einsum(
        "skhe,sthe->shkt", grad_heads, values, preferred_element_type=jnp.float32
    )
    delta = jnp.sum(chances * grad_chances, axis=-1, keepdims=True)
    grad_raw = (chances * (grad_chances - delta) * scale).astype(low)
    grad_queries = jnp.einsum(
        "shkt,sthe->skhe", grad_raw, keys_in, preferred_element_type=jnp.float32
    )
    grad_keys = jnp.einsum(
        "shkt,skhe->sthe", grad_raw, queries, preferred_element_type=jnp.float32
    )
    spot_cosine = jnp.sum(jnp.where(here[..., None], cosine, 0.0), axis=2)[:, :, None, :]
    spot_sine = jnp.sum(jnp.where(here[..., None], sine, 0.0), axis=2)[:, :, None, :]
    grad_queries = rotate(grad_queries, spot_cosine, -spot_sine).astype(low)
    grad_queries = jnp.einsum(
        "skt,skhe->sthe", chosen, grad_queries, preferred_element_type=jnp.float32
    )
    grad_keys = rotate(grad_keys, around[0], -around[1])
    grad_mixed = jnp.concatenate(
        [part.reshape(-1, width) for part in (grad_queries, grad_keys, grad_values)], axis=1
    ).astype(low)
    grad_attend = left_product(normed_one, grad_mixed)
    grad_normed = right_product(grad_mixed, attend_low)
    grad_inputs, grad_gain_one = jax.vjp(rms_scale, inputs_wide, gain_one)[1](grad_normed)
    grad_skip = jnp.sum(
        jnp.where(
            here[..., None], grad_middle.reshape(slots_local, spots_seq, 1, width), 0.0
        ),
        axis=1,
    ).reshape(-1, width)
    leaving = (grad_skip + grad_inputs).astype(low)
    leaving_all = lax.all_gather(leaving, "dp", axis=0, tiled=True)

    table_grad = table_grad + give(plan, leaving_all)
    table_grad = lax.while_loop(
        lambda state: state[0] < rounds,
        lambda state: (
            state[0] + 1,
            state[1] + give(exchange_plan(state[0]), leaving_all),
        ),
        (jnp.int32(1), table_grad),
    )[1]
    grad_mixing = lax.psum_scatter(
        jnp.concatenate([grad_attend, grad_output], axis=1), "dp", scatter_dimension=0, tiled=True
    )
    gain_grads = lax.all_gather(
        jnp.concatenate([grad_gain_one, grad_gain_two, grad_final]),
        ("mod", "dp"),
        axis=0,
        tiled=False,
    ).reshape(group_mod, group_dp, -1)
    grad_gains = jnp.sum(
        lax.dynamic_index_in_dim(gain_grads, mod_place, 0, keepdims=False), axis=0
    )
    grad_gains = lax.dynamic_slice_in_dim(grad_gains, dp_place * gain_part, gain_part)
    final_part = final_gain.shape[0]
    grad_final = lax.dynamic_slice_in_dim(
        jnp.sum(gain_grads[:, :, 2 * width :], axis=(0, 1)), mod_place * final_part, final_part
    )
    module_grads = (
        grad_mixing[None, :, : 3 * width],
        grad_mixing[None, :, 3 * width :],
        grad_widen[None],
        grad_narrow[None],
        grad_gains[None],
    )
    squares = sum((jnp.sum(g * g) for g in module_grads)) + jnp.sum(table_grad * table_grad)
    squares = squares + jnp.sum(grad_final * grad_final) / group_dp
    gradient_norm = jnp.sqrt(lax.psum(squares, ("mod", "dp"))) / count_total
    factor = CLIP_LIMIT / jnp.maximum(gradient_norm, CLIP_LIMIT) / count_total
    params = (attend, output, widen, narrow, gains, table, final_gain)
    grads = module_grads + (table_grad, grad_final)
    firsts = (
        first_attend,
        first_output,
        first_widen,
        first_narrow,
        first_gains,
        first_table,
        first_final,
    )
    seconds = (
        second_attend,
        second_output,
        second_widen,
        second_narrow,
        second_gains,
        second_table,
        second_final,
    )
    rates = (RATE_MATRIX, RATE_MATRIX, RATE_MATRIX, RATE_MATRIX, RATE_GAIN, RATE_MATRIX, RATE_GAIN)
    decays = (DECAY_MATRIX, DECAY_MATRIX, DECAY_MATRIX, DECAY_MATRIX, 0.0, DECAY_MATRIX, 0.0)
    updated = [
        adam_step(w, g * factor, f, s, r, c)
        for w, g, f, s, r, c in zip(params, grads, firsts, seconds, rates, decays)
    ]
    return (
        loss_total / count_total,
        gradient_norm,
        *(entry[0] for entry in updated),
        *(entry[1] for entry in updated),
        *(entry[2] for entry in updated),
    )


def solution(mesh):
    placed = (
        P(None, "mod", None),
        P(None, "mod", None),
        P(None, "mod", None),
        P(None, "mod", None),
        P(None, "mod"),
        P("mod", "dp", None),
        P("mod", "dp", None),
        P("mod", "dp", None),
        P("mod", "dp", None),
        P("mod", "dp"),
        P(("mod", "dp"), None),
        P("mod"),
        P("mod", "dp", None),
        P("mod", "dp", None),
        P("mod", "dp", None),
        P("mod", "dp", None),
        P("mod", "dp"),
        P(("mod", "dp"), None),
        P("mod"),
        P("mod", "dp", None),
        P("mod", "dp", None),
        P("mod", "dp", None),
        P("mod", "dp", None),
        P("mod", "dp"),
        P(("mod", "dp"), None),
        P("mod"),
    )
    return jax.shard_map(
        on_device,
        mesh=mesh,
        in_specs=placed,
        out_specs=(
            P(),
            P(),
            P("mod", "dp", None),
            P("mod", "dp", None),
            P("mod", "dp", None),
            P("mod", "dp", None),
            P("mod", "dp"),
            P(("mod", "dp"), None),
            P("mod"),
            P("mod", "dp", None),
            P("mod", "dp", None),
            P("mod", "dp", None),
            P("mod", "dp", None),
            P("mod", "dp"),
            P(("mod", "dp"), None),
            P("mod"),
            P("mod", "dp", None),
            P("mod", "dp", None),
            P("mod", "dp", None),
            P("mod", "dp", None),
            P("mod", "dp"),
            P(("mod", "dp"), None),
            P("mod"),
        ),
        check_vma=False,
    )
```

```python
import functools
import math

import jax
import jax.numpy as jnp
import numpy as np
from jax import lax
from jax.experimental import pallas as pl
from jax.experimental.pallas import tpu as pltpu
from jax.sharding import PartitionSpec as P

HEAD_DIM = 64


NORM_EPS = 1e-05
CLIP_LIMIT = 0.05
BETA_ONE = 0.5
BETA_TWO = 0.5
ADAM_STEP = 10.0
ADAM_EPS = 1e-08
RATE_MATRIX = 0.03
RATE_GAIN = 0.3
DECAY_MATRIX = 0.1


def rms_scale(values, gain):
    return values * lax.rsqrt(jnp.mean(values * values, axis=-1, keepdims=True) + NORM_EPS) * gain


def rotary_tables(length):
    half = HEAD_DIM // 2
    inverse = 10000.0 ** (-np.arange(half, dtype=np.float32) / half)
    angle = np.arange(length, dtype=np.float32)[:, None] * inverse[None, :]
    cosine, sine = np.cos(angle), np.sin(angle)
    cosine = np.concatenate([cosine] * 4, axis=1).astype(np.float32)
    sine = np.concatenate([-sine, sine] * 2, axis=1).astype(np.float32)
    return jnp.asarray(cosine), jnp.asarray(sine)


def product(left, right):
    return jnp.dot(left, right, preferred_element_type=jnp.float32)


def left_product(left, right):
    return lax.dot_general(
        left, right, (((0,), (0,)), ((), ())), preferred_element_type=jnp.float32
    )


def right_product(left, right):
    return lax.dot_general(
        left, right, (((1,), (1,)), ((), ())), preferred_element_type=jnp.float32
    )


def adam_step(weight, grad, first, second, rate, decay):
    mean = BETA_ONE * first + (1.0 - BETA_ONE) * grad
    square = BETA_TWO * second + (1.0 - BETA_TWO) * grad * grad
    mean_hat = mean / (1.0 - BETA_ONE**ADAM_STEP)
    square_hat = square / (1.0 - BETA_TWO**ADAM_STEP)
    return (
        weight - rate * (mean_hat / (jnp.sqrt(square_hat) + ADAM_EPS) + decay * weight),
        mean,
        square,
    )


def one_hot(index, extent):
    return (index[..., None] == jnp.arange(extent, dtype=jnp.int32)).astype(jnp.bfloat16)


def exchange_kernel(groups, plan, *refs):
    count = len(plan)
    ins, outs = refs[:count], refs[count : 2 * count]
    sends, recvs = refs[2 * count : 3 * count], refs[3 * count : 4 * count]
    local = refs[4 * count]
    sizes = [math.prod(lax.axis_size(axis) for axis in axes) for axes in groups]
    places = []
    for axes in groups:
        place = lax.axis_index(axes[0])
        for axis in axes[1:]:
            place = place * lax.axis_size(axis) + lax.axis_index(axis)
        places.append(place)

    def device(group, index):
        axes = groups[group]
        if len(axes) == 1:
            return {axes[0]: index}
        inner = lax.axis_size(axes[1])
        return {axes[0]: index // inner, axes[1]: lax.rem(index, inner)}

    barrier = pltpu.get_barrier_semaphore()
    for group, size in enumerate(sizes):

        def greet(step, carry, group=group, size=size):
            peer = lax.rem(places[group] + step, size)
            pl.semaphore_signal(
                barrier,
                inc=1,
                device_id=device(group, peer),
                device_id_type=pl.DeviceIdType.MESH,
            )
            return carry

        lax.fori_loop(1, size, greet, 0)
    pl.semaphore_wait(barrier, sum(sizes) - len(sizes))

    def copy(item, step, arriving):
        group, shared = plan[item]
        size, place = sizes[group], places[group]
        peer = lax.rem(place + step, size)
        source = ins[item] if shared else ins[item].at[peer]
        slot = lax.rem(place + size - step, size) if arriving else place
        return pltpu.make_async_remote_copy(
            src_ref=source,
            dst_ref=outs[item].at[slot],
            send_sem=sends[item].at[step],
            recv_sem=recvs[item].at[step],
            device_id=device(group, peer),
            device_id_type=pl.DeviceIdType.MESH,
        )

    for item in range(count):

        def begin(step, carry, item=item):
            copy(item, step, False).start()
            return carry

        lax.fori_loop(1, sizes[plan[item][0]], begin, 0)
    own = []
    for item in range(count):
        group, shared = plan[item]
        source = ins[item] if shared else ins[item].at[places[group]]
        own.append(
            pltpu.make_async_copy(source, outs[item].at[places[group]], local.at[item])
        )
        own[-1].start()
    for item in range(count):
        own[item].wait()

        def finish(step, carry, item=item):
            copy(item, step, False).wait_send()
            copy(item, step, True).wait_recv()
            return carry

        lax.fori_loop(1, sizes[plan[item][0]], finish, 0)


def exchange(ident, *items):
    groups, plan, shapes, scratch = [], [], [], []
    for axes, array, shared in items:
        if axes not in groups:
            groups.append(axes)
        plan.append((groups.index(axes), shared))
        size = math.prod(lax.axis_size(axis) for axis in axes)
        shape = (size,) + array.shape if shared else array.shape
        shapes.append(jax.ShapeDtypeStruct(shape, array.dtype))
        scratch.append(pltpu.SemaphoreType.DMA((size,)))
    result = pl.pallas_call(
        functools.partial(exchange_kernel, groups, plan),
        out_shape=shapes,
        in_specs=[pl.BlockSpec(memory_space=pltpu.VMEM)] * len(items),
        out_specs=[pl.BlockSpec(memory_space=pltpu.VMEM)] * len(items),
        scratch_shapes=scratch + scratch + [pltpu.SemaphoreType.DMA((len(items),))],
        compiler_params=pltpu.CompilerParams(collective_id=ident, has_side_effects=True),
        name="exchange_%d" % ident,
    )(*(array for _, array, _ in items))
    return result[0] if len(items) == 1 else result


GATHER_ORDERS = ((0, 1, 2), (2, 0, 1), (1, 2, 0))


def chip_grid():
    group_mod, group_dp = lax.axis_size("mod"), lax.axis_size("dp")
    deep = math.gcd(group_mod, 4)
    return deep, group_mod // deep, group_dp // 2


def row_pieces(rows):
    part = rows // 64 * 16
    return (0, part), (part, rows - 2 * part), (rows - part, part)


def chip_place(sizes):
    mod, dp = lax.axis_index("mod"), lax.axis_index("dp")
    return [mod // sizes[1], lax.rem(mod, sizes[1]), dp // 2], lax.rem(dp, 2)


def chip_device(sizes, at, core):
    return {"mod": at[0] * sizes[1] + at[1], "dp": at[2] * 2 + core}


def shifted(sizes, at, axis, step):
    at = list(at)
    at[axis] = lax.rem(at[axis] + step, sizes[axis])
    return at


def greet_lines(sizes, at, core):
    barrier = pltpu.get_barrier_semaphore()
    targets = [chip_device(sizes, at, 1 - core)]
    for axis in range(3):
        for step in range(1, sizes[axis]):
            targets.append(chip_device(sizes, shifted(sizes, at, axis, step), core))
    for target in targets:
        pl.semaphore_signal(
            barrier, inc=1, device_id=target, device_id_type=pl.DeviceIdType.MESH
        )
    pl.semaphore_wait(barrier, len(targets))


def line_copies(sizes):
    return sum(len(GATHER_ORDERS) * (size - 1) for size in sizes)


def gather_kernel(sizes, rows, in_ref, out_ref, send, recv, pair_send, pair_recv, local):
    at, core = chip_place(sizes)
    greet_lines(sizes, at, core)
    pieces = row_pieces(rows)
    keys = {}
    for piece, order in enumerate(GATHER_ORDERS):
        for stage, axis in enumerate(order):
            for step in range(1, sizes[axis]):
                keys[piece, stage, step] = len(keys)

    def region(at, done, core, piece):
        start, count = pieces[piece]
        index = tuple(slice(None) if axis in done else at[axis] for axis in range(3))
        return out_ref.at[index + (core, pl.ds(start, count))]

    def remote(source, target, sems, index, at, core):
        return pltpu.make_async_remote_copy(
            src_ref=source,
            dst_ref=target,
            send_sem=sems[0].at[index],
            recv_sem=sems[1].at[index],
            device_id=chip_device(sizes, at, core),
            device_id_type=pl.DeviceIdType.MESH,
        )

    def line(piece, stage, step, arriving):
        order = GATHER_ORDERS[piece]
        axis, done = order[stage], order[:stage]
        peer = shifted(sizes, at, axis, step)
        origin = shifted(sizes, at, axis, sizes[axis] - step)
        target = region(origin if arriving else at, done, core, piece)
        source = region(at, done, core, piece)
        if stage == 0:
            source = in_ref.at[pl.ds(*pieces[piece])]
        return remote(source, target, (send, recv), keys[piece, stage, step], peer, core)

    def pair(piece, stage, step, arriving):
        order = GATHER_ORDERS[piece]
        axis, done = order[stage], order[:stage]
        origin = shifted(sizes, at, axis, sizes[axis] - step)
        source = region(origin, done, core, piece)
        target = region(origin, done, 1 - core if arriving else core, piece)
        index = keys[piece, stage, step]
        return remote(source, target, (pair_send, pair_recv), index, at, 1 - core)

    def pair_own(arriving):
        target = out_ref.at[at[0], at[1], at[2], 1 - core if arriving else core]
        return remote(in_ref, target, (pair_send, pair_recv), len(keys), at, 1 - core)

    own = pltpu.make_async_copy(in_ref, out_ref.at[at[0], at[1], at[2], core], local)
    own.start()
    pair_own(False).start()
    for stage in range(4):
        for piece, order in enumerate(GATHER_ORDERS):
            if stage > 0:
                for step in range(1, sizes[order[stage - 1]]):
                    line(piece, stage - 1, step, True).wait_recv()
                if stage == 1 and piece == 0:
                    own.wait()
            if stage < 3:
                for step in range(1, sizes[order[stage]]):
                    line(piece, stage, step, False).start()
            if stage > 0:
                for step in range(1, sizes[order[stage - 1]]):
                    pair(piece, stage - 1, step, False).start()
    for piece, stage, step in keys:
        line(piece, stage, step, False).wait_send()
        pair(piece, stage, step, False).wait_send()
        pair(piece, stage, step, True).wait_recv()
    pair_own(False).wait_send()
    pair_own(True).wait_recv()


def gather_rows(ident, rows):
    sizes = chip_grid()
    count, width = rows.shape
    copies = line_copies(sizes)
    dma = pltpu.SemaphoreType.DMA
    gathered = pl.pallas_call(
        functools.partial(gather_kernel, sizes, count),
        out_shape=jax.ShapeDtypeStruct(sizes + (2, count, width), rows.dtype),
        in_specs=[pl.BlockSpec(memory_space=pltpu.VMEM)],
        out_specs=pl.BlockSpec(memory_space=pl.ANY),
        scratch_shapes=[dma((copies,)), dma((copies,)), dma((copies + 1,)), dma((copies + 1,)), dma],
        compiler_params=pltpu.CompilerParams(collective_id=ident, has_side_effects=True),
        name="gather_rows",
    )(rows)
    return gathered.reshape(-1, width)


def scatter_kernel(sizes, rows, in_ref, out_ref, acc, arrived, *rest):
    slots, (send, recv, pair_send, pair_recv, local) = rest[:-5], rest[-5:]
    at, core = chip_place(sizes)
    greet_lines(sizes, at, core)
    pieces = row_pieces(rows)
    orders = [order[::-1] for order in GATHER_ORDERS]
    keys = {}
    for piece, order in enumerate(orders):
        for stage, axis in enumerate(order):
            for step in range(1, sizes[axis]):
                keys[piece, stage, step] = len(keys)

    def line(piece, stage, step):
        order = orders[piece]
        axis, done = order[stage], order[:stage]
        peer = shifted(sizes, at, axis, step)
        index = tuple(
            peer[a] if a == axis else at[a] if a in done else slice(None) for a in range(3)
        )
        key = keys[piece, stage, step]
        return pltpu.make_async_remote_copy(
            src_ref=acc.at[index + (pl.ds(*pieces[piece]),)],
            dst_ref=slots[3 * piece + stage].at[step - 1],
            send_sem=send.at[key],
            recv_sem=recv.at[key],
            device_id=chip_device(sizes, peer, core),
            device_id_type=pl.DeviceIdType.MESH,
        )

    loads, pairs = [], []
    for piece in range(3):
        part = pl.ds(*pieces[piece])
        pairs.append(
            pltpu.make_async_remote_copy(
                src_ref=in_ref.at[:, :, :, 1 - core, part],
                dst_ref=arrived.at[:, :, :, part],
                send_sem=pair_send.at[piece],
                recv_sem=pair_recv.at[piece],
                device_id=chip_device(sizes, at, 1 - core),
                device_id_type=pl.DeviceIdType.MESH,
            )
        )
        pairs[-1].start()
        loads.append(
            pltpu.make_async_copy(
                in_ref.at[:, :, :, core, part], acc.at[:, :, :, part], local.at[piece]
            )
        )
        loads[-1].start()

    def add(piece, stage):
        order = orders[piece]
        done = order[:stage]
        left = [axis for axis in range(3) if axis not in done]
        part = pl.ds(*pieces[piece])

        def one(index, carry):
            where, inner = list(at), []
            for axis in reversed(left):
                where[axis] = lax.rem(index, sizes[axis])
                index = index // sizes[axis]
                inner.insert(0, where[axis])
            spot = tuple(where) + (part,)
            total = acc[spot].astype(jnp.float32)
            if stage == 0:
                total = total + arrived[spot].astype(jnp.float32)
            else:
                taken = slots[3 * piece + stage - 1]
                for step in range(taken.shape[0]):
                    total = total + taken[(step,) + tuple(inner)].astype(jnp.float32)
            if stage == 3:
                out_ref[part] = total
            else:
                acc[spot] = total.astype(acc.dtype)
            return carry

        lax.fori_loop(0, math.prod(sizes[axis] for axis in left), one, 0)

    for stage in range(4):
        for piece, order in enumerate(orders):
            if stage == 0:
                loads[piece].wait()
                pairs[piece].wait_recv()
            else:
                for step in range(1, sizes[order[stage - 1]]):
                    line(piece, stage - 1, step).wait_recv()
            add(piece, stage)
            if stage < 3:
                for step in range(1, sizes[order[stage]]):
                    line(piece, stage, step).start()
    for piece in range(3):
        pairs[piece].wait_send()
    for piece, stage, step in keys:
        line(piece, stage, step).wait_send()


def scatter_rows(ident, parts):
    sizes = chip_grid()
    width = parts.shape[1]
    count = parts.shape[0] // (2 * math.prod(sizes))
    copies = line_copies(sizes)
    dma = pltpu.SemaphoreType.DMA
    slots = []
    for piece, order in enumerate(GATHER_ORDERS):
        order = order[::-1]
        for stage, axis in enumerate(order):
            left = tuple(sizes[a] for a in range(3) if a not in order[: stage + 1])
            shape = (sizes[axis] - 1,) + left + (row_pieces(count)[piece][1], width)
            slots.append(pltpu.VMEM(shape, parts.dtype))
    return pl.pallas_call(
        functools.partial(scatter_kernel, sizes, count),
        out_shape=jax.ShapeDtypeStruct((count, width), jnp.float32),
        in_specs=[pl.BlockSpec(memory_space=pl.ANY)],
        out_specs=pl.BlockSpec(memory_space=pltpu.VMEM),
        scratch_shapes=[
            pltpu.VMEM(sizes + (count, width), parts.dtype),
            pltpu.VMEM(sizes + (count, width), parts.dtype),
            *slots,
            dma((copies,)),
            dma((copies,)),
            dma((3,)),
            dma((3,)),
            dma((3,)),
        ],
        compiler_params=pltpu.CompilerParams(collective_id=ident, has_side_effects=True),
        name="scatter_rows",
    )(parts.reshape(sizes + (2, count, width)))


GROUP_SEQS = 4


def wide_table(table_ref, tokens, width):
    table = table_ref[...]
    table = jnp.concatenate([table] * (tokens // table.shape[0]), axis=0)
    return jnp.concatenate([table] * (width // table.shape[1]), axis=1)


def turned(values, cosine, sine):
    width = values.shape[-1]
    half = HEAD_DIM // 2
    lane = lax.broadcasted_iota(jnp.int32, values.shape, 1)
    other = jnp.where(
        lane % HEAD_DIM < half,
        pltpu.roll(values, width - half, 1),
        pltpu.roll(values, half, 1),
    )
    return values * cosine + other * sine


def head_spread(values, heads):
    rows, width = values.shape
    lane = lax.broadcasted_iota(jnp.int32, (heads, rows, width), 2)
    head = lax.broadcasted_iota(jnp.int32, (heads, rows, width), 0)
    return jnp.where(lane // HEAD_DIM == head, values[None], jnp.zeros((), values.dtype))


def head_fold(values, heads):
    rows, width = values.shape
    values = values.reshape(heads, rows // heads, width)
    lane = lax.broadcasted_iota(jnp.int32, values.shape, 2)
    head = lax.broadcasted_iota(jnp.int32, values.shape, 0)
    return jnp.sum(jnp.where(lane // HEAD_DIM == head, values, 0.0), axis=0)


def attention_parts(length, spots_ref, mixed_ref, cosine_ref, sine_ref):
    tokens, width = mixed_ref.shape[0], mixed_ref.shape[1] // 3
    heads = width // HEAD_DIM
    cosine = wide_table(cosine_ref, tokens, width)
    sine = wide_table(sine_ref, tokens, width)
    spot = spots_ref[...]
    key = lax.broadcasted_iota(jnp.int32, (spot.shape[0], tokens), 1)
    chosen = key == spot
    seen = (key <= spot) & (key >= spot - spot % length)
    queries = turned(mixed_ref[:, :width], cosine, sine).astype(jnp.bfloat16)
    queries = product(chosen.astype(jnp.bfloat16), queries)
    queries = head_spread(queries, heads).reshape(-1, width).astype(jnp.bfloat16)
    keys_in = turned(mixed_ref[:, width : 2 * width], cosine, sine).astype(jnp.bfloat16)
    values = mixed_ref[:, 2 * width :].astype(jnp.bfloat16)
    raw = right_product(queries, keys_in).reshape(heads, -1, tokens)
    scores = jnp.where(seen[None], raw * HEAD_DIM ** (-0.5), -1e30).reshape(-1, tokens)
    top = jnp.max(scores, axis=1, keepdims=True)
    terms = jnp.exp(scores - top)
    chances = terms / jnp.sum(terms, axis=1, keepdims=True)
    return chosen, queries, keys_in, values, chances, cosine, sine


def attention_kernel(
    length, spots_ref, mixed_ref, inputs_ref, cosine_ref, sine_ref, heads_ref, picked_ref
):
    heads = inputs_ref.shape[1] // HEAD_DIM
    chosen, _, _, values, chances, _, _ = attention_parts(
        length, spots_ref, mixed_ref, cosine_ref, sine_ref
    )
    spread = product(chances.astype(jnp.bfloat16), values)
    heads_ref[...] = head_fold(spread, heads).astype(jnp.bfloat16)
    picked_ref[...] = product(chosen.astype(jnp.bfloat16), inputs_ref[...])


def attention_back_kernel(
    length, spots_ref, mixed_ref, grad_ref, cosine_ref, sine_ref, out_ref
):
    width = grad_ref.shape[1]
    heads = width // HEAD_DIM
    chosen, queries, keys_in, values, chances, cosine, sine = attention_parts(
        length, spots_ref, mixed_ref, cosine_ref, sine_ref
    )
    grad_heads = head_spread(grad_ref[...].astype(jnp.float32), heads)
    grad_heads = grad_heads.reshape(-1, width).astype(jnp.bfloat16)
    grad_values = left_product(chances.astype(jnp.bfloat16), grad_heads)
    grad_chances = right_product(grad_heads, values)
    delta = jnp.sum(chances * grad_chances, axis=1, keepdims=True)
    grad_raw = (chances * (grad_chances - delta) * HEAD_DIM ** (-0.5)).astype(jnp.bfloat16)
    grad_queries = head_fold(product(grad_raw, keys_in), heads)
    grad_queries = lax.dot_general(
        chosen.astype(jnp.float32),
        grad_queries,
        (((0,), (0,)), ((), ())),
        precision=lax.Precision.HIGHEST,
        preferred_element_type=jnp.float32,
    )
    grad_keys = left_product(grad_raw, queries)
    out_ref[:, :width] = turned(grad_queries, cosine, -sine).astype(jnp.bfloat16)
    out_ref[:, width : 2 * width] = turned(grad_keys, cosine, -sine).astype(jnp.bfloat16)
    out_ref[:, 2 * width :] = grad_values.astype(jnp.bfloat16)


def attention_call(body, length, operands, tables, outs, name):
    sequences = operands[1].shape[0] // length
    steps = sequences // math.gcd(GROUP_SEQS, sequences)

    def block(array):
        return pl.BlockSpec((array.shape[0] // steps, array.shape[1]), lambda i: (i, 0))

    fixed = [pl.BlockSpec(table.shape, lambda i: (0, 0)) for table in tables]
    return pl.pallas_call(
        functools.partial(body, length),
        grid=(steps,),
        out_shape=outs,
        in_specs=[block(array) for array in operands] + fixed,
        out_specs=[block(array) for array in outs],
        name=name,
    )(*operands, *tables)


def on_device(
    token_ids,
    targets,
    positions,
    loss_mask,
    paths,
    attend,
    output,
    widen,
    narrow,
    gains,
    table,
    final_gain,
    first_attend,
    first_output,
    first_widen,
    first_narrow,
    first_gains,
    first_table,
    first_final,
    second_attend,
    second_output,
    second_widen,
    second_narrow,
    second_gains,
    second_table,
    second_final,
):
    group_dp = lax.axis_size("dp")
    group_mod = lax.axis_size("mod")
    dp_place = lax.axis_index("dp")
    mod_place = lax.axis_index("mod")
    everyone = ("mod", "dp")
    place = mod_place * group_dp + dp_place
    sources = group_mod * group_dp
    micro, per_mod, length = token_ids.shape
    spots_seq = positions.shape[2]
    seq_dev = per_mod // group_dp
    shard_rows, width = table.shape
    heads = width // HEAD_DIM
    slots = micro * sources
    slots_local = slots // group_dp
    low = jnp.bfloat16

    mixing = lax.all_gather(
        jnp.concatenate([attend[0], output[0]], axis=1).astype(low), "dp", axis=0, tiled=True
    )
    attend_low, output_low = mixing[:, : 3 * width], mixing[:, 3 * width :]
    widen_low = lax.all_to_all(
        widen[0].astype(low), "dp", split_axis=1, concat_axis=0, tiled=True
    )
    narrow_low = narrow[0].astype(low)
    table_low = table.astype(low)

    fields = jnp.concatenate(
        [token_ids, positions, targets, loss_mask, paths[..., None]], axis=-1
    )
    fields, gain_parts, final_parts = exchange(
        0,
        (("mod",), fields.reshape(micro * per_mod, -1), True),
        (("dp",), jnp.broadcast_to(gains.astype(low), (16, gains.shape[1])), True),
        (("mod",), jnp.broadcast_to(final_gain.astype(low)[None], (16, final_gain.shape[0])), True),
    )
    own_gains = gain_parts[:, 0].reshape(-1).astype(jnp.float32)
    gain_one, gain_two = own_gains[:width], own_gains[width:]
    gain_final = final_parts[:, 0].reshape(-1).astype(jnp.float32)
    fields = fields.reshape(group_mod, micro, per_mod, -1).transpose(1, 0, 2, 3)
    fields = fields.reshape(slots, seq_dev, -1)
    own = lax.dynamic_slice_in_dim(fields, dp_place * slots_local, slots_local)
    own_match = own[..., -1] == mod_place
    own = jnp.sum(jnp.where(own_match[..., None], own[..., : length + spots_seq], 0), axis=1)
    own_tokens = own[:, :length].reshape(-1)
    spots = own[:, length:]
    held = jnp.repeat(jnp.any(own_match, axis=1), length)
    match = fields[None, ..., -1] == jnp.arange(group_mod, dtype=jnp.int32)[:, None, None]
    scoring = jnp.sum(
        jnp.where(match[..., None], fields[None, ..., length + spots_seq : -1], 0), axis=2
    )
    wanted = scoring[..., :spots_seq].reshape(-1)
    counted = scoring[..., spots_seq:].reshape(-1).astype(jnp.float32)
    count_total = jnp.sum(counted)

    shard = own_tokens // shard_rows
    row = own_tokens % shard_rows
    key = jnp.where(held, own_tokens, -1)
    order = jnp.arange(key.shape[0], dtype=jnp.int32)
    repeated = jnp.any((key[:, None] == key[None, :]) & (order[None, :] < order[:, None]), axis=1)
    leading = held & ~repeated
    rank = jnp.sum(
        (
            leading[None, :] & (shard[None, :] == shard[:, None]) & (key[None, :] < key[:, None])
        ).astype(jnp.int32),
        axis=1,
    )
    expected = -(-slots_local * length // sources)
    cap = -(-3 * expected // 16) * 8
    cap = min(max(cap, 16), -(-shard_rows // 8) * 8, 112)
    own_rounds = jnp.max(jnp.where(leading, rank // cap, 0)) + 1

    def ask(turn):
        slot = rank - turn * cap
        inside = held & (slot >= 0) & (slot < cap)
        slot = jnp.where(inside, shard * cap + slot, -1)
        asked = jnp.sum(
            jnp.where(
                leading[None, :]
                & (slot[None, :] == jnp.arange(sources * cap, dtype=jnp.int32)[:, None]),
                row[None, :] + 1,
                0,
            ),
            axis=1,
        ).reshape(sources, cap)
        return slot, asked

    slot, asked = ask(0)
    message = jnp.concatenate(
        [asked, jnp.broadcast_to(own_rounds, (sources, 128 - cap))], axis=1
    )
    message = exchange(
        1, (everyone, jnp.broadcast_to(message[:, None], (sources, 8, 128)), False)
    )
    rounds = jnp.max(message[:, 0, cap])
    spread = one_hot(slot, sources * cap)
    pick = one_hot(message[:, 0, :cap].reshape(-1) - 1, shard_rows)

    def other_plan(turn):
        slot, asked = ask(turn)
        asked = lax.all_to_all(asked, everyone, split_axis=0, concat_axis=0, tiled=True)
        return one_hot(slot, sources * cap), one_hot(asked.reshape(-1) - 1, shard_rows)

    def other_rows(state):
        turn, rows = state
        spread, pick = other_plan(turn)
        sent = product(pick, table_low).astype(low).reshape(sources, cap, width)
        got = lax.all_to_all(sent, everyone, split_axis=0, concat_axis=0, tiled=True)
        return turn + 1, rows + product(spread, got.reshape(-1, width)).astype(low)

    sent = product(pick, table_low).astype(low).reshape(sources, cap, width)
    got = exchange(2, (everyone, sent, False))
    inputs = product(spread, got.reshape(-1, width)).astype(low)
    inputs = lax.while_loop(
        lambda state: state[0] < rounds, other_rows, (jnp.int32(1), inputs)
    )[1]

    group = math.gcd(GROUP_SEQS, slots_local)
    tables = rotary_tables(length)
    flat_spots = spots + (jnp.arange(slots_local, dtype=jnp.int32) % group)[:, None] * length
    flat_spots = flat_spots.reshape(-1, 1)
    inputs_wide = inputs.astype(jnp.float32)
    normed_one = rms_scale(inputs_wide, gain_one).astype(low)
    mixed = product(normed_one, attend_low)
    picked_rows = slots_local * spots_seq
    heads_out, picked_inputs = attention_call(
        attention_kernel,
        length,
        (flat_spots, mixed, inputs),
        tables,
        [
            jax.ShapeDtypeStruct((picked_rows, width), low),
            jax.ShapeDtypeStruct((picked_rows, width), jnp.float32),
        ],
        "attention",
    )
    middle = picked_inputs + product(heads_out, output_low)

    def sum_parts(ident, parts):
        parts = parts.astype(low).reshape(group_dp, picked_rows, width)
        return jnp.sum(exchange(ident, (("dp",), parts, False)).astype(jnp.float32), axis=0)

    normed_two = rms_scale(middle, gain_two).astype(low)
    normed_all = exchange(3, (("dp",), normed_two, True)).reshape(-1, width)
    upper = product(normed_all, widen_low)
    gelu = lambda value: jax.nn.gelu(value, approximate=True)
    activated = gelu(upper).astype(low)
    lifted = sum_parts(4, product(activated, narrow_low))
    returned = (middle + lifted).astype(low).astype(jnp.float32)

    final, final_back = jax.vjp(rms_scale, returned, gain_final)
    scored = gather_rows(12, final.astype(low))
    logits = right_product(scored, table_low)
    target_row = wanted - place * shard_rows
    hits = target_row[:, None] == jnp.arange(shard_rows, dtype=jnp.int32)
    local_top = jnp.max(logits, axis=1)
    local_total = jnp.sum(jnp.exp(logits - local_top[:, None]), axis=1)
    local_target = jnp.sum(jnp.where(hits, logits, 0.0), axis=1)
    stats = jnp.stack(
        [part.reshape(sources, picked_rows) for part in (local_top, local_total, local_target)],
        axis=1,
    )
    stats = exchange(5, (everyone, jnp.pad(stats, ((0, 0), (0, 5), (0, 0))), False))
    top = jnp.max(stats[:, 0], axis=0)
    total = jnp.sum(stats[:, 1] * jnp.exp(stats[:, 0] - top), axis=0)
    own_totals = jnp.stack([top + jnp.log(total), jnp.sum(stats[:, 2], axis=0)])
    totals = exchange(6, (everyone, jnp.pad(own_totals, ((0, 6), (0, 0))), True))
    log_total = totals[:, 0].reshape(-1)
    loss_total = jnp.sum(counted * (log_total - totals[:, 1].reshape(-1)))
    grad_logits = (
        counted[:, None] * (jnp.exp(logits - log_total[:, None]) - hits.astype(jnp.float32))
    ).astype(low)
    table_grad = left_product(grad_logits, scored)
    grad_picked = scatter_rows(13, product(grad_logits, table_low).astype(low))

    grad_returned, grad_final = final_back(grad_picked)
    incoming = grad_returned.astype(low)
    incoming_all = exchange(7, (("dp",), incoming, True)).reshape(-1, width)
    grad_narrow = left_product(activated, incoming_all)
    grad_act = right_product(incoming_all, narrow_low)
    grad_upper = jax.vjp(gelu, upper)[1](grad_act)[0].astype(low)
    grad_widen = left_product(normed_all, grad_upper).astype(low)
    grad_widen = lax.all_to_all(grad_widen, "dp", split_axis=0, concat_axis=1, tiled=True)
    grad_widen = grad_widen.astype(jnp.float32)
    grad_normed_two = sum_parts(8, right_product(grad_upper, widen_low))
    grad_middle, grad_gain_two = jax.vjp(rms_scale, middle, gain_two)[1](grad_normed_two)
    grad_middle = grad_middle + incoming.astype(jnp.float32)

    branch_grad = grad_middle.astype(low)
    grad_output = left_product(heads_out, branch_grad)
    grad_heads = right_product(branch_grad, output_low).astype(low)
    (grad_mixed,) = attention_call(
        attention_back_kernel,
        length,
        (flat_spots, mixed, grad_heads),
        tables,
        [jax.ShapeDtypeStruct(mixed.shape, low)],
        "attention_back",
    )
    grad_attend = left_product(normed_one, grad_mixed)
    grad_normed = right_product(grad_mixed, attend_low)
    grad_inputs, grad_gain_one = jax.vjp(rms_scale, inputs_wide, gain_one)[1](grad_normed)
    here = spots[:, :, None] == jnp.arange(length, dtype=jnp.int32)
    grad_skip = jnp.sum(
        jnp.where(
            here[..., None], grad_middle.reshape(slots_local, spots_seq, 1, width), 0.0
        ),
        axis=1,
    ).reshape(-1, width)
    leaving = (grad_skip + grad_inputs).astype(low)

    grad_mixing = lax.psum_scatter(
        jnp.concatenate([grad_attend, grad_output], axis=1).astype(low),
        "dp",
        scatter_dimension=0,
        tiled=True,
    ).astype(jnp.float32)

    def other_grads(state):
        turn, total = state
        spread, pick = other_plan(turn)
        sent = left_product(spread, leaving).astype(low).reshape(sources, cap, width)
        got = lax.all_to_all(sent, everyone, split_axis=0, concat_axis=0, tiled=True)
        return turn + 1, total + left_product(pick, got.reshape(-1, width))

    given = left_product(spread, leaving).astype(low).reshape(sources, cap, width)
    given = exchange(9, (everyone, given, False))
    table_grad = table_grad + left_product(pick, given.reshape(-1, width))
    table_grad = lax.while_loop(
        lambda state: state[0] < rounds, other_grads, (jnp.int32(1), table_grad)
    )[1]
    gain_grads = jnp.concatenate([grad_gain_one, grad_gain_two, grad_final])
    gain_grads = jnp.pad(gain_grads.reshape(-1, 128), ((0, -gain_grads.shape[0] // 128 % 8), (0, 0)))
    gain_grads = jnp.sum(exchange(10, (("dp",), gain_grads, True)), axis=0).reshape(-1)
    own_gain_grads = gain_grads[: 2 * width]
    final_rows = gain_grads[2 * width : 3 * width].reshape(-1, 128)
    gain_part = gains.shape[1]
    grad_gains = lax.dynamic_slice_in_dim(own_gain_grads, dp_place * gain_part, gain_part)
    matrix_grads = (
        grad_mixing[None, :, : 3 * width],
        grad_mixing[None, :, 3 * width :],
        grad_widen[None],
        grad_narrow[None],
    )
    squares = sum((jnp.sum(g * g) for g in matrix_grads)) + jnp.sum(table_grad * table_grad)
    squares = squares + jnp.sum(grad_gains * grad_gains)
    last = jnp.concatenate(
        [final_rows, jnp.broadcast_to(squares, (16 - final_rows.shape[0] % 8 - 8, 128))], axis=0
    )
    last = exchange(11, (everyone, last, True))
    final_count = final_rows.shape[0]
    grad_final = (
        jnp.sum(last[:, :final_count].reshape(group_mod, group_dp, -1)[:, 0], axis=0)
    )
    squares = jnp.sum(last[:, final_count, 0]) + jnp.sum(grad_final * grad_final)
    final_part = final_gain.shape[0]
    grad_final = lax.dynamic_slice_in_dim(grad_final, mod_place * final_part, final_part)
    gradient_norm = jnp.sqrt(squares) / count_total
    factor = CLIP_LIMIT / jnp.maximum(gradient_norm, CLIP_LIMIT) / count_total
    params = (attend, output, widen, narrow, gains, table, final_gain)
    grads = matrix_grads + (grad_gains[None], table_grad, grad_final)
    firsts = (
        first_attend,
        first_output,
        first_widen,
        first_narrow,
        first_gains,
        first_table,
        first_final,
    )
    seconds = (
        second_attend,
        second_output,
        second_widen,
        second_narrow,
        second_gains,
        second_table,
        second_final,
    )
    rates = (RATE_MATRIX, RATE_MATRIX, RATE_MATRIX, RATE_MATRIX, RATE_GAIN, RATE_MATRIX, RATE_GAIN)
    decays = (DECAY_MATRIX, DECAY_MATRIX, DECAY_MATRIX, DECAY_MATRIX, 0.0, DECAY_MATRIX, 0.0)
    updated = [
        adam_step(w, g * factor, f, s, r, c)
        for w, g, f, s, r, c in zip(params, grads, firsts, seconds, rates, decays)
    ]
    return (
        loss_total / count_total,
        gradient_norm,
        *(entry[0] for entry in updated),
        *(entry[1] for entry in updated),
        *(entry[2] for entry in updated),
    )


def solution(mesh):
    placed = (
        P(None, "mod", None),
        P(None, "mod", None),
        P(None, "mod", None),
        P(None, "mod", None),
        P(None, "mod"),
        P("mod", "dp", None),
        P("mod", "dp", None),
        P("mod", "dp", None),
        P("mod", "dp", None),
        P("mod", "dp"),
        P(("mod", "dp"), None),
        P("mod"),
        P("mod", "dp", None),
        P("mod", "dp", None),
        P("mod", "dp", None),
        P("mod", "dp", None),
        P("mod", "dp"),
        P(("mod", "dp"), None),
        P("mod"),
        P("mod", "dp", None),
        P("mod", "dp", None),
        P("mod", "dp", None),
        P("mod", "dp", None),
        P("mod", "dp"),
        P(("mod", "dp"), None),
        P("mod"),
    )
    return jax.shard_map(
        on_device,
        mesh=mesh,
        in_specs=placed,
        out_specs=(
            P(),
            P(),
            P("mod", "dp", None),
            P("mod", "dp", None),
            P("mod", "dp", None),
            P("mod", "dp", None),
            P("mod", "dp"),
            P(("mod", "dp"), None),
            P("mod"),
            P("mod", "dp", None),
            P("mod", "dp", None),
            P("mod", "dp", None),
            P("mod", "dp", None),
            P("mod", "dp"),
            P(("mod", "dp"), None),
            P("mod"),
            P("mod", "dp", None),
            P("mod", "dp", None),
            P("mod", "dp", None),
            P("mod", "dp", None),
            P("mod", "dp"),
            P(("mod", "dp"), None),
            P("mod"),
        ),
        check_vma=False,
    )
```

```python
import functools
import math

import jax
import jax.numpy as jnp
import numpy as np
from jax import lax
from jax.experimental import pallas as pl
from jax.experimental.pallas import tpu as pltpu
from jax.sharding import PartitionSpec as P

HEAD_DIM = 64


NORM_EPS = 1e-05
CLIP_LIMIT = 0.05
BETA_ONE = 0.5
BETA_TWO = 0.5
ADAM_STEP = 10.0
ADAM_EPS = 1e-08
RATE_MATRIX = 0.03
RATE_GAIN = 0.3
DECAY_MATRIX = 0.1


def rms_scale(values, gain):
    return values * lax.rsqrt(jnp.mean(values * values, axis=-1, keepdims=True) + NORM_EPS) * gain


def rotary_tables(length):
    half = HEAD_DIM // 2
    inverse = 10000.0 ** (-np.arange(half, dtype=np.float32) / half)
    angle = np.arange(length, dtype=np.float32)[:, None] * inverse[None, :]
    cosine, sine = np.cos(angle), np.sin(angle)
    cosine = np.concatenate([cosine] * 4, axis=1).astype(np.float32)
    sine = np.concatenate([-sine, sine] * 2, axis=1).astype(np.float32)
    return jnp.asarray(cosine), jnp.asarray(sine)


def product(left, right):
    return jnp.dot(left, right, preferred_element_type=jnp.float32)


def left_product(left, right):
    return lax.dot_general(
        left, right, (((0,), (0,)), ((), ())), preferred_element_type=jnp.float32
    )


def right_product(left, right):
    return lax.dot_general(
        left, right, (((1,), (1,)), ((), ())), preferred_element_type=jnp.float32
    )


def adam_step(weight, grad, first, second, rate, decay):
    mean = BETA_ONE * first + (1.0 - BETA_ONE) * grad
    square = BETA_TWO * second + (1.0 - BETA_TWO) * grad * grad
    mean_hat = mean / (1.0 - BETA_ONE**ADAM_STEP)
    square_hat = square / (1.0 - BETA_TWO**ADAM_STEP)
    return (
        weight - rate * (mean_hat / (jnp.sqrt(square_hat) + ADAM_EPS) + decay * weight),
        mean,
        square,
    )


def one_hot(index, extent):
    return (index[..., None] == jnp.arange(extent, dtype=jnp.int32)).astype(jnp.bfloat16)


def exchange_kernel(groups, plan, *refs):
    count = len(plan)
    ins, outs = refs[:count], refs[count : 2 * count]
    sends, recvs = refs[2 * count : 3 * count], refs[3 * count : 4 * count]
    local = refs[4 * count]
    sizes = [math.prod(lax.axis_size(axis) for axis in axes) for axes in groups]
    places = []
    for axes in groups:
        place = lax.axis_index(axes[0])
        for axis in axes[1:]:
            place = place * lax.axis_size(axis) + lax.axis_index(axis)
        places.append(place)

    def device(group, index):
        axes = groups[group]
        if len(axes) == 1:
            return {axes[0]: index}
        inner = lax.axis_size(axes[1])
        return {axes[0]: index // inner, axes[1]: lax.rem(index, inner)}

    barrier = pltpu.get_barrier_semaphore()
    for group, size in enumerate(sizes):

        def greet(step, carry, group=group, size=size):
            peer = lax.rem(places[group] + step, size)
            pl.semaphore_signal(
                barrier,
                inc=1,
                device_id=device(group, peer),
                device_id_type=pl.DeviceIdType.MESH,
            )
            return carry

        lax.fori_loop(1, size, greet, 0)
    pl.semaphore_wait(barrier, sum(sizes) - len(sizes))

    def copy(item, step, arriving):
        group, shared = plan[item]
        size, place = sizes[group], places[group]
        peer = lax.rem(place + step, size)
        source = ins[item] if shared else ins[item].at[peer]
        slot = lax.rem(place + size - step, size) if arriving else place
        return pltpu.make_async_remote_copy(
            src_ref=source,
            dst_ref=outs[item].at[slot],
            send_sem=sends[item].at[step],
            recv_sem=recvs[item].at[step],
            device_id=device(group, peer),
            device_id_type=pl.DeviceIdType.MESH,
        )

    for item in range(count):

        def begin(step, carry, item=item):
            copy(item, step, False).start()
            return carry

        lax.fori_loop(1, sizes[plan[item][0]], begin, 0)
    own = []
    for item in range(count):
        group, shared = plan[item]
        source = ins[item] if shared else ins[item].at[places[group]]
        own.append(
            pltpu.make_async_copy(source, outs[item].at[places[group]], local.at[item])
        )
        own[-1].start()
    for item in range(count):
        own[item].wait()

        def finish(step, carry, item=item):
            copy(item, step, False).wait_send()
            copy(item, step, True).wait_recv()
            return carry

        lax.fori_loop(1, sizes[plan[item][0]], finish, 0)


def exchange(ident, *items):
    groups, plan, shapes, scratch = [], [], [], []
    for axes, array, shared in items:
        if axes not in groups:
            groups.append(axes)
        plan.append((groups.index(axes), shared))
        size = math.prod(lax.axis_size(axis) for axis in axes)
        shape = (size,) + array.shape if shared else array.shape
        shapes.append(jax.ShapeDtypeStruct(shape, array.dtype))
        scratch.append(pltpu.SemaphoreType.DMA((size,)))
    result = pl.pallas_call(
        functools.partial(exchange_kernel, groups, plan),
        out_shape=shapes,
        in_specs=[pl.BlockSpec(memory_space=pltpu.VMEM)] * len(items),
        out_specs=[pl.BlockSpec(memory_space=pltpu.VMEM)] * len(items),
        scratch_shapes=scratch + scratch + [pltpu.SemaphoreType.DMA((len(items),))],
        compiler_params=pltpu.CompilerParams(collective_id=ident, has_side_effects=True),
        name="exchange_%d" % ident,
    )(*(array for _, array, _ in items))
    return result[0] if len(items) == 1 else result


GATHER_ORDERS = ((0, 1, 2), (2, 0, 1), (1, 2, 0))


def chip_grid():
    group_mod, group_dp = lax.axis_size("mod"), lax.axis_size("dp")
    deep = math.gcd(group_mod, 4)
    return deep, group_mod // deep, group_dp // 2


def row_pieces(rows):
    part = rows // 64 * 16
    return (0, part), (part, rows - 2 * part), (rows - part, part)


def chip_place(sizes):
    mod, dp = lax.axis_index("mod"), lax.axis_index("dp")
    return [mod // sizes[1], lax.rem(mod, sizes[1]), dp // 2], lax.rem(dp, 2)


def chip_device(sizes, at, core):
    return {"mod": at[0] * sizes[1] + at[1], "dp": at[2] * 2 + core}


def shifted(sizes, at, axis, step):
    at = list(at)
    at[axis] = lax.rem(at[axis] + step, sizes[axis])
    return at


def greet_lines(sizes, at, core):
    barrier = pltpu.get_barrier_semaphore()
    targets = [chip_device(sizes, at, 1 - core)]
    for axis in range(3):
        for step in range(1, sizes[axis]):
            targets.append(chip_device(sizes, shifted(sizes, at, axis, step), core))
    for target in targets:
        pl.semaphore_signal(
            barrier, inc=1, device_id=target, device_id_type=pl.DeviceIdType.MESH
        )
    pl.semaphore_wait(barrier, len(targets))


def line_copies(sizes):
    return sum(len(GATHER_ORDERS) * (size - 1) for size in sizes)


def gather_kernel(sizes, rows, in_ref, out_ref, send, recv, pair_send, pair_recv, local):
    at, core = chip_place(sizes)
    greet_lines(sizes, at, core)
    pieces = row_pieces(rows)
    keys = {}
    for piece, order in enumerate(GATHER_ORDERS):
        for stage, axis in enumerate(order):
            for step in range(1, sizes[axis]):
                keys[piece, stage, step] = len(keys)

    def region(at, done, core, piece):
        start, count = pieces[piece]
        index = tuple(slice(None) if axis in done else at[axis] for axis in range(3))
        return out_ref.at[index + (core, pl.ds(start, count))]

    def remote(source, target, sems, index, at, core):
        return pltpu.make_async_remote_copy(
            src_ref=source,
            dst_ref=target,
            send_sem=sems[0].at[index],
            recv_sem=sems[1].at[index],
            device_id=chip_device(sizes, at, core),
            device_id_type=pl.DeviceIdType.MESH,
        )

    def line(piece, stage, step, arriving):
        order = GATHER_ORDERS[piece]
        axis, done = order[stage], order[:stage]
        peer = shifted(sizes, at, axis, step)
        origin = shifted(sizes, at, axis, sizes[axis] - step)
        target = region(origin if arriving else at, done, core, piece)
        source = region(at, done, core, piece)
        if stage == 0:
            source = in_ref.at[pl.ds(*pieces[piece])]
        return remote(source, target, (send, recv), keys[piece, stage, step], peer, core)

    def pair(piece, stage, step, arriving):
        order = GATHER_ORDERS[piece]
        axis, done = order[stage], order[:stage]
        origin = shifted(sizes, at, axis, sizes[axis] - step)
        source = region(origin, done, core, piece)
        target = region(origin, done, 1 - core if arriving else core, piece)
        index = keys[piece, stage, step]
        return remote(source, target, (pair_send, pair_recv), index, at, 1 - core)

    def pair_own(arriving):
        target = out_ref.at[at[0], at[1], at[2], 1 - core if arriving else core]
        return remote(in_ref, target, (pair_send, pair_recv), len(keys), at, 1 - core)

    own = pltpu.make_async_copy(in_ref, out_ref.at[at[0], at[1], at[2], core], local)
    own.start()
    pair_own(False).start()
    for stage in range(4):
        for piece, order in enumerate(GATHER_ORDERS):
            if stage > 0:
                for step in range(1, sizes[order[stage - 1]]):
                    line(piece, stage - 1, step, True).wait_recv()
                if stage == 1 and piece == 0:
                    own.wait()
            if stage < 3:
                for step in range(1, sizes[order[stage]]):
                    line(piece, stage, step, False).start()
            if stage > 0:
                for step in range(1, sizes[order[stage - 1]]):
                    pair(piece, stage - 1, step, False).start()
    for piece, stage, step in keys:
        line(piece, stage, step, False).wait_send()
        pair(piece, stage, step, False).wait_send()
        pair(piece, stage, step, True).wait_recv()
    pair_own(False).wait_send()
    pair_own(True).wait_recv()


def gather_rows(ident, rows):
    sizes = chip_grid()
    count, width = rows.shape
    copies = line_copies(sizes)
    dma = pltpu.SemaphoreType.DMA
    gathered = pl.pallas_call(
        functools.partial(gather_kernel, sizes, count),
        out_shape=jax.ShapeDtypeStruct(sizes + (2, count, width), rows.dtype),
        in_specs=[pl.BlockSpec(memory_space=pltpu.VMEM)],
        out_specs=pl.BlockSpec(memory_space=pl.ANY),
        scratch_shapes=[dma((copies,)), dma((copies,)), dma((copies + 1,)), dma((copies + 1,)), dma],
        compiler_params=pltpu.CompilerParams(collective_id=ident, has_side_effects=True),
        name="gather_rows",
    )(rows)
    return gathered.reshape(-1, width)


def scatter_kernel(sizes, rows, in_ref, out_ref, acc, arrived, *rest):
    slots, (send, recv, pair_send, pair_recv, local) = rest[:-5], rest[-5:]
    at, core = chip_place(sizes)
    greet_lines(sizes, at, core)
    pieces = row_pieces(rows)
    orders = [order[::-1] for order in GATHER_ORDERS]
    keys = {}
    for piece, order in enumerate(orders):
        for stage, axis in enumerate(order):
            for step in range(1, sizes[axis]):
                keys[piece, stage, step] = len(keys)

    def line(piece, stage, step):
        order = orders[piece]
        axis, done = order[stage], order[:stage]
        peer = shifted(sizes, at, axis, step)
        index = tuple(
            peer[a] if a == axis else at[a] if a in done else slice(None) for a in range(3)
        )
        key = keys[piece, stage, step]
        return pltpu.make_async_remote_copy(
            src_ref=acc.at[index + (pl.ds(*pieces[piece]),)],
            dst_ref=slots[3 * piece + stage].at[step - 1],
            send_sem=send.at[key],
            recv_sem=recv.at[key],
            device_id=chip_device(sizes, peer, core),
            device_id_type=pl.DeviceIdType.MESH,
        )

    loads, pairs = [], []
    for piece in range(3):
        part = pl.ds(*pieces[piece])
        pairs.append(
            pltpu.make_async_remote_copy(
                src_ref=in_ref.at[:, :, :, 1 - core, part],
                dst_ref=arrived.at[:, :, :, part],
                send_sem=pair_send.at[piece],
                recv_sem=pair_recv.at[piece],
                device_id=chip_device(sizes, at, 1 - core),
                device_id_type=pl.DeviceIdType.MESH,
            )
        )
        pairs[-1].start()
        loads.append(
            pltpu.make_async_copy(
                in_ref.at[:, :, :, core, part], acc.at[:, :, :, part], local.at[piece]
            )
        )
        loads[-1].start()

    def add(piece, stage):
        order = orders[piece]
        done = order[:stage]
        left = [axis for axis in range(3) if axis not in done]
        part = pl.ds(*pieces[piece])

        def one(index, carry):
            where, inner = list(at), []
            for axis in reversed(left):
                where[axis] = lax.rem(index, sizes[axis])
                index = index // sizes[axis]
                inner.insert(0, where[axis])
            spot = tuple(where) + (part,)
            total = acc[spot].astype(jnp.float32)
            if stage == 0:
                total = total + arrived[spot].astype(jnp.float32)
            else:
                taken = slots[3 * piece + stage - 1]
                for step in range(taken.shape[0]):
                    total = total + taken[(step,) + tuple(inner)].astype(jnp.float32)
            if stage == 3:
                out_ref[part] = total
            else:
                acc[spot] = total.astype(acc.dtype)
            return carry

        lax.fori_loop(0, math.prod(sizes[axis] for axis in left), one, 0)

    for stage in range(4):
        for piece, order in enumerate(orders):
            if stage == 0:
                loads[piece].wait()
                pairs[piece].wait_recv()
            else:
                for step in range(1, sizes[order[stage - 1]]):
                    line(piece, stage - 1, step).wait_recv()
            add(piece, stage)
            if stage < 3:
                for step in range(1, sizes[order[stage]]):
                    line(piece, stage, step).start()
    for piece in range(3):
        pairs[piece].wait_send()
    for piece, stage, step in keys:
        line(piece, stage, step).wait_send()


def scatter_rows(ident, parts):
    sizes = chip_grid()
    width = parts.shape[1]
    count = parts.shape[0] // (2 * math.prod(sizes))
    copies = line_copies(sizes)
    dma = pltpu.SemaphoreType.DMA
    slots = []
    for piece, order in enumerate(GATHER_ORDERS):
        order = order[::-1]
        for stage, axis in enumerate(order):
            left = tuple(sizes[a] for a in range(3) if a not in order[: stage + 1])
            shape = (sizes[axis] - 1,) + left + (row_pieces(count)[piece][1], width)
            slots.append(pltpu.VMEM(shape, parts.dtype))
    return pl.pallas_call(
        functools.partial(scatter_kernel, sizes, count),
        out_shape=jax.ShapeDtypeStruct((count, width), jnp.float32),
        in_specs=[pl.BlockSpec(memory_space=pl.ANY)],
        out_specs=pl.BlockSpec(memory_space=pltpu.VMEM),
        scratch_shapes=[
            pltpu.VMEM(sizes + (count, width), parts.dtype),
            pltpu.VMEM(sizes + (count, width), parts.dtype),
            *slots,
            dma((copies,)),
            dma((copies,)),
            dma((3,)),
            dma((3,)),
            dma((3,)),
        ],
        compiler_params=pltpu.CompilerParams(collective_id=ident, has_side_effects=True),
        name="scatter_rows",
    )(parts.reshape(sizes + (2, count, width)))


def totals_kernel(in_ref, out_ref, arrived, mine, send, recv, back_send, back_recv):
    group_mod, group_dp = lax.axis_size("mod"), lax.axis_size("dp")
    size = group_mod * group_dp
    place = lax.axis_index("mod") * group_dp + lax.axis_index("dp")

    def device(index):
        return {"mod": index // group_dp, "dp": lax.rem(index, group_dp)}

    barrier = pltpu.get_barrier_semaphore()

    def greet(step, carry):
        pl.semaphore_signal(
            barrier,
            inc=1,
            device_id=device(lax.rem(place + step, size)),
            device_id_type=pl.DeviceIdType.MESH,
        )
        return carry

    def ahead(step, slot):
        peer = lax.rem(place + step, size)
        return pltpu.make_async_remote_copy(
            src_ref=in_ref.at[peer],
            dst_ref=arrived.at[slot],
            send_sem=send.at[step],
            recv_sem=recv.at[step],
            device_id=device(peer),
            device_id_type=pl.DeviceIdType.MESH,
        )

    def back(step, slot):
        return pltpu.make_async_remote_copy(
            src_ref=mine,
            dst_ref=out_ref.at[slot],
            send_sem=back_send.at[step],
            recv_sem=back_recv.at[step],
            device_id=device(lax.rem(place + step, size)),
            device_id_type=pl.DeviceIdType.MESH,
        )

    def begin(copy):
        def one(step, carry):
            copy(step, place).start()
            return carry

        lax.fori_loop(1, size, one, 0)

    def finish(copy):
        def one(step, carry):
            copy(step, place).wait_send()
            copy(step, lax.rem(place + size - step, size)).wait_recv()
            return carry

        lax.fori_loop(1, size, one, 0)

    lax.fori_loop(1, size, greet, 0)
    pl.semaphore_wait(barrier, size - 1)
    begin(ahead)
    arrived[place] = in_ref[place]
    finish(ahead)
    tops = arrived[:, 0:1]
    top = jnp.max(tops, axis=0)
    total = jnp.sum(arrived[:, 1:2] * jnp.exp(tops - top[None]), axis=0)
    hit = jnp.sum(arrived[:, 2:3], axis=0)
    line = lax.broadcasted_iota(jnp.int32, mine.shape, 0)
    mine[...] = jnp.where(line == 0, top + jnp.log(total), jnp.where(line == 1, hit, 0.0))
    out_ref[place] = mine[...]
    begin(back)
    finish(back)


def totals_call(ident, stats):
    dma = pltpu.SemaphoreType.DMA((stats.shape[0],))
    return pl.pallas_call(
        totals_kernel,
        out_shape=jax.ShapeDtypeStruct(stats.shape, stats.dtype),
        in_specs=[pl.BlockSpec(memory_space=pltpu.VMEM)],
        out_specs=pl.BlockSpec(memory_space=pltpu.VMEM),
        scratch_shapes=[
            pltpu.VMEM(stats.shape, stats.dtype),
            pltpu.VMEM(stats.shape[1:], stats.dtype),
            dma,
            dma,
            dma,
            dma,
        ],
        compiler_params=pltpu.CompilerParams(collective_id=ident, has_side_effects=True),
        name="totals",
    )(stats)


def side_by_side(blocks):
    count, rows, columns = blocks.shape
    if columns % 128:
        return jnp.concatenate(list(blocks.astype(jnp.float32)), axis=1)

    def place(in_ref, out_ref):
        out_ref[...] = in_ref[0].astype(jnp.float32)

    return pl.pallas_call(
        place,
        grid=(count,),
        out_shape=jax.ShapeDtypeStruct((rows, count * columns), jnp.float32),
        in_specs=[pl.BlockSpec((1, rows, columns), lambda i: (i, 0, 0))],
        out_specs=pl.BlockSpec((rows, columns), lambda i: (0, i)),
        name="side_by_side",
    )(blocks)


GROUP_SEQS = 4


def wide_table(table_ref, tokens, width):
    table = table_ref[...]
    table = jnp.concatenate([table] * (tokens // table.shape[0]), axis=0)
    return jnp.concatenate([table] * (width // table.shape[1]), axis=1)


def turned(values, cosine, sine):
    width = values.shape[-1]
    half = HEAD_DIM // 2
    lane = lax.broadcasted_iota(jnp.int32, values.shape, 1)
    other = jnp.where(
        lane % HEAD_DIM < half,
        pltpu.roll(values, width - half, 1),
        pltpu.roll(values, half, 1),
    )
    return values * cosine + other * sine


def head_spread(values, heads):
    rows, width = values.shape
    lane = lax.broadcasted_iota(jnp.int32, (heads, rows, width), 2)
    head = lax.broadcasted_iota(jnp.int32, (heads, rows, width), 0)
    return jnp.where(lane // HEAD_DIM == head, values[None], jnp.zeros((), values.dtype))


def head_fold(values, heads):
    rows, width = values.shape
    values = values.reshape(heads, rows // heads, width)
    lane = lax.broadcasted_iota(jnp.int32, values.shape, 2)
    head = lax.broadcasted_iota(jnp.int32, values.shape, 0)
    return jnp.sum(jnp.where(lane // HEAD_DIM == head, values, 0.0), axis=0)


def attention_parts(length, spots_ref, mixed_ref, cosine_ref, sine_ref):
    tokens, width = mixed_ref.shape[0], mixed_ref.shape[1] // 3
    heads = width // HEAD_DIM
    cosine = wide_table(cosine_ref, tokens, width)
    sine = wide_table(sine_ref, tokens, width)
    spot = spots_ref[...]
    key = lax.broadcasted_iota(jnp.int32, (spot.shape[0], tokens), 1)
    chosen = key == spot
    seen = (key <= spot) & (key >= spot - spot % length)
    queries = turned(mixed_ref[:, :width], cosine, sine).astype(jnp.bfloat16)
    queries = product(chosen.astype(jnp.bfloat16), queries)
    queries = head_spread(queries, heads).reshape(-1, width).astype(jnp.bfloat16)
    keys_in = turned(mixed_ref[:, width : 2 * width], cosine, sine).astype(jnp.bfloat16)
    values = mixed_ref[:, 2 * width :].astype(jnp.bfloat16)
    raw = right_product(queries, keys_in).reshape(heads, -1, tokens)
    scores = jnp.where(seen[None], raw * HEAD_DIM ** (-0.5), -1e30).reshape(-1, tokens)
    top = jnp.max(scores, axis=1, keepdims=True)
    terms = jnp.exp(scores - top)
    chances = terms / jnp.sum(terms, axis=1, keepdims=True)
    return chosen, queries, keys_in, values, chances, cosine, sine


def attention_kernel(
    length, spots_ref, mixed_ref, inputs_ref, cosine_ref, sine_ref, heads_ref, picked_ref
):
    heads = inputs_ref.shape[1] // HEAD_DIM
    chosen, _, _, values, chances, _, _ = attention_parts(
        length, spots_ref, mixed_ref, cosine_ref, sine_ref
    )
    spread = product(chances.astype(jnp.bfloat16), values)
    heads_ref[...] = head_fold(spread, heads).astype(jnp.bfloat16)
    picked_ref[...] = product(chosen.astype(jnp.bfloat16), inputs_ref[...])


def attention_back_kernel(
    length, spots_ref, mixed_ref, grad_ref, cosine_ref, sine_ref, out_ref
):
    width = grad_ref.shape[1]
    heads = width // HEAD_DIM
    chosen, queries, keys_in, values, chances, cosine, sine = attention_parts(
        length, spots_ref, mixed_ref, cosine_ref, sine_ref
    )
    grad_heads = head_spread(grad_ref[...].astype(jnp.float32), heads)
    grad_heads = grad_heads.reshape(-1, width).astype(jnp.bfloat16)
    grad_values = left_product(chances.astype(jnp.bfloat16), grad_heads)
    grad_chances = right_product(grad_heads, values)
    delta = jnp.sum(chances * grad_chances, axis=1, keepdims=True)
    grad_raw = (chances * (grad_chances - delta) * HEAD_DIM ** (-0.5)).astype(jnp.bfloat16)
    grad_queries = head_fold(product(grad_raw, keys_in), heads)
    grad_queries = lax.dot_general(
        chosen.astype(jnp.float32),
        grad_queries,
        (((0,), (0,)), ((), ())),
        precision=lax.Precision.HIGHEST,
        preferred_element_type=jnp.float32,
    )
    grad_keys = left_product(grad_raw, queries)
    out_ref[:, :width] = turned(grad_queries, cosine, -sine).astype(jnp.bfloat16)
    out_ref[:, width : 2 * width] = turned(grad_keys, cosine, -sine).astype(jnp.bfloat16)
    out_ref[:, 2 * width :] = grad_values.astype(jnp.bfloat16)


def attention_call(body, length, operands, tables, outs, name):
    sequences = operands[1].shape[0] // length
    steps = sequences // math.gcd(GROUP_SEQS, sequences)

    def block(array):
        return pl.BlockSpec((array.shape[0] // steps, array.shape[1]), lambda i: (i, 0))

    fixed = [pl.BlockSpec(table.shape, lambda i: (0, 0)) for table in tables]
    return pl.pallas_call(
        functools.partial(body, length),
        grid=(steps,),
        out_shape=outs,
        in_specs=[block(array) for array in operands] + fixed,
        out_specs=[block(array) for array in outs],
        name=name,
    )(*operands, *tables)


def on_device(
    token_ids,
    targets,
    positions,
    loss_mask,
    paths,
    attend,
    output,
    widen,
    narrow,
    gains,
    table,
    final_gain,
    first_attend,
    first_output,
    first_widen,
    first_narrow,
    first_gains,
    first_table,
    first_final,
    second_attend,
    second_output,
    second_widen,
    second_narrow,
    second_gains,
    second_table,
    second_final,
):
    group_dp = lax.axis_size("dp")
    group_mod = lax.axis_size("mod")
    dp_place = lax.axis_index("dp")
    mod_place = lax.axis_index("mod")
    everyone = ("mod", "dp")
    place = mod_place * group_dp + dp_place
    sources = group_mod * group_dp
    micro, per_mod, length = token_ids.shape
    spots_seq = positions.shape[2]
    seq_dev = per_mod // group_dp
    shard_rows, width = table.shape
    heads = width // HEAD_DIM
    slots = micro * sources
    slots_local = slots // group_dp
    low = jnp.bfloat16

    mixing = lax.all_gather(
        jnp.concatenate([attend[0], output[0]], axis=1).astype(low), "dp", axis=0, tiled=True
    )
    attend_low, output_low = mixing[:, : 3 * width], mixing[:, 3 * width :]
    hidden = narrow.shape[1]
    widen_low = jnp.stack(
        [widen[0, :, i * hidden : (i + 1) * hidden].astype(low) for i in range(group_dp)]
    )
    widen_low = lax.all_to_all(widen_low, "dp", split_axis=0, concat_axis=0, tiled=True)
    widen_low = widen_low.reshape(width, hidden)
    narrow_low = narrow[0].astype(low)
    table_low = table.astype(low)

    fields = jnp.concatenate(
        [token_ids, positions, targets, loss_mask, paths[..., None]], axis=-1
    )
    fields, gain_parts, final_parts = exchange(
        0,
        (("mod",), fields.reshape(micro * per_mod, -1), True),
        (("dp",), jnp.broadcast_to(gains.astype(low), (16, gains.shape[1])), True),
        (("mod",), jnp.broadcast_to(final_gain.astype(low)[None], (16, final_gain.shape[0])), True),
    )
    own_gains = gain_parts[:, 0].reshape(-1).astype(jnp.float32)
    gain_one, gain_two = own_gains[:width], own_gains[width:]
    gain_final = final_parts[:, 0].reshape(-1).astype(jnp.float32)
    fields = fields.reshape(group_mod, micro, per_mod, -1).transpose(1, 0, 2, 3)
    fields = fields.reshape(slots, seq_dev, -1)
    own = lax.dynamic_slice_in_dim(fields, dp_place * slots_local, slots_local)
    own_match = own[..., -1] == mod_place
    own = jnp.sum(jnp.where(own_match[..., None], own[..., : length + spots_seq], 0), axis=1)
    own_tokens = own[:, :length].reshape(-1)
    spots = own[:, length:]
    held = jnp.repeat(jnp.any(own_match, axis=1), length)
    match = fields[None, ..., -1] == jnp.arange(group_mod, dtype=jnp.int32)[:, None, None]
    scoring = jnp.sum(
        jnp.where(match[..., None], fields[None, ..., length + spots_seq : -1], 0), axis=2
    )
    wanted = scoring[..., :spots_seq].reshape(-1)
    counted = scoring[..., spots_seq:].reshape(-1).astype(jnp.float32)
    count_total = jnp.sum(counted)

    shard = own_tokens // shard_rows
    row = own_tokens % shard_rows
    key = jnp.where(held, own_tokens, -1)
    order = jnp.arange(key.shape[0], dtype=jnp.int32)
    repeated = jnp.any((key[:, None] == key[None, :]) & (order[None, :] < order[:, None]), axis=1)
    leading = held & ~repeated
    rank = jnp.sum(
        (
            leading[None, :] & (shard[None, :] == shard[:, None]) & (key[None, :] < key[:, None])
        ).astype(jnp.int32),
        axis=1,
    )
    expected = -(-slots_local * length // sources)
    cap = -(-3 * expected // 16) * 8
    cap = min(max(cap, 16), -(-shard_rows // 8) * 8, 112)
    own_rounds = jnp.max(jnp.where(leading, rank // cap, 0)) + 1

    def ask(turn):
        slot = rank - turn * cap
        inside = held & (slot >= 0) & (slot < cap)
        slot = jnp.where(inside, shard * cap + slot, -1)
        asked = jnp.sum(
            jnp.where(
                leading[None, :]
                & (slot[None, :] == jnp.arange(sources * cap, dtype=jnp.int32)[:, None]),
                row[None, :] + 1,
                0,
            ),
            axis=1,
        ).reshape(sources, cap)
        return slot, asked

    slot, asked = ask(0)
    message = jnp.concatenate(
        [asked, jnp.broadcast_to(own_rounds, (sources, 128 - cap))], axis=1
    )
    message = exchange(
        1, (everyone, jnp.broadcast_to(message[:, None], (sources, 8, 128)), False)
    )
    rounds = jnp.max(message[:, 0, cap])
    spread = one_hot(slot, sources * cap)
    pick = one_hot(message[:, 0, :cap].reshape(-1) - 1, shard_rows)

    def other_plan(turn):
        slot, asked = ask(turn)
        asked = lax.all_to_all(asked, everyone, split_axis=0, concat_axis=0, tiled=True)
        return one_hot(slot, sources * cap), one_hot(asked.reshape(-1) - 1, shard_rows)

    def other_rows(state):
        turn, rows = state
        spread, pick = other_plan(turn)
        sent = product(pick, table_low).astype(low).reshape(sources, cap, width)
        got = lax.all_to_all(sent, everyone, split_axis=0, concat_axis=0, tiled=True)
        return turn + 1, rows + product(spread, got.reshape(-1, width)).astype(low)

    sent = product(pick, table_low).astype(low).reshape(sources, cap, width)
    got = exchange(2, (everyone, sent, False))
    inputs = product(spread, got.reshape(-1, width)).astype(low)
    inputs = lax.while_loop(
        lambda state: state[0] < rounds, other_rows, (jnp.int32(1), inputs)
    )[1]

    group = math.gcd(GROUP_SEQS, slots_local)
    tables = rotary_tables(length)
    flat_spots = spots + (jnp.arange(slots_local, dtype=jnp.int32) % group)[:, None] * length
    flat_spots = flat_spots.reshape(-1, 1)
    inputs_wide = inputs.astype(jnp.float32)
    normed_one = rms_scale(inputs_wide, gain_one).astype(low)
    mixed = product(normed_one, attend_low)
    picked_rows = slots_local * spots_seq
    heads_out, picked_inputs = attention_call(
        attention_kernel,
        length,
        (flat_spots, mixed, inputs),
        tables,
        [
            jax.ShapeDtypeStruct((picked_rows, width), low),
            jax.ShapeDtypeStruct((picked_rows, width), jnp.float32),
        ],
        "attention",
    )
    middle = picked_inputs + product(heads_out, output_low)

    def sum_parts(ident, parts):
        parts = parts.astype(low).reshape(group_dp, picked_rows, width)
        return jnp.sum(exchange(ident, (("dp",), parts, False)).astype(jnp.float32), axis=0)

    normed_two = rms_scale(middle, gain_two).astype(low)
    normed_all = exchange(3, (("dp",), normed_two, True)).reshape(-1, width)
    upper = product(normed_all, widen_low)
    gelu = lambda value: jax.nn.gelu(value, approximate=True)
    activated = gelu(upper).astype(low)
    lifted = sum_parts(4, product(activated, narrow_low))
    returned = (middle + lifted).astype(low).astype(jnp.float32)

    final, final_back = jax.vjp(rms_scale, returned, gain_final)
    scored = gather_rows(12, final.astype(low))
    logits = right_product(scored, table_low)
    target_row = wanted - place * shard_rows
    hits = target_row[:, None] == jnp.arange(shard_rows, dtype=jnp.int32)
    local_top = jnp.max(logits, axis=1)
    local_total = jnp.sum(jnp.exp(logits - local_top[:, None]), axis=1)
    local_target = jnp.sum(jnp.where(hits, logits, 0.0), axis=1)
    stats = jnp.stack(
        [part.reshape(sources, picked_rows) for part in (local_top, local_total, local_target)],
        axis=1,
    )
    totals = totals_call(5, jnp.pad(stats, ((0, 0), (0, 5), (0, 0))))
    log_total = totals[:, 0].reshape(-1)
    loss_total = jnp.sum(counted * (log_total - totals[:, 1].reshape(-1)))
    grad_logits = (
        counted[:, None] * (jnp.exp(logits - log_total[:, None]) - hits.astype(jnp.float32))
    ).astype(low)
    table_grad = left_product(grad_logits, scored)
    grad_picked = scatter_rows(13, product(grad_logits, table_low).astype(low))

    grad_returned, grad_final = final_back(grad_picked)
    incoming = grad_returned.astype(low)
    incoming_all = exchange(7, (("dp",), incoming, True)).reshape(-1, width)
    grad_narrow = left_product(activated, incoming_all)
    grad_act = right_product(incoming_all, narrow_low)
    grad_upper = jax.vjp(gelu, upper)[1](grad_act)[0].astype(low)
    grad_widen = left_product(normed_all, grad_upper).astype(low)
    grad_widen = lax.all_to_all(
        grad_widen.reshape(group_dp, -1, hidden), "dp", split_axis=0, concat_axis=0, tiled=True
    )
    grad_normed_two = sum_parts(8, right_product(grad_upper, widen_low))
    grad_middle, grad_gain_two = jax.vjp(rms_scale, middle, gain_two)[1](grad_normed_two)
    grad_middle = grad_middle + incoming.astype(jnp.float32)

    branch_grad = grad_middle.astype(low)
    grad_output = lax.psum_scatter(
        left_product(heads_out, branch_grad).astype(low), "dp", scatter_dimension=0, tiled=True
    ).astype(jnp.float32)
    grad_heads = right_product(branch_grad, output_low).astype(low)
    (grad_mixed,) = attention_call(
        attention_back_kernel,
        length,
        (flat_spots, mixed, grad_heads),
        tables,
        [jax.ShapeDtypeStruct(mixed.shape, low)],
        "attention_back",
    )
    grad_attend = left_product(normed_one, grad_mixed)
    grad_normed = right_product(grad_mixed, attend_low)
    grad_inputs, grad_gain_one = jax.vjp(rms_scale, inputs_wide, gain_one)[1](grad_normed)
    here = spots[:, :, None] == jnp.arange(length, dtype=jnp.int32)
    grad_skip = jnp.sum(
        jnp.where(
            here[..., None], grad_middle.reshape(slots_local, spots_seq, 1, width), 0.0
        ),
        axis=1,
    ).reshape(-1, width)
    leaving = (grad_skip + grad_inputs).astype(low)

    grad_attend = lax.psum_scatter(
        grad_attend.astype(low), "dp", scatter_dimension=0, tiled=True
    ).astype(jnp.float32)

    def other_grads(state):
        turn, total = state
        spread, pick = other_plan(turn)
        sent = left_product(spread, leaving).astype(low).reshape(sources, cap, width)
        got = lax.all_to_all(sent, everyone, split_axis=0, concat_axis=0, tiled=True)
        return turn + 1, total + left_product(pick, got.reshape(-1, width))

    given = left_product(spread, leaving).astype(low).reshape(sources, cap, width)
    gain_grads = jnp.concatenate([grad_gain_one, grad_gain_two, grad_final])
    gain_grads = jnp.pad(gain_grads.reshape(-1, 128), ((0, -gain_grads.shape[0] // 128 % 8), (0, 0)))
    given, gain_grads = exchange(
        9, (everyone, given, False), (("dp",), gain_grads, True)
    )
    table_grad = table_grad + left_product(pick, given.reshape(-1, width))
    table_grad = lax.while_loop(
        lambda state: state[0] < rounds, other_grads, (jnp.int32(1), table_grad)
    )[1]
    gain_grads = jnp.sum(gain_grads, axis=0).reshape(-1)
    own_gain_grads = gain_grads[: 2 * width]
    final_rows = gain_grads[2 * width : 3 * width].reshape(-1, 128)
    gain_part = gains.shape[1]
    grad_gains = lax.dynamic_slice_in_dim(own_gain_grads, dp_place * gain_part, gain_part)
    widen_squares = jnp.sum(jnp.square(grad_widen.astype(jnp.float32)))
    grad_widen = side_by_side(grad_widen)
    matrix_grads = (grad_attend[None], grad_output[None], grad_widen[None], grad_narrow[None])
    squares = sum((jnp.sum(g * g) for g in (grad_attend, grad_output, grad_narrow, table_grad)))
    squares = squares + widen_squares
    squares = squares + jnp.sum(grad_gains * grad_gains)
    last = jnp.concatenate(
        [final_rows, jnp.broadcast_to(squares, (16 - final_rows.shape[0] % 8 - 8, 128))], axis=0
    )
    last = exchange(11, (everyone, last, True))
    final_count = final_rows.shape[0]
    grad_final = (
        jnp.sum(last[:, :final_count].reshape(group_mod, group_dp, -1)[:, 0], axis=0)
    )
    squares = jnp.sum(last[:, final_count, 0]) + jnp.sum(grad_final * grad_final)
    final_part = final_gain.shape[0]
    grad_final = lax.dynamic_slice_in_dim(grad_final, mod_place * final_part, final_part)
    gradient_norm = jnp.sqrt(squares) / count_total
    factor = CLIP_LIMIT / jnp.maximum(gradient_norm, CLIP_LIMIT) / count_total
    params = (attend, output, widen, narrow, gains, table, final_gain)
    grads = matrix_grads + (grad_gains[None], table_grad, grad_final)
    firsts = (
        first_attend,
        first_output,
        first_widen,
        first_narrow,
        first_gains,
        first_table,
        first_final,
    )
    seconds = (
        second_attend,
        second_output,
        second_widen,
        second_narrow,
        second_gains,
        second_table,
        second_final,
    )
    rates = (RATE_MATRIX, RATE_MATRIX, RATE_MATRIX, RATE_MATRIX, RATE_GAIN, RATE_MATRIX, RATE_GAIN)
    decays = (DECAY_MATRIX, DECAY_MATRIX, DECAY_MATRIX, DECAY_MATRIX, 0.0, DECAY_MATRIX, 0.0)
    updated = [
        adam_step(w, g * factor, f, s, r, c)
        for w, g, f, s, r, c in zip(params, grads, firsts, seconds, rates, decays)
    ]
    return (
        loss_total / count_total,
        gradient_norm,
        *(entry[0] for entry in updated),
        *(entry[1] for entry in updated),
        *(entry[2] for entry in updated),
    )


def solution(mesh):
    placed = (
        P(None, "mod", None),
        P(None, "mod", None),
        P(None, "mod", None),
        P(None, "mod", None),
        P(None, "mod"),
        P("mod", "dp", None),
        P("mod", "dp", None),
        P("mod", "dp", None),
        P("mod", "dp", None),
        P("mod", "dp"),
        P(("mod", "dp"), None),
        P("mod"),
        P("mod", "dp", None),
        P("mod", "dp", None),
        P("mod", "dp", None),
        P("mod", "dp", None),
        P("mod", "dp"),
        P(("mod", "dp"), None),
        P("mod"),
        P("mod", "dp", None),
        P("mod", "dp", None),
        P("mod", "dp", None),
        P("mod", "dp", None),
        P("mod", "dp"),
        P(("mod", "dp"), None),
        P("mod"),
    )
    return jax.shard_map(
        on_device,
        mesh=mesh,
        in_specs=placed,
        out_specs=(
            P(),
            P(),
            P("mod", "dp", None),
            P("mod", "dp", None),
            P("mod", "dp", None),
            P("mod", "dp", None),
            P("mod", "dp"),
            P(("mod", "dp"), None),
            P("mod"),
            P("mod", "dp", None),
            P("mod", "dp", None),
            P("mod", "dp", None),
            P("mod", "dp", None),
            P("mod", "dp"),
            P(("mod", "dp"), None),
            P("mod"),
            P("mod", "dp", None),
            P("mod", "dp", None),
            P("mod", "dp", None),
            P("mod", "dp", None),
            P("mod", "dp"),
            P(("mod", "dp"), None),
            P("mod"),
        ),
        check_vma=False,
    )
```

```python
import functools
import math

import jax
import jax.numpy as jnp
import numpy as np
from jax import lax
from jax.experimental import pallas as pl
from jax.experimental.pallas import tpu as pltpu
from jax.sharding import PartitionSpec as P

HEAD_DIM = 64


NORM_EPS = 1e-05
CLIP_LIMIT = 0.05
BETA_ONE = 0.5
BETA_TWO = 0.5
ADAM_STEP = 10.0
ADAM_EPS = 1e-08
RATE_MATRIX = 0.03
RATE_GAIN = 0.3
DECAY_MATRIX = 0.1


def rms_scale(values, gain):
    return values * lax.rsqrt(jnp.mean(values * values, axis=-1, keepdims=True) + NORM_EPS) * gain


def rotary_tables(length):
    half = HEAD_DIM // 2
    inverse = 10000.0 ** (-np.arange(half, dtype=np.float32) / half)
    angle = np.arange(length, dtype=np.float32)[:, None] * inverse[None, :]
    cosine, sine = np.cos(angle), np.sin(angle)
    cosine = np.concatenate([cosine] * 4, axis=1).astype(np.float32)
    sine = np.concatenate([-sine, sine] * 2, axis=1).astype(np.float32)
    return jnp.asarray(cosine), jnp.asarray(sine)


def product(left, right):
    return jnp.dot(left, right, preferred_element_type=jnp.float32)


def left_product(left, right):
    return lax.dot_general(
        left, right, (((0,), (0,)), ((), ())), preferred_element_type=jnp.float32
    )


def right_product(left, right):
    return lax.dot_general(
        left, right, (((1,), (1,)), ((), ())), preferred_element_type=jnp.float32
    )


def adam_step(weight, grad, first, second, rate, decay):
    mean = BETA_ONE * first + (1.0 - BETA_ONE) * grad
    square = BETA_TWO * second + (1.0 - BETA_TWO) * grad * grad
    mean_hat = mean / (1.0 - BETA_ONE**ADAM_STEP)
    square_hat = square / (1.0 - BETA_TWO**ADAM_STEP)
    return (
        weight - rate * (mean_hat / (jnp.sqrt(square_hat) + ADAM_EPS) + decay * weight),
        mean,
        square,
    )


def one_hot(index, extent):
    return (index[..., None] == jnp.arange(extent, dtype=jnp.int32)).astype(jnp.bfloat16)


def exchange_kernel(groups, plan, *refs):
    count = len(plan)
    ins, outs = refs[:count], refs[count : 2 * count]
    sends, recvs = refs[2 * count : 3 * count], refs[3 * count : 4 * count]
    local = refs[4 * count]
    sizes = [math.prod(lax.axis_size(axis) for axis in axes) for axes in groups]
    places = []
    for axes in groups:
        place = lax.axis_index(axes[0])
        for axis in axes[1:]:
            place = place * lax.axis_size(axis) + lax.axis_index(axis)
        places.append(place)

    def device(group, index):
        axes = groups[group]
        if len(axes) == 1:
            return {axes[0]: index}
        inner = lax.axis_size(axes[1])
        return {axes[0]: index // inner, axes[1]: lax.rem(index, inner)}

    barrier = pltpu.get_barrier_semaphore()
    for group, size in enumerate(sizes):

        def greet(step, carry, group=group, size=size):
            peer = lax.rem(places[group] + step, size)
            pl.semaphore_signal(
                barrier,
                inc=1,
                device_id=device(group, peer),
                device_id_type=pl.DeviceIdType.MESH,
            )
            return carry

        lax.fori_loop(1, size, greet, 0)
    pl.semaphore_wait(barrier, sum(sizes) - len(sizes))

    def copy(item, step, arriving):
        group, shared = plan[item]
        size, place = sizes[group], places[group]
        peer = lax.rem(place + step, size)
        source = ins[item] if shared else ins[item].at[peer]
        slot = lax.rem(place + size - step, size) if arriving else place
        return pltpu.make_async_remote_copy(
            src_ref=source,
            dst_ref=outs[item].at[slot],
            send_sem=sends[item].at[step],
            recv_sem=recvs[item].at[step],
            device_id=device(group, peer),
            device_id_type=pl.DeviceIdType.MESH,
        )

    for item in range(count):

        def begin(step, carry, item=item):
            copy(item, step, False).start()
            return carry

        lax.fori_loop(1, sizes[plan[item][0]], begin, 0)
    own = []
    for item in range(count):
        group, shared = plan[item]
        source = ins[item] if shared else ins[item].at[places[group]]
        own.append(
            pltpu.make_async_copy(source, outs[item].at[places[group]], local.at[item])
        )
        own[-1].start()
    for item in range(count):
        own[item].wait()

        def finish(step, carry, item=item):
            copy(item, step, False).wait_send()
            copy(item, step, True).wait_recv()
            return carry

        lax.fori_loop(1, sizes[plan[item][0]], finish, 0)


def exchange(ident, *items):
    groups, plan, shapes, scratch = [], [], [], []
    for axes, array, shared in items:
        if axes not in groups:
            groups.append(axes)
        plan.append((groups.index(axes), shared))
        size = math.prod(lax.axis_size(axis) for axis in axes)
        shape = (size,) + array.shape if shared else array.shape
        shapes.append(jax.ShapeDtypeStruct(shape, array.dtype))
        scratch.append(pltpu.SemaphoreType.DMA((size,)))
    result = pl.pallas_call(
        functools.partial(exchange_kernel, groups, plan),
        out_shape=shapes,
        in_specs=[pl.BlockSpec(memory_space=pltpu.VMEM)] * len(items),
        out_specs=[pl.BlockSpec(memory_space=pltpu.VMEM)] * len(items),
        scratch_shapes=scratch + scratch + [pltpu.SemaphoreType.DMA((len(items),))],
        compiler_params=pltpu.CompilerParams(collective_id=ident, has_side_effects=True),
        name="exchange_%d" % ident,
    )(*(array for _, array, _ in items))
    return result[0] if len(items) == 1 else result


GATHER_ORDERS = ((0, 1, 2), (2, 0, 1), (1, 2, 0))


def chip_grid():
    group_mod, group_dp = lax.axis_size("mod"), lax.axis_size("dp")
    deep = math.gcd(group_mod, 4)
    return deep, group_mod // deep, group_dp // 2


def row_pieces(rows):
    part = rows // 64 * 16
    return (0, part), (part, rows - 2 * part), (rows - part, part)


def chip_place(sizes):
    mod, dp = lax.axis_index("mod"), lax.axis_index("dp")
    return [mod // sizes[1], lax.rem(mod, sizes[1]), dp // 2], lax.rem(dp, 2)


def chip_device(sizes, at, core):
    return {"mod": at[0] * sizes[1] + at[1], "dp": at[2] * 2 + core}


def shifted(sizes, at, axis, step):
    at = list(at)
    at[axis] = lax.rem(at[axis] + step, sizes[axis])
    return at


def greet_lines(sizes, at, core):
    barrier = pltpu.get_barrier_semaphore()
    targets = [chip_device(sizes, at, 1 - core)]
    for axis in range(3):
        for step in range(1, sizes[axis]):
            targets.append(chip_device(sizes, shifted(sizes, at, axis, step), core))
    for target in targets:
        pl.semaphore_signal(
            barrier, inc=1, device_id=target, device_id_type=pl.DeviceIdType.MESH
        )
    pl.semaphore_wait(barrier, len(targets))


def line_copies(sizes):
    return sum(len(GATHER_ORDERS) * (size - 1) for size in sizes)


def gather_kernel(sizes, rows, in_ref, out_ref, send, recv, pair_send, pair_recv, local):
    at, core = chip_place(sizes)
    greet_lines(sizes, at, core)
    pieces = row_pieces(rows)
    keys = {}
    for piece, order in enumerate(GATHER_ORDERS):
        for stage, axis in enumerate(order):
            for step in range(1, sizes[axis]):
                keys[piece, stage, step] = len(keys)

    def region(at, done, core, piece):
        start, count = pieces[piece]
        index = tuple(slice(None) if axis in done else at[axis] for axis in range(3))
        return out_ref.at[index + (core, pl.ds(start, count))]

    def remote(source, target, sems, index, at, core):
        return pltpu.make_async_remote_copy(
            src_ref=source,
            dst_ref=target,
            send_sem=sems[0].at[index],
            recv_sem=sems[1].at[index],
            device_id=chip_device(sizes, at, core),
            device_id_type=pl.DeviceIdType.MESH,
        )

    def line(piece, stage, step, arriving):
        order = GATHER_ORDERS[piece]
        axis, done = order[stage], order[:stage]
        peer = shifted(sizes, at, axis, step)
        origin = shifted(sizes, at, axis, sizes[axis] - step)
        target = region(origin if arriving else at, done, core, piece)
        source = region(at, done, core, piece)
        if stage == 0:
            source = in_ref.at[pl.ds(*pieces[piece])]
        return remote(source, target, (send, recv), keys[piece, stage, step], peer, core)

    def pair(piece, stage, step, arriving):
        order = GATHER_ORDERS[piece]
        axis, done = order[stage], order[:stage]
        origin = shifted(sizes, at, axis, sizes[axis] - step)
        source = region(origin, done, core, piece)
        target = region(origin, done, 1 - core if arriving else core, piece)
        index = keys[piece, stage, step]
        return remote(source, target, (pair_send, pair_recv), index, at, 1 - core)

    def pair_own(arriving):
        target = out_ref.at[at[0], at[1], at[2], 1 - core if arriving else core]
        return remote(in_ref, target, (pair_send, pair_recv), len(keys), at, 1 - core)

    own = pltpu.make_async_copy(in_ref, out_ref.at[at[0], at[1], at[2], core], local)
    own.start()
    pair_own(False).start()
    for stage in range(4):
        for piece, order in enumerate(GATHER_ORDERS):
            if stage > 0:
                for step in range(1, sizes[order[stage - 1]]):
                    line(piece, stage - 1, step, True).wait_recv()
                if stage == 1 and piece == 0:
                    own.wait()
            if stage < 3:
                for step in range(1, sizes[order[stage]]):
                    line(piece, stage, step, False).start()
            if stage > 0:
                for step in range(1, sizes[order[stage - 1]]):
                    pair(piece, stage - 1, step, False).start()
    for piece, stage, step in keys:
        line(piece, stage, step, False).wait_send()
        pair(piece, stage, step, False).wait_send()
        pair(piece, stage, step, True).wait_recv()
    pair_own(False).wait_send()
    pair_own(True).wait_recv()


def gather_rows(ident, rows):
    sizes = chip_grid()
    count, width = rows.shape
    copies = line_copies(sizes)
    dma = pltpu.SemaphoreType.DMA
    gathered = pl.pallas_call(
        functools.partial(gather_kernel, sizes, count),
        out_shape=jax.ShapeDtypeStruct(sizes + (2, count, width), rows.dtype),
        in_specs=[pl.BlockSpec(memory_space=pltpu.VMEM)],
        out_specs=pl.BlockSpec(memory_space=pl.ANY),
        scratch_shapes=[dma((copies,)), dma((copies,)), dma((copies + 1,)), dma((copies + 1,)), dma],
        compiler_params=pltpu.CompilerParams(collective_id=ident, has_side_effects=True),
        name="gather_rows",
    )(rows)
    return gathered.reshape(-1, width)


def scatter_kernel(sizes, rows, in_ref, out_ref, acc, arrived, *rest):
    slots, (send, recv, pair_send, pair_recv, local) = rest[:-5], rest[-5:]
    at, core = chip_place(sizes)
    greet_lines(sizes, at, core)
    pieces = row_pieces(rows)
    orders = [order[::-1] for order in GATHER_ORDERS]
    keys = {}
    for piece, order in enumerate(orders):
        for stage, axis in enumerate(order):
            for step in range(1, sizes[axis]):
                keys[piece, stage, step] = len(keys)

    def line(piece, stage, step):
        order = orders[piece]
        axis, done = order[stage], order[:stage]
        peer = shifted(sizes, at, axis, step)
        index = tuple(
            peer[a] if a == axis else at[a] if a in done else slice(None) for a in range(3)
        )
        key = keys[piece, stage, step]
        return pltpu.make_async_remote_copy(
            src_ref=acc.at[index + (pl.ds(*pieces[piece]),)],
            dst_ref=slots[3 * piece + stage].at[step - 1],
            send_sem=send.at[key],
            recv_sem=recv.at[key],
            device_id=chip_device(sizes, peer, core),
            device_id_type=pl.DeviceIdType.MESH,
        )

    loads, pairs = [], []
    for piece in range(3):
        part = pl.ds(*pieces[piece])
        pairs.append(
            pltpu.make_async_remote_copy(
                src_ref=in_ref.at[:, :, :, 1 - core, part],
                dst_ref=arrived.at[:, :, :, part],
                send_sem=pair_send.at[piece],
                recv_sem=pair_recv.at[piece],
                device_id=chip_device(sizes, at, 1 - core),
                device_id_type=pl.DeviceIdType.MESH,
            )
        )
        pairs[-1].start()
        loads.append(
            pltpu.make_async_copy(
                in_ref.at[:, :, :, core, part], acc.at[:, :, :, part], local.at[piece]
            )
        )
        loads[-1].start()

    def add(piece, stage):
        order = orders[piece]
        done = order[:stage]
        left = [axis for axis in range(3) if axis not in done]
        part = pl.ds(*pieces[piece])

        def one(index, carry):
            where, inner = list(at), []
            for axis in reversed(left):
                where[axis] = lax.rem(index, sizes[axis])
                index = index // sizes[axis]
                inner.insert(0, where[axis])
            spot = tuple(where) + (part,)
            total = acc[spot].astype(jnp.float32)
            if stage == 0:
                total = total + arrived[spot].astype(jnp.float32)
            else:
                taken = slots[3 * piece + stage - 1]
                for step in range(taken.shape[0]):
                    total = total + taken[(step,) + tuple(inner)].astype(jnp.float32)
            if stage == 3:
                out_ref[part] = total
            else:
                acc[spot] = total.astype(acc.dtype)
            return carry

        lax.fori_loop(0, math.prod(sizes[axis] for axis in left), one, 0)

    for stage in range(4):
        for piece, order in enumerate(orders):
            if stage == 0:
                loads[piece].wait()
                pairs[piece].wait_recv()
            else:
                for step in range(1, sizes[order[stage - 1]]):
                    line(piece, stage - 1, step).wait_recv()
            add(piece, stage)
            if stage < 3:
                for step in range(1, sizes[order[stage]]):
                    line(piece, stage, step).start()
    for piece in range(3):
        pairs[piece].wait_send()
    for piece, stage, step in keys:
        line(piece, stage, step).wait_send()


def scatter_rows(ident, parts):
    sizes = chip_grid()
    width = parts.shape[1]
    count = parts.shape[0] // (2 * math.prod(sizes))
    copies = line_copies(sizes)
    dma = pltpu.SemaphoreType.DMA
    slots = []
    for piece, order in enumerate(GATHER_ORDERS):
        order = order[::-1]
        for stage, axis in enumerate(order):
            left = tuple(sizes[a] for a in range(3) if a not in order[: stage + 1])
            shape = (sizes[axis] - 1,) + left + (row_pieces(count)[piece][1], width)
            slots.append(pltpu.VMEM(shape, parts.dtype))
    return pl.pallas_call(
        functools.partial(scatter_kernel, sizes, count),
        out_shape=jax.ShapeDtypeStruct((count, width), jnp.float32),
        in_specs=[pl.BlockSpec(memory_space=pl.ANY)],
        out_specs=pl.BlockSpec(memory_space=pltpu.VMEM),
        scratch_shapes=[
            pltpu.VMEM(sizes + (count, width), parts.dtype),
            pltpu.VMEM(sizes + (count, width), parts.dtype),
            *slots,
            dma((copies,)),
            dma((copies,)),
            dma((3,)),
            dma((3,)),
            dma((3,)),
        ],
        compiler_params=pltpu.CompilerParams(collective_id=ident, has_side_effects=True),
        name="scatter_rows",
    )(parts.reshape(sizes + (2, count, width)))


def totals_kernel(in_ref, out_ref, arrived, mine, send, recv, back_send, back_recv):
    group_mod, group_dp = lax.axis_size("mod"), lax.axis_size("dp")
    size = group_mod * group_dp
    place = lax.axis_index("mod") * group_dp + lax.axis_index("dp")

    def device(index):
        return {"mod": index // group_dp, "dp": lax.rem(index, group_dp)}

    barrier = pltpu.get_barrier_semaphore()

    def greet(step, carry):
        pl.semaphore_signal(
            barrier,
            inc=1,
            device_id=device(lax.rem(place + step, size)),
            device_id_type=pl.DeviceIdType.MESH,
        )
        return carry

    def ahead(step, slot):
        peer = lax.rem(place + step, size)
        return pltpu.make_async_remote_copy(
            src_ref=in_ref.at[peer],
            dst_ref=arrived.at[slot],
            send_sem=send.at[step],
            recv_sem=recv.at[step],
            device_id=device(peer),
            device_id_type=pl.DeviceIdType.MESH,
        )

    def back(step, slot):
        return pltpu.make_async_remote_copy(
            src_ref=mine,
            dst_ref=out_ref.at[slot],
            send_sem=back_send.at[step],
            recv_sem=back_recv.at[step],
            device_id=device(lax.rem(place + step, size)),
            device_id_type=pl.DeviceIdType.MESH,
        )

    def begin(copy):
        def one(step, carry):
            copy(step, place).start()
            return carry

        lax.fori_loop(1, size, one, 0)

    def finish(copy):
        def one(step, carry):
            copy(step, place).wait_send()
            copy(step, lax.rem(place + size - step, size)).wait_recv()
            return carry

        lax.fori_loop(1, size, one, 0)

    lax.fori_loop(1, size, greet, 0)
    pl.semaphore_wait(barrier, size - 1)
    begin(ahead)
    arrived[place] = in_ref[place]
    finish(ahead)
    tops = arrived[:, 0:1]
    top = jnp.max(tops, axis=0)
    total = jnp.sum(arrived[:, 1:2] * jnp.exp(tops - top[None]), axis=0)
    hit = jnp.sum(arrived[:, 2:3], axis=0)
    line = lax.broadcasted_iota(jnp.int32, mine.shape, 0)
    mine[...] = jnp.where(line == 0, top + jnp.log(total), jnp.where(line == 1, hit, 0.0))
    out_ref[place] = mine[...]
    begin(back)
    finish(back)


def totals_call(ident, stats):
    dma = pltpu.SemaphoreType.DMA((stats.shape[0],))
    return pl.pallas_call(
        totals_kernel,
        out_shape=jax.ShapeDtypeStruct(stats.shape, stats.dtype),
        in_specs=[pl.BlockSpec(memory_space=pltpu.VMEM)],
        out_specs=pl.BlockSpec(memory_space=pltpu.VMEM),
        scratch_shapes=[
            pltpu.VMEM(stats.shape, stats.dtype),
            pltpu.VMEM(stats.shape[1:], stats.dtype),
            dma,
            dma,
            dma,
            dma,
        ],
        compiler_params=pltpu.CompilerParams(collective_id=ident, has_side_effects=True),
        name="totals",
    )(stats)


def side_by_side(blocks):
    count, rows, columns = blocks.shape
    if columns % 128:
        return jnp.concatenate(list(blocks.astype(jnp.float32)), axis=1)

    def place(in_ref, out_ref):
        out_ref[...] = in_ref[0].astype(jnp.float32)

    return pl.pallas_call(
        place,
        grid=(count,),
        out_shape=jax.ShapeDtypeStruct((rows, count * columns), jnp.float32),
        in_specs=[pl.BlockSpec((1, rows, columns), lambda i: (i, 0, 0))],
        out_specs=pl.BlockSpec((rows, columns), lambda i: (0, i)),
        name="side_by_side",
    )(blocks)


HEAD_ROWS = 256


def logits_of(rows_ref, table_ref, wanted_ref):
    logits = right_product(table_ref[...], rows_ref[...])
    hits = lax.broadcasted_iota(jnp.int32, logits.shape, 0) == wanted_ref[...]
    return logits, hits


def scores_kernel(rows_ref, table_ref, wanted_ref, out_ref):
    logits, hits = logits_of(rows_ref, table_ref, wanted_ref)
    top = jnp.max(logits, axis=0, keepdims=True)
    total = jnp.sum(jnp.exp(logits - top), axis=0, keepdims=True)
    hit = jnp.sum(jnp.where(hits, logits, 0.0), axis=0, keepdims=True)
    count, lines, part = out_ref.shape
    line = lax.broadcasted_iota(jnp.int32, (lines, part), 0)
    for block in range(count):
        at = slice(block * part, (block + 1) * part)
        out_ref[block] = jnp.where(
            line == 0, top[:, at], jnp.where(line == 1, total[:, at], hit[:, at])
        )


def scores_back_kernel(
    rows_ref, table_ref, wanted_ref, counted_ref, totals_ref, out_ref, table_grad_ref
):
    logits, hits = logits_of(rows_ref, table_ref, wanted_ref)
    log_total = jnp.concatenate([totals_ref[i, 0:1] for i in range(totals_ref.shape[0])], axis=1)
    chances = jnp.exp(logits - log_total)
    grad = (counted_ref[...] * jnp.where(hits, chances - 1.0, chances)).astype(jnp.bfloat16)
    out_ref[...] = left_product(grad, table_ref[...]).astype(out_ref.dtype)
    part = product(grad, rows_ref[...])

    @pl.when(pl.program_id(0) == 0)
    def first():
        table_grad_ref[...] = part

    @pl.when(pl.program_id(0) > 0)
    def later():
        table_grad_ref[...] += part


def scores_call(rows, table, wanted, part):
    step = math.gcd(HEAD_ROWS, rows.shape[0])
    return pl.pallas_call(
        scores_kernel,
        grid=(rows.shape[0] // step,),
        out_shape=jax.ShapeDtypeStruct((rows.shape[0] // part, 8, part), jnp.float32),
        in_specs=[
            pl.BlockSpec((step, rows.shape[1]), lambda i: (i, 0)),
            pl.BlockSpec(table.shape, lambda i: (0, 0)),
            pl.BlockSpec((1, step), lambda i: (0, i)),
        ],
        out_specs=pl.BlockSpec((step // part, 8, part), lambda i: (i, 0, 0)),
        name="scores",
    )(rows, table, wanted[None])


def scores_back_call(rows, table, wanted, counted, totals):
    part = totals.shape[2]
    step = math.gcd(HEAD_ROWS, rows.shape[0])
    line = pl.BlockSpec((1, step), lambda i: (0, i))
    return pl.pallas_call(
        scores_back_kernel,
        grid=(rows.shape[0] // step,),
        out_shape=[
            jax.ShapeDtypeStruct(rows.shape, rows.dtype),
            jax.ShapeDtypeStruct(table.shape, jnp.float32),
        ],
        in_specs=[
            pl.BlockSpec((step, rows.shape[1]), lambda i: (i, 0)),
            pl.BlockSpec(table.shape, lambda i: (0, 0)),
            line,
            line,
            pl.BlockSpec((step // part, 8, part), lambda i: (i, 0, 0)),
        ],
        out_specs=[
            pl.BlockSpec((step, rows.shape[1]), lambda i: (i, 0)),
            pl.BlockSpec(table.shape, lambda i: (0, 0)),
        ],
        name="scores_back",
    )(rows, table, wanted[None], counted[None], totals)


GROUP_SEQS = 4


def wide_table(table_ref, tokens, width):
    table = table_ref[...]
    table = jnp.concatenate([table] * (tokens // table.shape[0]), axis=0)
    return jnp.concatenate([table] * (width // table.shape[1]), axis=1)


def turned(values, cosine, sine):
    width = values.shape[-1]
    half = HEAD_DIM // 2
    lane = lax.broadcasted_iota(jnp.int32, values.shape, 1)
    other = jnp.where(
        lane % HEAD_DIM < half,
        pltpu.roll(values, width - half, 1),
        pltpu.roll(values, half, 1),
    )
    return values * cosine + other * sine


def head_spread(values, heads):
    rows, width = values.shape
    lane = lax.broadcasted_iota(jnp.int32, (heads, rows, width), 2)
    head = lax.broadcasted_iota(jnp.int32, (heads, rows, width), 0)
    return jnp.where(lane // HEAD_DIM == head, values[None], jnp.zeros((), values.dtype))


def head_fold(values, heads):
    rows, width = values.shape
    values = values.reshape(heads, rows // heads, width)
    lane = lax.broadcasted_iota(jnp.int32, values.shape, 2)
    head = lax.broadcasted_iota(jnp.int32, values.shape, 0)
    return jnp.sum(jnp.where(lane // HEAD_DIM == head, values, 0.0), axis=0)


def attention_parts(length, spots_ref, mixed_ref, cosine_ref, sine_ref):
    tokens, width = mixed_ref.shape[0], mixed_ref.shape[1] // 3
    heads = width // HEAD_DIM
    cosine = wide_table(cosine_ref, tokens, width)
    sine = wide_table(sine_ref, tokens, width)
    spot = spots_ref[...]
    key = lax.broadcasted_iota(jnp.int32, (spot.shape[0], tokens), 1)
    chosen = key == spot
    seen = (key <= spot) & (key >= spot - spot % length)
    queries = turned(mixed_ref[:, :width], cosine, sine).astype(jnp.bfloat16)
    queries = product(chosen.astype(jnp.bfloat16), queries)
    queries = head_spread(queries, heads).reshape(-1, width).astype(jnp.bfloat16)
    keys_in = turned(mixed_ref[:, width : 2 * width], cosine, sine).astype(jnp.bfloat16)
    values = mixed_ref[:, 2 * width :].astype(jnp.bfloat16)
    raw = right_product(queries, keys_in).reshape(heads, -1, tokens)
    scores = jnp.where(seen[None], raw * HEAD_DIM ** (-0.5), -1e30).reshape(-1, tokens)
    top = jnp.max(scores, axis=1, keepdims=True)
    terms = jnp.exp(scores - top)
    chances = terms / jnp.sum(terms, axis=1, keepdims=True)
    return chosen, queries, keys_in, values, chances, cosine, sine


def attention_kernel(
    length, spots_ref, mixed_ref, inputs_ref, cosine_ref, sine_ref, heads_ref, picked_ref
):
    heads = inputs_ref.shape[1] // HEAD_DIM
    chosen, _, _, values, chances, _, _ = attention_parts(
        length, spots_ref, mixed_ref, cosine_ref, sine_ref
    )
    spread = product(chances.astype(jnp.bfloat16), values)
    heads_ref[...] = head_fold(spread, heads).astype(jnp.bfloat16)
    picked_ref[...] = product(chosen.astype(jnp.bfloat16), inputs_ref[...])


def attention_back_kernel(
    length, spots_ref, mixed_ref, grad_ref, cosine_ref, sine_ref, out_ref
):
    width = grad_ref.shape[1]
    heads = width // HEAD_DIM
    chosen, queries, keys_in, values, chances, cosine, sine = attention_parts(
        length, spots_ref, mixed_ref, cosine_ref, sine_ref
    )
    grad_heads = head_spread(grad_ref[...].astype(jnp.float32), heads)
    grad_heads = grad_heads.reshape(-1, width).astype(jnp.bfloat16)
    grad_values = left_product(chances.astype(jnp.bfloat16), grad_heads)
    grad_chances = right_product(grad_heads, values)
    delta = jnp.sum(chances * grad_chances, axis=1, keepdims=True)
    grad_raw = (chances * (grad_chances - delta) * HEAD_DIM ** (-0.5)).astype(jnp.bfloat16)
    grad_queries = head_fold(product(grad_raw, keys_in), heads)
    grad_queries = lax.dot_general(
        chosen.astype(jnp.float32),
        grad_queries,
        (((0,), (0,)), ((), ())),
        precision=lax.Precision.HIGHEST,
        preferred_element_type=jnp.float32,
    )
    grad_keys = left_product(grad_raw, queries)
    out_ref[:, :width] = turned(grad_queries, cosine, -sine).astype(jnp.bfloat16)
    out_ref[:, width : 2 * width] = turned(grad_keys, cosine, -sine).astype(jnp.bfloat16)
    out_ref[:, 2 * width :] = grad_values.astype(jnp.bfloat16)


def attention_call(body, length, operands, tables, outs, name):
    sequences = operands[1].shape[0] // length
    steps = sequences // math.gcd(GROUP_SEQS, sequences)

    def block(array):
        return pl.BlockSpec((array.shape[0] // steps, array.shape[1]), lambda i: (i, 0))

    fixed = [pl.BlockSpec(table.shape, lambda i: (0, 0)) for table in tables]
    return pl.pallas_call(
        functools.partial(body, length),
        grid=(steps,),
        out_shape=outs,
        in_specs=[block(array) for array in operands] + fixed,
        out_specs=[block(array) for array in outs],
        name=name,
    )(*operands, *tables)


def on_device(
    token_ids,
    targets,
    positions,
    loss_mask,
    paths,
    attend,
    output,
    widen,
    narrow,
    gains,
    table,
    final_gain,
    first_attend,
    first_output,
    first_widen,
    first_narrow,
    first_gains,
    first_table,
    first_final,
    second_attend,
    second_output,
    second_widen,
    second_narrow,
    second_gains,
    second_table,
    second_final,
):
    group_dp = lax.axis_size("dp")
    group_mod = lax.axis_size("mod")
    dp_place = lax.axis_index("dp")
    mod_place = lax.axis_index("mod")
    everyone = ("mod", "dp")
    place = mod_place * group_dp + dp_place
    sources = group_mod * group_dp
    micro, per_mod, length = token_ids.shape
    spots_seq = positions.shape[2]
    seq_dev = per_mod // group_dp
    shard_rows, width = table.shape
    heads = width // HEAD_DIM
    slots = micro * sources
    slots_local = slots // group_dp
    low = jnp.bfloat16

    mixing = lax.all_gather(
        jnp.concatenate([attend[0], output[0]], axis=1).astype(low), "dp", axis=0, tiled=True
    )
    attend_low, output_low = mixing[:, : 3 * width], mixing[:, 3 * width :]
    hidden = narrow.shape[1]
    widen_low = jnp.stack(
        [widen[0, :, i * hidden : (i + 1) * hidden].astype(low) for i in range(group_dp)]
    )
    widen_low = lax.all_to_all(widen_low, "dp", split_axis=0, concat_axis=0, tiled=True)
    widen_low = widen_low.reshape(width, hidden)
    narrow_low = narrow[0].astype(low)
    table_low = table.astype(low)

    fields = jnp.concatenate(
        [token_ids, positions, targets, loss_mask, paths[..., None]], axis=-1
    )
    fields, gain_parts, final_parts = exchange(
        0,
        (("mod",), fields.reshape(micro * per_mod, -1), True),
        (("dp",), jnp.broadcast_to(gains.astype(low), (16, gains.shape[1])), True),
        (("mod",), jnp.broadcast_to(final_gain.astype(low)[None], (16, final_gain.shape[0])), True),
    )
    own_gains = gain_parts[:, 0].reshape(-1).astype(jnp.float32)
    gain_one, gain_two = own_gains[:width], own_gains[width:]
    gain_final = final_parts[:, 0].reshape(-1).astype(jnp.float32)
    fields = fields.reshape(group_mod, micro, per_mod, -1).transpose(1, 0, 2, 3)
    fields = fields.reshape(slots, seq_dev, -1)
    own = lax.dynamic_slice_in_dim(fields, dp_place * slots_local, slots_local)
    own_match = own[..., -1] == mod_place
    own = jnp.sum(jnp.where(own_match[..., None], own[..., : length + spots_seq], 0), axis=1)
    own_tokens = own[:, :length].reshape(-1)
    spots = own[:, length:]
    held = jnp.repeat(jnp.any(own_match, axis=1), length)
    match = fields[None, ..., -1] == jnp.arange(group_mod, dtype=jnp.int32)[:, None, None]
    scoring = jnp.sum(
        jnp.where(match[..., None], fields[None, ..., length + spots_seq : -1], 0), axis=2
    )
    wanted = scoring[..., :spots_seq].reshape(-1)
    counted = scoring[..., spots_seq:].reshape(-1).astype(jnp.float32)
    count_total = jnp.sum(counted)

    shard = own_tokens // shard_rows
    row = own_tokens % shard_rows
    key = jnp.where(held, own_tokens, -1)
    order = jnp.arange(key.shape[0], dtype=jnp.int32)
    repeated = jnp.any((key[:, None] == key[None, :]) & (order[None, :] < order[:, None]), axis=1)
    leading = held & ~repeated
    rank = jnp.sum(
        (
            leading[None, :] & (shard[None, :] == shard[:, None]) & (key[None, :] < key[:, None])
        ).astype(jnp.int32),
        axis=1,
    )
    expected = -(-slots_local * length // sources)
    cap = -(-3 * expected // 16) * 8
    cap = min(max(cap, 16), -(-shard_rows // 8) * 8, 112)
    own_rounds = jnp.max(jnp.where(leading, rank // cap, 0)) + 1

    def ask(turn):
        slot = rank - turn * cap
        inside = held & (slot >= 0) & (slot < cap)
        slot = jnp.where(inside, shard * cap + slot, -1)
        asked = jnp.sum(
            jnp.where(
                leading[None, :]
                & (slot[None, :] == jnp.arange(sources * cap, dtype=jnp.int32)[:, None]),
                row[None, :] + 1,
                0,
            ),
            axis=1,
        ).reshape(sources, cap)
        return slot, asked

    slot, asked = ask(0)
    message = jnp.concatenate(
        [asked, jnp.broadcast_to(own_rounds, (sources, 128 - cap))], axis=1
    )
    message = exchange(
        1, (everyone, jnp.broadcast_to(message[:, None], (sources, 8, 128)), False)
    )
    rounds = jnp.max(message[:, 0, cap])
    spread = one_hot(slot, sources * cap)
    pick = one_hot(message[:, 0, :cap].reshape(-1) - 1, shard_rows)

    def other_plan(turn):
        slot, asked = ask(turn)
        asked = lax.all_to_all(asked, everyone, split_axis=0, concat_axis=0, tiled=True)
        return one_hot(slot, sources * cap), one_hot(asked.reshape(-1) - 1, shard_rows)

    def other_rows(state):
        turn, rows = state
        spread, pick = other_plan(turn)
        sent = product(pick, table_low).astype(low).reshape(sources, cap, width)
        got = lax.all_to_all(sent, everyone, split_axis=0, concat_axis=0, tiled=True)
        return turn + 1, rows + product(spread, got.reshape(-1, width)).astype(low)

    sent = product(pick, table_low).astype(low).reshape(sources, cap, width)
    got = exchange(2, (everyone, sent, False))
    inputs = product(spread, got.reshape(-1, width)).astype(low)
    inputs = lax.while_loop(
        lambda state: state[0] < rounds, other_rows, (jnp.int32(1), inputs)
    )[1]

    group = math.gcd(GROUP_SEQS, slots_local)
    tables = rotary_tables(length)
    flat_spots = spots + (jnp.arange(slots_local, dtype=jnp.int32) % group)[:, None] * length
    flat_spots = flat_spots.reshape(-1, 1)
    inputs_wide = inputs.astype(jnp.float32)
    normed_one = rms_scale(inputs_wide, gain_one).astype(low)
    mixed = product(normed_one, attend_low)
    picked_rows = slots_local * spots_seq
    heads_out, picked_inputs = attention_call(
        attention_kernel,
        length,
        (flat_spots, mixed, inputs),
        tables,
        [
            jax.ShapeDtypeStruct((picked_rows, width), low),
            jax.ShapeDtypeStruct((picked_rows, width), jnp.float32),
        ],
        "attention",
    )
    middle = picked_inputs + product(heads_out, output_low)

    def sum_parts(ident, parts):
        parts = parts.astype(low).reshape(group_dp, picked_rows, width)
        return jnp.sum(exchange(ident, (("dp",), parts, False)).astype(jnp.float32), axis=0)

    normed_two = rms_scale(middle, gain_two).astype(low)
    normed_all = exchange(3, (("dp",), normed_two, True)).reshape(-1, width)
    upper = product(normed_all, widen_low)
    gelu = lambda value: jax.nn.gelu(value, approximate=True)
    activated = gelu(upper).astype(low)
    lifted = sum_parts(4, product(activated, narrow_low))
    returned = (middle + lifted).astype(low).astype(jnp.float32)

    final, final_back = jax.vjp(rms_scale, returned, gain_final)
    scored = gather_rows(12, final.astype(low))
    target_row = wanted - place * shard_rows
    totals = totals_call(5, scores_call(scored, table_low, target_row, picked_rows))
    loss_total = jnp.sum(counted * (totals[:, 0] - totals[:, 1]).reshape(-1))
    partial, table_grad = scores_back_call(scored, table_low, target_row, counted, totals)
    grad_picked = scatter_rows(13, partial)

    grad_returned, grad_final = final_back(grad_picked)
    incoming = grad_returned.astype(low)
    incoming_all = exchange(7, (("dp",), incoming, True)).reshape(-1, width)
    grad_narrow = left_product(activated, incoming_all)
    grad_act = right_product(incoming_all, narrow_low)
    grad_upper = jax.vjp(gelu, upper)[1](grad_act)[0].astype(low)
    grad_widen = left_product(normed_all, grad_upper).astype(low)
    grad_widen = lax.all_to_all(
        grad_widen.reshape(group_dp, -1, hidden), "dp", split_axis=0, concat_axis=0, tiled=True
    )
    grad_normed_two = sum_parts(8, right_product(grad_upper, widen_low))
    grad_middle, grad_gain_two = jax.vjp(rms_scale, middle, gain_two)[1](grad_normed_two)
    grad_middle = grad_middle + incoming.astype(jnp.float32)

    branch_grad = grad_middle.astype(low)
    grad_output = lax.psum_scatter(
        left_product(heads_out, branch_grad).astype(low), "dp", scatter_dimension=0, tiled=True
    ).astype(jnp.float32)
    grad_heads = right_product(branch_grad, output_low).astype(low)
    (grad_mixed,) = attention_call(
        attention_back_kernel,
        length,
        (flat_spots, mixed, grad_heads),
        tables,
        [jax.ShapeDtypeStruct(mixed.shape, low)],
        "attention_back",
    )
    grad_attend = left_product(normed_one, grad_mixed)
    grad_normed = right_product(grad_mixed, attend_low)
    grad_inputs, grad_gain_one = jax.vjp(rms_scale, inputs_wide, gain_one)[1](grad_normed)
    here = spots[:, :, None] == jnp.arange(length, dtype=jnp.int32)
    grad_skip = jnp.sum(
        jnp.where(
            here[..., None], grad_middle.reshape(slots_local, spots_seq, 1, width), 0.0
        ),
        axis=1,
    ).reshape(-1, width)
    leaving = (grad_skip + grad_inputs).astype(low)

    grad_attend = lax.psum_scatter(
        grad_attend.astype(low), "dp", scatter_dimension=0, tiled=True
    ).astype(jnp.float32)

    def other_grads(state):
        turn, total = state
        spread, pick = other_plan(turn)
        sent = left_product(spread, leaving).astype(low).reshape(sources, cap, width)
        got = lax.all_to_all(sent, everyone, split_axis=0, concat_axis=0, tiled=True)
        return turn + 1, total + left_product(pick, got.reshape(-1, width))

    given = left_product(spread, leaving).astype(low).reshape(sources, cap, width)
    gain_grads = jnp.concatenate([grad_gain_one, grad_gain_two, grad_final])
    gain_grads = jnp.pad(gain_grads.reshape(-1, 128), ((0, -gain_grads.shape[0] // 128 % 8), (0, 0)))
    given, gain_grads = exchange(
        9, (everyone, given, False), (("dp",), gain_grads, True)
    )
    table_grad = table_grad + left_product(pick, given.reshape(-1, width))
    table_grad = lax.while_loop(
        lambda state: state[0] < rounds, other_grads, (jnp.int32(1), table_grad)
    )[1]
    gain_grads = jnp.sum(gain_grads, axis=0).reshape(-1)
    own_gain_grads = gain_grads[: 2 * width]
    final_rows = gain_grads[2 * width : 3 * width].reshape(-1, 128)
    gain_part = gains.shape[1]
    grad_gains = lax.dynamic_slice_in_dim(own_gain_grads, dp_place * gain_part, gain_part)
    widen_squares = jnp.sum(jnp.square(grad_widen.astype(jnp.float32)))
    grad_widen = side_by_side(grad_widen)
    matrix_grads = (grad_attend[None], grad_output[None], grad_widen[None], grad_narrow[None])
    squares = sum((jnp.sum(g * g) for g in (grad_attend, grad_output, grad_narrow, table_grad)))
    squares = squares + widen_squares
    squares = squares + jnp.sum(grad_gains * grad_gains)
    last = jnp.concatenate(
        [final_rows, jnp.broadcast_to(squares, (16 - final_rows.shape[0] % 8 - 8, 128))], axis=0
    )
    last = exchange(11, (everyone, last, True))
    final_count = final_rows.shape[0]
    grad_final = (
        jnp.sum(last[:, :final_count].reshape(group_mod, group_dp, -1)[:, 0], axis=0)
    )
    squares = jnp.sum(last[:, final_count, 0]) + jnp.sum(grad_final * grad_final)
    final_part = final_gain.shape[0]
    grad_final = lax.dynamic_slice_in_dim(grad_final, mod_place * final_part, final_part)
    gradient_norm = jnp.sqrt(squares) / count_total
    factor = CLIP_LIMIT / jnp.maximum(gradient_norm, CLIP_LIMIT) / count_total
    params = (attend, output, widen, narrow, gains, table, final_gain)
    grads = matrix_grads + (grad_gains[None], table_grad, grad_final)
    firsts = (
        first_attend,
        first_output,
        first_widen,
        first_narrow,
        first_gains,
        first_table,
        first_final,
    )
    seconds = (
        second_attend,
        second_output,
        second_widen,
        second_narrow,
        second_gains,
        second_table,
        second_final,
    )
    rates = (RATE_MATRIX, RATE_MATRIX, RATE_MATRIX, RATE_MATRIX, RATE_GAIN, RATE_MATRIX, RATE_GAIN)
    decays = (DECAY_MATRIX, DECAY_MATRIX, DECAY_MATRIX, DECAY_MATRIX, 0.0, DECAY_MATRIX, 0.0)
    updated = [
        adam_step(w, g * factor, f, s, r, c)
        for w, g, f, s, r, c in zip(params, grads, firsts, seconds, rates, decays)
    ]
    return (
        loss_total / count_total,
        gradient_norm,
        *(entry[0] for entry in updated),
        *(entry[1] for entry in updated),
        *(entry[2] for entry in updated),
    )


def solution(mesh):
    placed = (
        P(None, "mod", None),
        P(None, "mod", None),
        P(None, "mod", None),
        P(None, "mod", None),
        P(None, "mod"),
        P("mod", "dp", None),
        P("mod", "dp", None),
        P("mod", "dp", None),
        P("mod", "dp", None),
        P("mod", "dp"),
        P(("mod", "dp"), None),
        P("mod"),
        P("mod", "dp", None),
        P("mod", "dp", None),
        P("mod", "dp", None),
        P("mod", "dp", None),
        P("mod", "dp"),
        P(("mod", "dp"), None),
        P("mod"),
        P("mod", "dp", None),
        P("mod", "dp", None),
        P("mod", "dp", None),
        P("mod", "dp", None),
        P("mod", "dp"),
        P(("mod", "dp"), None),
        P("mod"),
    )
    return jax.shard_map(
        on_device,
        mesh=mesh,
        in_specs=placed,
        out_specs=(
            P(),
            P(),
            P("mod", "dp", None),
            P("mod", "dp", None),
            P("mod", "dp", None),
            P("mod", "dp", None),
            P("mod", "dp"),
            P(("mod", "dp"), None),
            P("mod"),
            P("mod", "dp", None),
            P("mod", "dp", None),
            P("mod", "dp", None),
            P("mod", "dp", None),
            P("mod", "dp"),
            P(("mod", "dp"), None),
            P("mod"),
            P("mod", "dp", None),
            P("mod", "dp", None),
            P("mod", "dp", None),
            P("mod", "dp", None),
            P("mod", "dp"),
            P(("mod", "dp"), None),
            P("mod"),
        ),
        check_vma=False,
    )
```

```python
import functools
import math

import jax
import jax.numpy as jnp
import numpy as np
from jax import lax
from jax.experimental import pallas as pl
from jax.experimental.pallas import tpu as pltpu
from jax.sharding import PartitionSpec as P

HEAD_DIM = 64


NORM_EPS = 1e-05
CLIP_LIMIT = 0.05
BETA_ONE = 0.5
BETA_TWO = 0.5
ADAM_STEP = 10.0
ADAM_EPS = 1e-08
RATE_MATRIX = 0.03
RATE_GAIN = 0.3
DECAY_MATRIX = 0.1


def rms_scale(values, gain):
    return values * lax.rsqrt(jnp.mean(values * values, axis=-1, keepdims=True) + NORM_EPS) * gain


def rotary_tables(length):
    half = HEAD_DIM // 2
    inverse = 10000.0 ** (-np.arange(half, dtype=np.float32) / half)
    angle = np.arange(length, dtype=np.float32)[:, None] * inverse[None, :]
    cosine, sine = np.cos(angle), np.sin(angle)
    cosine = np.concatenate([cosine] * 4, axis=1).astype(np.float32)
    sine = np.concatenate([-sine, sine] * 2, axis=1).astype(np.float32)
    return jnp.asarray(cosine), jnp.asarray(sine)


def product(left, right):
    return jnp.dot(left, right, preferred_element_type=jnp.float32)


def left_product(left, right):
    return lax.dot_general(
        left, right, (((0,), (0,)), ((), ())), preferred_element_type=jnp.float32
    )


def right_product(left, right):
    return lax.dot_general(
        left, right, (((1,), (1,)), ((), ())), preferred_element_type=jnp.float32
    )


def adam_step(weight, grad, first, second, rate, decay):
    mean = BETA_ONE * first + (1.0 - BETA_ONE) * grad
    square = BETA_TWO * second + (1.0 - BETA_TWO) * grad * grad
    mean_hat = mean / (1.0 - BETA_ONE**ADAM_STEP)
    square_hat = square / (1.0 - BETA_TWO**ADAM_STEP)
    return (
        weight - rate * (mean_hat / (jnp.sqrt(square_hat) + ADAM_EPS) + decay * weight),
        mean,
        square,
    )


def one_hot(index, extent):
    return (index[..., None] == jnp.arange(extent, dtype=jnp.int32)).astype(jnp.bfloat16)


def exchange_kernel(groups, plan, *refs):
    count = len(plan)
    ins, outs = refs[:count], refs[count : 2 * count]
    sends, recvs = refs[2 * count : 3 * count], refs[3 * count : 4 * count]
    local = refs[4 * count]
    sizes = [math.prod(lax.axis_size(axis) for axis in axes) for axes in groups]
    places = []
    for axes in groups:
        place = lax.axis_index(axes[0])
        for axis in axes[1:]:
            place = place * lax.axis_size(axis) + lax.axis_index(axis)
        places.append(place)

    def device(group, index):
        axes = groups[group]
        if len(axes) == 1:
            return {axes[0]: index}
        inner = lax.axis_size(axes[1])
        return {axes[0]: index // inner, axes[1]: lax.rem(index, inner)}

    barrier = pltpu.get_barrier_semaphore()
    for group, size in enumerate(sizes):

        def greet(step, carry, group=group, size=size):
            peer = lax.rem(places[group] + step, size)
            pl.semaphore_signal(
                barrier,
                inc=1,
                device_id=device(group, peer),
                device_id_type=pl.DeviceIdType.MESH,
            )
            return carry

        lax.fori_loop(1, size, greet, 0)
    pl.semaphore_wait(barrier, sum(sizes) - len(sizes))

    def copy(item, step, arriving):
        group, shared = plan[item]
        size, place = sizes[group], places[group]
        peer = lax.rem(place + step, size)
        source = ins[item] if shared else ins[item].at[peer]
        slot = lax.rem(place + size - step, size) if arriving else place
        return pltpu.make_async_remote_copy(
            src_ref=source,
            dst_ref=outs[item].at[slot],
            send_sem=sends[item].at[step],
            recv_sem=recvs[item].at[step],
            device_id=device(group, peer),
            device_id_type=pl.DeviceIdType.MESH,
        )

    for item in range(count):

        def begin(step, carry, item=item):
            copy(item, step, False).start()
            return carry

        lax.fori_loop(1, sizes[plan[item][0]], begin, 0)
    own = []
    for item in range(count):
        group, shared = plan[item]
        source = ins[item] if shared else ins[item].at[places[group]]
        own.append(
            pltpu.make_async_copy(source, outs[item].at[places[group]], local.at[item])
        )
        own[-1].start()
    for item in range(count):
        own[item].wait()

        def finish(step, carry, item=item):
            copy(item, step, False).wait_send()
            copy(item, step, True).wait_recv()
            return carry

        lax.fori_loop(1, sizes[plan[item][0]], finish, 0)


def exchange(ident, *items):
    groups, plan, shapes, scratch = [], [], [], []
    for axes, array, shared in items:
        if axes not in groups:
            groups.append(axes)
        plan.append((groups.index(axes), shared))
        size = math.prod(lax.axis_size(axis) for axis in axes)
        shape = (size,) + array.shape if shared else array.shape
        shapes.append(jax.ShapeDtypeStruct(shape, array.dtype))
        scratch.append(pltpu.SemaphoreType.DMA((size,)))
    result = pl.pallas_call(
        functools.partial(exchange_kernel, groups, plan),
        out_shape=shapes,
        in_specs=[pl.BlockSpec(memory_space=pltpu.VMEM)] * len(items),
        out_specs=[pl.BlockSpec(memory_space=pltpu.VMEM)] * len(items),
        scratch_shapes=scratch + scratch + [pltpu.SemaphoreType.DMA((len(items),))],
        compiler_params=pltpu.CompilerParams(collective_id=ident, has_side_effects=True),
        name="exchange_%d" % ident,
    )(*(array for _, array, _ in items))
    return result[0] if len(items) == 1 else result


GATHER_ORDERS = ((0, 1, 2), (2, 0, 1), (1, 2, 0))


def chip_grid():
    group_mod, group_dp = lax.axis_size("mod"), lax.axis_size("dp")
    deep = math.gcd(group_mod, 4)
    return deep, group_mod // deep, group_dp // 2


def row_pieces(rows):
    part = rows // 64 * 16
    return (0, part), (part, rows - 2 * part), (rows - part, part)


def chip_place(sizes):
    mod, dp = lax.axis_index("mod"), lax.axis_index("dp")
    return [mod // sizes[1], lax.rem(mod, sizes[1]), dp // 2], lax.rem(dp, 2)


def chip_device(sizes, at, core):
    return {"mod": at[0] * sizes[1] + at[1], "dp": at[2] * 2 + core}


def shifted(sizes, at, axis, step):
    at = list(at)
    at[axis] = lax.rem(at[axis] + step, sizes[axis])
    return at


def greet_lines(sizes, at, core):
    barrier = pltpu.get_barrier_semaphore()
    targets = [chip_device(sizes, at, 1 - core)]
    for axis in range(3):
        for step in range(1, sizes[axis]):
            targets.append(chip_device(sizes, shifted(sizes, at, axis, step), core))
    for target in targets:
        pl.semaphore_signal(
            barrier, inc=1, device_id=target, device_id_type=pl.DeviceIdType.MESH
        )
    pl.semaphore_wait(barrier, len(targets))


def line_copies(sizes):
    return sum(len(GATHER_ORDERS) * (size - 1) for size in sizes)


def gather_kernel(sizes, rows, in_ref, out_ref, send, recv, pair_send, pair_recv, local):
    at, core = chip_place(sizes)
    greet_lines(sizes, at, core)
    pieces = row_pieces(rows)
    keys = {}
    for piece, order in enumerate(GATHER_ORDERS):
        for stage, axis in enumerate(order):
            for step in range(1, sizes[axis]):
                keys[piece, stage, step] = len(keys)

    def region(at, done, core, piece):
        start, count = pieces[piece]
        index = tuple(slice(None) if axis in done else at[axis] for axis in range(3))
        return out_ref.at[index + (core, pl.ds(start, count))]

    def remote(source, target, sems, index, at, core):
        return pltpu.make_async_remote_copy(
            src_ref=source,
            dst_ref=target,
            send_sem=sems[0].at[index],
            recv_sem=sems[1].at[index],
            device_id=chip_device(sizes, at, core),
            device_id_type=pl.DeviceIdType.MESH,
        )

    def line(piece, stage, step, arriving):
        order = GATHER_ORDERS[piece]
        axis, done = order[stage], order[:stage]
        peer = shifted(sizes, at, axis, step)
        origin = shifted(sizes, at, axis, sizes[axis] - step)
        target = region(origin if arriving else at, done, core, piece)
        source = region(at, done, core, piece)
        if stage == 0:
            source = in_ref.at[pl.ds(*pieces[piece])]
        return remote(source, target, (send, recv), keys[piece, stage, step], peer, core)

    def pair(piece, stage, step, arriving):
        order = GATHER_ORDERS[piece]
        axis, done = order[stage], order[:stage]
        origin = shifted(sizes, at, axis, sizes[axis] - step)
        source = region(origin, done, core, piece)
        target = region(origin, done, 1 - core if arriving else core, piece)
        index = keys[piece, stage, step]
        return remote(source, target, (pair_send, pair_recv), index, at, 1 - core)

    def pair_own(arriving):
        target = out_ref.at[at[0], at[1], at[2], 1 - core if arriving else core]
        return remote(in_ref, target, (pair_send, pair_recv), len(keys), at, 1 - core)

    own = pltpu.make_async_copy(in_ref, out_ref.at[at[0], at[1], at[2], core], local)
    own.start()
    pair_own(False).start()
    for stage in range(4):
        for piece, order in enumerate(GATHER_ORDERS):
            if stage > 0:
                for step in range(1, sizes[order[stage - 1]]):
                    line(piece, stage - 1, step, True).wait_recv()
                if stage == 1 and piece == 0:
                    own.wait()
            if stage < 3:
                for step in range(1, sizes[order[stage]]):
                    line(piece, stage, step, False).start()
            if stage > 0:
                for step in range(1, sizes[order[stage - 1]]):
                    pair(piece, stage - 1, step, False).start()
    for piece, stage, step in keys:
        line(piece, stage, step, False).wait_send()
        pair(piece, stage, step, False).wait_send()
        pair(piece, stage, step, True).wait_recv()
    pair_own(False).wait_send()
    pair_own(True).wait_recv()


def gather_rows(ident, rows):
    sizes = chip_grid()
    count, width = rows.shape
    copies = line_copies(sizes)
    dma = pltpu.SemaphoreType.DMA
    gathered = pl.pallas_call(
        functools.partial(gather_kernel, sizes, count),
        out_shape=jax.ShapeDtypeStruct(sizes + (2, count, width), rows.dtype),
        in_specs=[pl.BlockSpec(memory_space=pltpu.VMEM)],
        out_specs=pl.BlockSpec(memory_space=pltpu.VMEM),
        scratch_shapes=[dma((copies,)), dma((copies,)), dma((copies + 1,)), dma((copies + 1,)), dma],
        compiler_params=pltpu.CompilerParams(collective_id=ident, has_side_effects=True),
        name="gather_rows",
    )(rows)
    return gathered.reshape(-1, width)


def scatter_kernel(sizes, rows, in_ref, out_ref, acc, arrived, *rest):
    slots, (send, recv, pair_send, pair_recv, local) = rest[:-5], rest[-5:]
    at, core = chip_place(sizes)
    greet_lines(sizes, at, core)
    pieces = row_pieces(rows)
    orders = [order[::-1] for order in GATHER_ORDERS]
    keys = {}
    for piece, order in enumerate(orders):
        for stage, axis in enumerate(order):
            for step in range(1, sizes[axis]):
                keys[piece, stage, step] = len(keys)

    def line(piece, stage, step):
        order = orders[piece]
        axis, done = order[stage], order[:stage]
        peer = shifted(sizes, at, axis, step)
        index = tuple(
            peer[a] if a == axis else at[a] if a in done else slice(None) for a in range(3)
        )
        key = keys[piece, stage, step]
        return pltpu.make_async_remote_copy(
            src_ref=acc.at[index + (pl.ds(*pieces[piece]),)],
            dst_ref=slots[3 * piece + stage].at[step - 1],
            send_sem=send.at[key],
            recv_sem=recv.at[key],
            device_id=chip_device(sizes, peer, core),
            device_id_type=pl.DeviceIdType.MESH,
        )

    loads, pairs = [], []
    for piece in range(3):
        part = pl.ds(*pieces[piece])
        pairs.append(
            pltpu.make_async_remote_copy(
                src_ref=in_ref.at[:, :, :, 1 - core, part],
                dst_ref=arrived.at[:, :, :, part],
                send_sem=pair_send.at[piece],
                recv_sem=pair_recv.at[piece],
                device_id=chip_device(sizes, at, 1 - core),
                device_id_type=pl.DeviceIdType.MESH,
            )
        )
        pairs[-1].start()
        loads.append(
            pltpu.make_async_copy(
                in_ref.at[:, :, :, core, part], acc.at[:, :, :, part], local.at[piece]
            )
        )
        loads[-1].start()

    def add(piece, stage):
        order = orders[piece]
        done = order[:stage]
        left = [axis for axis in range(3) if axis not in done]
        part = pl.ds(*pieces[piece])

        def one(index, carry):
            where, inner = list(at), []
            for axis in reversed(left):
                where[axis] = lax.rem(index, sizes[axis])
                index = index // sizes[axis]
                inner.insert(0, where[axis])
            spot = tuple(where) + (part,)
            total = acc[spot].astype(jnp.float32)
            if stage == 0:
                total = total + arrived[spot].astype(jnp.float32)
            else:
                taken = slots[3 * piece + stage - 1]
                for step in range(taken.shape[0]):
                    total = total + taken[(step,) + tuple(inner)].astype(jnp.float32)
            if stage == 3:
                out_ref[part] = total
            else:
                acc[spot] = total.astype(acc.dtype)
            return carry

        lax.fori_loop(0, math.prod(sizes[axis] for axis in left), one, 0)

    for stage in range(4):
        for piece, order in enumerate(orders):
            if stage == 0:
                loads[piece].wait()
                pairs[piece].wait_recv()
            else:
                for step in range(1, sizes[order[stage - 1]]):
                    line(piece, stage - 1, step).wait_recv()
            add(piece, stage)
            if stage < 3:
                for step in range(1, sizes[order[stage]]):
                    line(piece, stage, step).start()
    for piece in range(3):
        pairs[piece].wait_send()
    for piece, stage, step in keys:
        line(piece, stage, step).wait_send()


def scatter_rows(ident, parts):
    sizes = chip_grid()
    width = parts.shape[1]
    count = parts.shape[0] // (2 * math.prod(sizes))
    copies = line_copies(sizes)
    dma = pltpu.SemaphoreType.DMA
    slots = []
    for piece, order in enumerate(GATHER_ORDERS):
        order = order[::-1]
        for stage, axis in enumerate(order):
            left = tuple(sizes[a] for a in range(3) if a not in order[: stage + 1])
            shape = (sizes[axis] - 1,) + left + (row_pieces(count)[piece][1], width)
            slots.append(pltpu.VMEM(shape, parts.dtype))
    return pl.pallas_call(
        functools.partial(scatter_kernel, sizes, count),
        out_shape=jax.ShapeDtypeStruct((count, width), jnp.float32),
        in_specs=[pl.BlockSpec(memory_space=pl.ANY)],
        out_specs=pl.BlockSpec(memory_space=pltpu.VMEM),
        scratch_shapes=[
            pltpu.VMEM(sizes + (count, width), parts.dtype),
            pltpu.VMEM(sizes + (count, width), parts.dtype),
            *slots,
            dma((copies,)),
            dma((copies,)),
            dma((3,)),
            dma((3,)),
            dma((3,)),
        ],
        compiler_params=pltpu.CompilerParams(collective_id=ident, has_side_effects=True),
        name="scatter_rows",
    )(parts.reshape(sizes + (2, count, width)))


def totals_kernel(in_ref, out_ref, arrived, mine, send, recv, back_send, back_recv):
    group_mod, group_dp = lax.axis_size("mod"), lax.axis_size("dp")
    size = group_mod * group_dp
    place = lax.axis_index("mod") * group_dp + lax.axis_index("dp")

    def device(index):
        return {"mod": index // group_dp, "dp": lax.rem(index, group_dp)}

    barrier = pltpu.get_barrier_semaphore()

    def greet(step, carry):
        pl.semaphore_signal(
            barrier,
            inc=1,
            device_id=device(lax.rem(place + step, size)),
            device_id_type=pl.DeviceIdType.MESH,
        )
        return carry

    def ahead(step, slot):
        peer = lax.rem(place + step, size)
        return pltpu.make_async_remote_copy(
            src_ref=in_ref.at[peer],
            dst_ref=arrived.at[slot],
            send_sem=send.at[step],
            recv_sem=recv.at[step],
            device_id=device(peer),
            device_id_type=pl.DeviceIdType.MESH,
        )

    def back(step, slot):
        return pltpu.make_async_remote_copy(
            src_ref=mine,
            dst_ref=out_ref.at[slot],
            send_sem=back_send.at[step],
            recv_sem=back_recv.at[step],
            device_id=device(lax.rem(place + step, size)),
            device_id_type=pl.DeviceIdType.MESH,
        )

    def begin(copy):
        def one(step, carry):
            copy(step, place).start()
            return carry

        lax.fori_loop(1, size, one, 0)

    def finish(copy):
        def one(step, carry):
            copy(step, place).wait_send()
            copy(step, lax.rem(place + size - step, size)).wait_recv()
            return carry

        lax.fori_loop(1, size, one, 0)

    lax.fori_loop(1, size, greet, 0)
    pl.semaphore_wait(barrier, size - 1)
    begin(ahead)
    arrived[place] = in_ref[place]
    finish(ahead)
    tops = arrived[:, 0:1]
    top = jnp.max(tops, axis=0)
    total = jnp.sum(arrived[:, 1:2] * jnp.exp(tops - top[None]), axis=0)
    hit = jnp.sum(arrived[:, 2:3], axis=0)
    line = lax.broadcasted_iota(jnp.int32, mine.shape, 0)
    mine[...] = jnp.where(line == 0, top + jnp.log(total), jnp.where(line == 1, hit, 0.0))
    out_ref[place] = mine[...]
    begin(back)
    finish(back)


def totals_call(ident, stats):
    dma = pltpu.SemaphoreType.DMA((stats.shape[0],))
    return pl.pallas_call(
        totals_kernel,
        out_shape=jax.ShapeDtypeStruct(stats.shape, stats.dtype),
        in_specs=[pl.BlockSpec(memory_space=pltpu.VMEM)],
        out_specs=pl.BlockSpec(memory_space=pltpu.VMEM),
        scratch_shapes=[
            pltpu.VMEM(stats.shape, stats.dtype),
            pltpu.VMEM(stats.shape[1:], stats.dtype),
            dma,
            dma,
            dma,
            dma,
        ],
        compiler_params=pltpu.CompilerParams(collective_id=ident, has_side_effects=True),
        name="totals",
    )(stats)


def side_by_side(blocks):
    count, rows, columns = blocks.shape
    if columns % 128:
        return jnp.concatenate(list(blocks.astype(jnp.float32)), axis=1)

    def place(in_ref, out_ref):
        out_ref[...] = in_ref[0].astype(jnp.float32)

    return pl.pallas_call(
        place,
        grid=(count,),
        out_shape=jax.ShapeDtypeStruct((rows, count * columns), jnp.float32),
        in_specs=[pl.BlockSpec((1, rows, columns), lambda i: (i, 0, 0))],
        out_specs=pl.BlockSpec((rows, columns), lambda i: (0, i)),
        name="side_by_side",
    )(blocks)


HEAD_ROWS = 256


def scores_kernel(rows_ref, table_ref, wanted_ref, out_ref, logits_ref):
    logits = right_product(table_ref[...], rows_ref[...])
    logits_ref[...] = logits
    hits = lax.broadcasted_iota(jnp.int32, logits.shape, 0) == wanted_ref[...]
    top = jnp.max(logits, axis=0, keepdims=True)
    total = jnp.sum(jnp.exp(logits - top), axis=0, keepdims=True)
    hit = jnp.sum(jnp.where(hits, logits, 0.0), axis=0, keepdims=True)
    count, lines, part = out_ref.shape
    line = lax.broadcasted_iota(jnp.int32, (lines, part), 0)
    for block in range(count):
        at = slice(block * part, (block + 1) * part)
        out_ref[block] = jnp.where(
            line == 0, top[:, at], jnp.where(line == 1, total[:, at], hit[:, at])
        )


def scores_call(rows, table, wanted, part):
    step = math.gcd(HEAD_ROWS, rows.shape[0])
    return pl.pallas_call(
        scores_kernel,
        grid=(rows.shape[0] // step,),
        out_shape=[
            jax.ShapeDtypeStruct((rows.shape[0] // part, 8, part), jnp.float32),
            jax.ShapeDtypeStruct((table.shape[0], rows.shape[0]), jnp.float32),
        ],
        in_specs=[
            pl.BlockSpec((step, rows.shape[1]), lambda i: (i, 0)),
            pl.BlockSpec(table.shape, lambda i: (0, 0)),
            pl.BlockSpec((1, step), lambda i: (0, i)),
        ],
        out_specs=[
            pl.BlockSpec((step // part, 8, part), lambda i: (i, 0, 0)),
            pl.BlockSpec((table.shape[0], step), lambda i: (0, i)),
        ],
        name="scores",
    )(rows, table, wanted[None])


def norm_kernel(group_mod, group_dp, final_lines, in_ref, out_ref, gathered, send, recv, local):
    exchange_kernel([("mod", "dp")], [(0, True)], in_ref, gathered, send, recv, local)
    final = gathered[0]
    for mod in range(1, group_mod):
        final = final + gathered[mod * group_dp]
    line = lax.broadcasted_iota(jnp.int32, final.shape, 0)
    final = jnp.where(line < final_lines, final, 0.0)
    squares = jnp.sum(jnp.sum(final * final, axis=1, keepdims=True), axis=0, keepdims=True)
    total = jnp.sum(gathered[...], axis=0) + squares
    out_ref[...] = jnp.where(line < final_lines, final, total)


def norm_call(ident, last, final_lines):
    group_mod, group_dp = lax.axis_size("mod"), lax.axis_size("dp")
    size = group_mod * group_dp
    dma = pltpu.SemaphoreType.DMA
    return pl.pallas_call(
        functools.partial(norm_kernel, group_mod, group_dp, final_lines),
        out_shape=jax.ShapeDtypeStruct(last.shape, last.dtype),
        in_specs=[pl.BlockSpec(memory_space=pltpu.VMEM)],
        out_specs=pl.BlockSpec(memory_space=pltpu.VMEM),
        scratch_shapes=[
            pltpu.VMEM((size,) + last.shape, last.dtype),
            dma((size,)),
            dma((size,)),
            dma((1,)),
        ],
        compiler_params=pltpu.CompilerParams(collective_id=ident, has_side_effects=True),
        name="norm",
    )(last)


GROUP_SEQS = 4


def wide_table(table_ref, tokens, width):
    table = table_ref[...]
    table = jnp.concatenate([table] * (tokens // table.shape[0]), axis=0)
    return jnp.concatenate([table] * (width // table.shape[1]), axis=1)


def turned(values, cosine, sine):
    width = values.shape[-1]
    half = HEAD_DIM // 2
    lane = lax.broadcasted_iota(jnp.int32, values.shape, 1)
    other = jnp.where(
        lane % HEAD_DIM < half,
        pltpu.roll(values, width - half, 1),
        pltpu.roll(values, half, 1),
    )
    return values * cosine + other * sine


def head_spread(values, heads):
    rows, width = values.shape
    lane = lax.broadcasted_iota(jnp.int32, (heads, rows, width), 2)
    head = lax.broadcasted_iota(jnp.int32, (heads, rows, width), 0)
    return jnp.where(lane // HEAD_DIM == head, values[None], jnp.zeros((), values.dtype))


def head_fold(values, heads):
    rows, width = values.shape
    values = values.reshape(heads, rows // heads, width)
    lane = lax.broadcasted_iota(jnp.int32, values.shape, 2)
    head = lax.broadcasted_iota(jnp.int32, values.shape, 0)
    return jnp.sum(jnp.where(lane // HEAD_DIM == head, values, 0.0), axis=0)


def attention_parts(length, spots_ref, mixed_ref, cosine_ref, sine_ref):
    tokens, width = mixed_ref.shape[0], mixed_ref.shape[1] // 3
    heads = width // HEAD_DIM
    cosine = wide_table(cosine_ref, tokens, width)
    sine = wide_table(sine_ref, tokens, width)
    spot = spots_ref[...]
    key = lax.broadcasted_iota(jnp.int32, (spot.shape[0], tokens), 1)
    chosen = key == spot
    seen = (key <= spot) & (key >= spot - spot % length)
    queries = turned(mixed_ref[:, :width], cosine, sine).astype(jnp.bfloat16)
    queries = product(chosen.astype(jnp.bfloat16), queries)
    queries = head_spread(queries, heads).reshape(-1, width).astype(jnp.bfloat16)
    keys_in = turned(mixed_ref[:, width : 2 * width], cosine, sine).astype(jnp.bfloat16)
    values = mixed_ref[:, 2 * width :].astype(jnp.bfloat16)
    raw = right_product(queries, keys_in).reshape(heads, -1, tokens)
    scores = jnp.where(seen[None], raw * HEAD_DIM ** (-0.5), -1e30).reshape(-1, tokens)
    top = jnp.max(scores, axis=1, keepdims=True)
    terms = jnp.exp(scores - top)
    chances = terms / jnp.sum(terms, axis=1, keepdims=True)
    return chosen, queries, keys_in, values, chances, cosine, sine


def attention_kernel(
    length, spots_ref, mixed_ref, inputs_ref, cosine_ref, sine_ref, heads_ref, picked_ref
):
    heads = inputs_ref.shape[1] // HEAD_DIM
    chosen, _, _, values, chances, _, _ = attention_parts(
        length, spots_ref, mixed_ref, cosine_ref, sine_ref
    )
    spread = product(chances.astype(jnp.bfloat16), values)
    heads_ref[...] = head_fold(spread, heads).astype(jnp.bfloat16)
    picked_ref[...] = product(chosen.astype(jnp.bfloat16), inputs_ref[...])


def attention_back_kernel(
    length, spots_ref, mixed_ref, grad_ref, cosine_ref, sine_ref, out_ref
):
    width = grad_ref.shape[1]
    heads = width // HEAD_DIM
    chosen, queries, keys_in, values, chances, cosine, sine = attention_parts(
        length, spots_ref, mixed_ref, cosine_ref, sine_ref
    )
    grad_heads = head_spread(grad_ref[...].astype(jnp.float32), heads)
    grad_heads = grad_heads.reshape(-1, width).astype(jnp.bfloat16)
    grad_values = left_product(chances.astype(jnp.bfloat16), grad_heads)
    grad_chances = right_product(grad_heads, values)
    delta = jnp.sum(chances * grad_chances, axis=1, keepdims=True)
    grad_raw = (chances * (grad_chances - delta) * HEAD_DIM ** (-0.5)).astype(jnp.bfloat16)
    grad_queries = head_fold(product(grad_raw, keys_in), heads)
    grad_queries = lax.dot_general(
        chosen.astype(jnp.float32),
        grad_queries,
        (((0,), (0,)), ((), ())),
        precision=lax.Precision.HIGHEST,
        preferred_element_type=jnp.float32,
    )
    grad_keys = left_product(grad_raw, queries)
    out_ref[:, :width] = turned(grad_queries, cosine, -sine).astype(jnp.bfloat16)
    out_ref[:, width : 2 * width] = turned(grad_keys, cosine, -sine).astype(jnp.bfloat16)
    out_ref[:, 2 * width :] = grad_values.astype(jnp.bfloat16)


def attention_call(body, length, operands, tables, outs, name):
    sequences = operands[1].shape[0] // length
    steps = sequences // math.gcd(GROUP_SEQS, sequences)

    def block(array):
        return pl.BlockSpec((array.shape[0] // steps, array.shape[1]), lambda i: (i, 0))

    fixed = [pl.BlockSpec(table.shape, lambda i: (0, 0)) for table in tables]
    return pl.pallas_call(
        functools.partial(body, length),
        grid=(steps,),
        out_shape=outs,
        in_specs=[block(array) for array in operands] + fixed,
        out_specs=[block(array) for array in outs],
        name=name,
    )(*operands, *tables)


def on_device(
    token_ids,
    targets,
    positions,
    loss_mask,
    paths,
    attend,
    output,
    widen,
    narrow,
    gains,
    table,
    final_gain,
    first_attend,
    first_output,
    first_widen,
    first_narrow,
    first_gains,
    first_table,
    first_final,
    second_attend,
    second_output,
    second_widen,
    second_narrow,
    second_gains,
    second_table,
    second_final,
):
    group_dp = lax.axis_size("dp")
    group_mod = lax.axis_size("mod")
    dp_place = lax.axis_index("dp")
    mod_place = lax.axis_index("mod")
    everyone = ("mod", "dp")
    place = mod_place * group_dp + dp_place
    sources = group_mod * group_dp
    micro, per_mod, length = token_ids.shape
    spots_seq = positions.shape[2]
    seq_dev = per_mod // group_dp
    shard_rows, width = table.shape
    heads = width // HEAD_DIM
    slots = micro * sources
    slots_local = slots // group_dp
    low = jnp.bfloat16

    mixing = lax.all_gather(
        jnp.concatenate([attend[0], output[0]], axis=1).astype(low), "dp", axis=0, tiled=True
    )
    attend_low, output_low = mixing[:, : 3 * width], mixing[:, 3 * width :]
    hidden = narrow.shape[1]
    widen_low = jnp.stack(
        [widen[0, :, i * hidden : (i + 1) * hidden].astype(low) for i in range(group_dp)]
    )
    narrow_low = narrow[0].astype(low)
    table_low = table.astype(low)

    fields = jnp.concatenate(
        [token_ids, positions, targets, loss_mask, paths[..., None]], axis=-1
    )
    fields, gain_parts, final_parts = exchange(
        0,
        (("mod",), fields.reshape(micro * per_mod, -1), True),
        (("dp",), jnp.broadcast_to(gains.astype(low), (16, gains.shape[1])), True),
        (("mod",), jnp.broadcast_to(final_gain.astype(low)[None], (16, final_gain.shape[0])), True),
    )
    own_gains = gain_parts[:, 0].reshape(-1).astype(jnp.float32)
    gain_one, gain_two = own_gains[:width], own_gains[width:]
    gain_final = final_parts[:, 0].reshape(-1).astype(jnp.float32)
    fields = fields.reshape(group_mod, micro, per_mod, -1).transpose(1, 0, 2, 3)
    fields = fields.reshape(slots, seq_dev, -1)
    own = lax.dynamic_slice_in_dim(fields, dp_place * slots_local, slots_local)
    own_match = own[..., -1] == mod_place
    own = jnp.sum(jnp.where(own_match[..., None], own[..., : length + spots_seq], 0), axis=1)
    own_tokens = own[:, :length].reshape(-1)
    spots = own[:, length:]
    held = jnp.repeat(jnp.any(own_match, axis=1), length)
    match = fields[None, ..., -1] == jnp.arange(group_mod, dtype=jnp.int32)[:, None, None]
    scoring = jnp.sum(
        jnp.where(match[..., None], fields[None, ..., length + spots_seq : -1], 0), axis=2
    )
    wanted = scoring[..., :spots_seq].reshape(-1)
    counted = scoring[..., spots_seq:].reshape(-1).astype(jnp.float32)
    count_total = jnp.sum(counted)

    shard = own_tokens // shard_rows
    row = own_tokens % shard_rows
    key = jnp.where(held, own_tokens, -1)
    order = jnp.arange(key.shape[0], dtype=jnp.int32)
    repeated = jnp.any((key[:, None] == key[None, :]) & (order[None, :] < order[:, None]), axis=1)
    leading = held & ~repeated
    rank = jnp.sum(
        (
            leading[None, :] & (shard[None, :] == shard[:, None]) & (key[None, :] < key[:, None])
        ).astype(jnp.int32),
        axis=1,
    )
    expected = -(-slots_local * length // sources)
    cap = -(-3 * expected // 16) * 8
    cap = min(max(cap, 16), -(-shard_rows // 8) * 8, 112)
    own_rounds = jnp.max(jnp.where(leading, rank // cap, 0)) + 1

    def ask(turn):
        slot = rank - turn * cap
        inside = held & (slot >= 0) & (slot < cap)
        slot = jnp.where(inside, shard * cap + slot, -1)
        asked = jnp.sum(
            jnp.where(
                leading[None, :]
                & (slot[None, :] == jnp.arange(sources * cap, dtype=jnp.int32)[:, None]),
                row[None, :] + 1,
                0,
            ),
            axis=1,
        ).reshape(sources, cap)
        return slot, asked

    slot, asked = ask(0)
    message = jnp.concatenate(
        [asked, jnp.broadcast_to(own_rounds, (sources, 128 - cap))], axis=1
    )
    message = exchange(
        1, (everyone, jnp.broadcast_to(message[:, None], (sources, 8, 128)), False)
    )
    rounds = jnp.max(message[:, 0, cap])
    spread = one_hot(slot, sources * cap)
    pick = one_hot(message[:, 0, :cap].reshape(-1) - 1, shard_rows)

    def other_plan(turn):
        slot, asked = ask(turn)
        asked = lax.all_to_all(asked, everyone, split_axis=0, concat_axis=0, tiled=True)
        return one_hot(slot, sources * cap), one_hot(asked.reshape(-1) - 1, shard_rows)

    def other_rows(state):
        turn, rows = state
        spread, pick = other_plan(turn)
        sent = product(pick, table_low).astype(low).reshape(sources, cap, width)
        got = lax.all_to_all(sent, everyone, split_axis=0, concat_axis=0, tiled=True)
        return turn + 1, rows + product(spread, got.reshape(-1, width)).astype(low)

    sent = product(pick, table_low).astype(low).reshape(sources, cap, width)
    got, widen_low = exchange(2, (everyone, sent, False), (("dp",), widen_low, False))
    widen_low = widen_low.reshape(width, hidden)
    inputs = product(spread, got.reshape(-1, width)).astype(low)
    inputs = lax.while_loop(
        lambda state: state[0] < rounds, other_rows, (jnp.int32(1), inputs)
    )[1]

    group = math.gcd(GROUP_SEQS, slots_local)
    tables = rotary_tables(length)
    flat_spots = spots + (jnp.arange(slots_local, dtype=jnp.int32) % group)[:, None] * length
    flat_spots = flat_spots.reshape(-1, 1)
    inputs_wide = inputs.astype(jnp.float32)
    normed_one = rms_scale(inputs_wide, gain_one).astype(low)
    mixed = product(normed_one, attend_low)
    picked_rows = slots_local * spots_seq
    heads_out, picked_inputs = attention_call(
        attention_kernel,
        length,
        (flat_spots, mixed, inputs),
        tables,
        [
            jax.ShapeDtypeStruct((picked_rows, width), low),
            jax.ShapeDtypeStruct((picked_rows, width), jnp.float32),
        ],
        "attention",
    )
    middle = picked_inputs + product(heads_out, output_low)

    def sum_parts(ident, parts):
        parts = parts.astype(low).reshape(group_dp, picked_rows, width)
        return jnp.sum(exchange(ident, (("dp",), parts, False)).astype(jnp.float32), axis=0)

    normed_two = rms_scale(middle, gain_two).astype(low)
    normed_all = exchange(3, (("dp",), normed_two, True)).reshape(-1, width)
    upper = product(normed_all, widen_low)
    gelu = lambda value: jax.nn.gelu(value, approximate=True)
    activated = gelu(upper).astype(low)
    lifted = sum_parts(4, product(activated, narrow_low))
    returned = (middle + lifted).astype(low).astype(jnp.float32)

    final, final_back = jax.vjp(rms_scale, returned, gain_final)
    scored = gather_rows(12, final.astype(low))
    target_row = wanted - place * shard_rows
    stats, logits = scores_call(scored, table_low, target_row, picked_rows)
    totals = totals_call(5, stats)
    log_total = totals[:, 0].reshape(-1)
    loss_total = jnp.sum(counted * (log_total - totals[:, 1].reshape(-1)))
    hits = target_row[None, :] == jnp.arange(shard_rows, dtype=jnp.int32)[:, None]
    grad_logits = (
        counted[None] * (jnp.exp(logits - log_total[None]) - hits.astype(jnp.float32))
    ).astype(low)
    table_grad = product(grad_logits, scored)
    grad_picked = scatter_rows(13, left_product(grad_logits, table_low).astype(low))

    grad_returned, grad_final = final_back(grad_picked)
    incoming = grad_returned.astype(low)
    incoming_all = exchange(7, (("dp",), incoming, True)).reshape(-1, width)
    grad_narrow = left_product(activated, incoming_all)
    grad_act = right_product(incoming_all, narrow_low)
    grad_upper = jax.vjp(gelu, upper)[1](grad_act)[0].astype(low)
    grad_widen = left_product(normed_all, grad_upper).astype(low)
    grad_widen = grad_widen.reshape(group_dp, -1, hidden)
    grad_normed_two = sum_parts(8, right_product(grad_upper, widen_low))
    grad_middle, grad_gain_two = jax.vjp(rms_scale, middle, gain_two)[1](grad_normed_two)
    grad_middle = grad_middle + incoming.astype(jnp.float32)

    branch_grad = grad_middle.astype(low)
    grad_output = lax.psum_scatter(
        left_product(heads_out, branch_grad).astype(low), "dp", scatter_dimension=0, tiled=True
    ).astype(jnp.float32)
    grad_heads = right_product(branch_grad, output_low).astype(low)
    (grad_mixed,) = attention_call(
        attention_back_kernel,
        length,
        (flat_spots, mixed, grad_heads),
        tables,
        [jax.ShapeDtypeStruct(mixed.shape, low)],
        "attention_back",
    )
    grad_attend = left_product(normed_one, grad_mixed)
    grad_normed = right_product(grad_mixed, attend_low)
    grad_inputs, grad_gain_one = jax.vjp(rms_scale, inputs_wide, gain_one)[1](grad_normed)
    here = spots[:, :, None] == jnp.arange(length, dtype=jnp.int32)
    grad_skip = jnp.sum(
        jnp.where(
            here[..., None], grad_middle.reshape(slots_local, spots_seq, 1, width), 0.0
        ),
        axis=1,
    ).reshape(-1, width)
    leaving = (grad_skip + grad_inputs).astype(low)

    grad_attend = lax.psum_scatter(
        grad_attend.astype(low), "dp", scatter_dimension=0, tiled=True
    ).astype(jnp.float32)

    def other_grads(state):
        turn, total = state
        spread, pick = other_plan(turn)
        sent = left_product(spread, leaving).astype(low).reshape(sources, cap, width)
        got = lax.all_to_all(sent, everyone, split_axis=0, concat_axis=0, tiled=True)
        return turn + 1, total + left_product(pick, got.reshape(-1, width))

    given = left_product(spread, leaving).astype(low).reshape(sources, cap, width)
    gain_grads = jnp.concatenate([grad_gain_one, grad_gain_two, grad_final])
    gain_grads = jnp.pad(gain_grads.reshape(-1, 128), ((0, -gain_grads.shape[0] // 128 % 8), (0, 0)))
    given, gain_grads, grad_widen = exchange(
        9, (everyone, given, False), (("dp",), gain_grads, True), (("dp",), grad_widen, False)
    )
    table_grad = table_grad + left_product(pick, given.reshape(-1, width))
    table_grad = lax.while_loop(
        lambda state: state[0] < rounds, other_grads, (jnp.int32(1), table_grad)
    )[1]
    gain_grads = jnp.sum(gain_grads, axis=0).reshape(-1)
    own_gain_grads = gain_grads[: 2 * width]
    final_rows = gain_grads[2 * width : 3 * width].reshape(-1, 128)
    gain_part = gains.shape[1]
    grad_gains = lax.dynamic_slice_in_dim(own_gain_grads, dp_place * gain_part, gain_part)
    widen_squares = jnp.sum(jnp.square(grad_widen.astype(jnp.float32)))
    grad_widen = side_by_side(grad_widen)
    matrix_grads = (grad_attend[None], grad_output[None], grad_widen[None], grad_narrow[None])
    squares = sum((jnp.sum(g * g) for g in (grad_attend, grad_output, grad_narrow, table_grad)))
    squares = squares + widen_squares
    squares = squares + jnp.sum(grad_gains * grad_gains)
    last = jnp.concatenate(
        [final_rows, jnp.broadcast_to(squares, (16 - final_rows.shape[0] % 8 - 8, 128))], axis=0
    )
    final_count = final_rows.shape[0]
    last = norm_call(11, last, final_count)
    grad_final = last[:final_count].reshape(-1)
    squares = last[final_count, 0]
    final_part = final_gain.shape[0]
    grad_final = lax.dynamic_slice_in_dim(grad_final, mod_place * final_part, final_part)
    gradient_norm = jnp.sqrt(squares) / count_total
    factor = CLIP_LIMIT / jnp.maximum(gradient_norm, CLIP_LIMIT) / count_total
    params = (attend, output, widen, narrow, gains, table, final_gain)
    grads = matrix_grads + (grad_gains[None], table_grad, grad_final)
    firsts = (
        first_attend,
        first_output,
        first_widen,
        first_narrow,
        first_gains,
        first_table,
        first_final,
    )
    seconds = (
        second_attend,
        second_output,
        second_widen,
        second_narrow,
        second_gains,
        second_table,
        second_final,
    )
    rates = (RATE_MATRIX, RATE_MATRIX, RATE_MATRIX, RATE_MATRIX, RATE_GAIN, RATE_MATRIX, RATE_GAIN)
    decays = (DECAY_MATRIX, DECAY_MATRIX, DECAY_MATRIX, DECAY_MATRIX, 0.0, DECAY_MATRIX, 0.0)
    updated = [
        adam_step(w, g * factor, f, s, r, c)
        for w, g, f, s, r, c in zip(params, grads, firsts, seconds, rates, decays)
    ]
    return (
        loss_total / count_total,
        gradient_norm,
        *(entry[0] for entry in updated),
        *(entry[1] for entry in updated),
        *(entry[2] for entry in updated),
    )


def solution(mesh):
    placed = (
        P(None, "mod", None),
        P(None, "mod", None),
        P(None, "mod", None),
        P(None, "mod", None),
        P(None, "mod"),
        P("mod", "dp", None),
        P("mod", "dp", None),
        P("mod", "dp", None),
        P("mod", "dp", None),
        P("mod", "dp"),
        P(("mod", "dp"), None),
        P("mod"),
        P("mod", "dp", None),
        P("mod", "dp", None),
        P("mod", "dp", None),
        P("mod", "dp", None),
        P("mod", "dp"),
        P(("mod", "dp"), None),
        P("mod"),
        P("mod", "dp", None),
        P("mod", "dp", None),
        P("mod", "dp", None),
        P("mod", "dp", None),
        P("mod", "dp"),
        P(("mod", "dp"), None),
        P("mod"),
    )
    return jax.shard_map(
        on_device,
        mesh=mesh,
        in_specs=placed,
        out_specs=(
            P(),
            P(),
            P("mod", "dp", None),
            P("mod", "dp", None),
            P("mod", "dp", None),
            P("mod", "dp", None),
            P("mod", "dp"),
            P(("mod", "dp"), None),
            P("mod"),
            P("mod", "dp", None),
            P("mod", "dp", None),
            P("mod", "dp", None),
            P("mod", "dp", None),
            P("mod", "dp"),
            P(("mod", "dp"), None),
            P("mod"),
            P("mod", "dp", None),
            P("mod", "dp", None),
            P("mod", "dp", None),
            P("mod", "dp", None),
            P("mod", "dp"),
            P(("mod", "dp"), None),
            P("mod"),
        ),
        check_vma=False,
    )
```

```python
import functools
import math

import jax
import jax.numpy as jnp
import numpy as np
from jax import lax
from jax.experimental import pallas as pl
from jax.experimental.pallas import tpu as pltpu
from jax.sharding import PartitionSpec as P

HEAD_DIM = 64


NORM_EPS = 1e-05
CLIP_LIMIT = 0.05
BETA_ONE = 0.5
BETA_TWO = 0.5
ADAM_STEP = 10.0
ADAM_EPS = 1e-08
RATE_MATRIX = 0.03
RATE_GAIN = 0.3
DECAY_MATRIX = 0.1


def rms_scale(values, gain):
    return values * lax.rsqrt(jnp.mean(values * values, axis=-1, keepdims=True) + NORM_EPS) * gain


def rotary_tables(length):
    half = HEAD_DIM // 2
    inverse = 10000.0 ** (-np.arange(half, dtype=np.float32) / half)
    angle = np.arange(length, dtype=np.float32)[:, None] * inverse[None, :]
    cosine, sine = np.cos(angle), np.sin(angle)
    cosine = np.concatenate([cosine] * 4, axis=1).astype(np.float32)
    sine = np.concatenate([-sine, sine] * 2, axis=1).astype(np.float32)
    return jnp.asarray(cosine), jnp.asarray(sine)


def product(left, right):
    return jnp.dot(left, right, preferred_element_type=jnp.float32)


def left_product(left, right):
    return lax.dot_general(
        left, right, (((0,), (0,)), ((), ())), preferred_element_type=jnp.float32
    )


def right_product(left, right):
    return lax.dot_general(
        left, right, (((1,), (1,)), ((), ())), preferred_element_type=jnp.float32
    )


def adam_step(weight, grad, first, second, rate, decay):
    mean = BETA_ONE * first + (1.0 - BETA_ONE) * grad
    square = BETA_TWO * second + (1.0 - BETA_TWO) * grad * grad
    mean_hat = mean / (1.0 - BETA_ONE**ADAM_STEP)
    square_hat = square / (1.0 - BETA_TWO**ADAM_STEP)
    return (
        weight - rate * (mean_hat / (jnp.sqrt(square_hat) + ADAM_EPS) + decay * weight),
        mean,
        square,
    )


def one_hot(index, extent):
    return (index[..., None] == jnp.arange(extent, dtype=jnp.int32)).astype(jnp.bfloat16)


def exchange_kernel(groups, plan, *refs):
    count = len(plan)
    ins, outs = refs[:count], refs[count : 2 * count]
    sends, recvs = refs[2 * count : 3 * count], refs[3 * count : 4 * count]
    local = refs[4 * count]
    sizes = [math.prod(lax.axis_size(axis) for axis in axes) for axes in groups]
    places = []
    for axes in groups:
        place = lax.axis_index(axes[0])
        for axis in axes[1:]:
            place = place * lax.axis_size(axis) + lax.axis_index(axis)
        places.append(place)

    def device(group, index):
        axes = groups[group]
        if len(axes) == 1:
            return {axes[0]: index}
        inner = lax.axis_size(axes[1])
        return {axes[0]: index // inner, axes[1]: lax.rem(index, inner)}

    barrier = pltpu.get_barrier_semaphore()
    for group, size in enumerate(sizes):

        def greet(step, carry, group=group, size=size):
            peer = lax.rem(places[group] + step, size)
            pl.semaphore_signal(
                barrier,
                inc=1,
                device_id=device(group, peer),
                device_id_type=pl.DeviceIdType.MESH,
            )
            return carry

        lax.fori_loop(1, size, greet, 0)
    pl.semaphore_wait(barrier, sum(sizes) - len(sizes))

    def copy(item, step, arriving):
        group, shared = plan[item]
        size, place = sizes[group], places[group]
        peer = lax.rem(place + step, size)
        source = ins[item] if shared else ins[item].at[peer]
        slot = lax.rem(place + size - step, size) if arriving else place
        return pltpu.make_async_remote_copy(
            src_ref=source,
            dst_ref=outs[item].at[slot],
            send_sem=sends[item].at[step],
            recv_sem=recvs[item].at[step],
            device_id=device(group, peer),
            device_id_type=pl.DeviceIdType.MESH,
        )

    for item in range(count):

        def begin(step, carry, item=item):
            copy(item, step, False).start()
            return carry

        lax.fori_loop(1, sizes[plan[item][0]], begin, 0)
    own = []
    for item in range(count):
        group, shared = plan[item]
        source = ins[item] if shared else ins[item].at[places[group]]
        own.append(
            pltpu.make_async_copy(source, outs[item].at[places[group]], local.at[item])
        )
        own[-1].start()
    for item in range(count):
        own[item].wait()

        def finish(step, carry, item=item):
            copy(item, step, False).wait_send()
            copy(item, step, True).wait_recv()
            return carry

        lax.fori_loop(1, sizes[plan[item][0]], finish, 0)


def exchange(ident, *items):
    groups, plan, shapes, scratch = [], [], [], []
    for axes, array, shared in items:
        if axes not in groups:
            groups.append(axes)
        plan.append((groups.index(axes), shared))
        size = math.prod(lax.axis_size(axis) for axis in axes)
        shape = (size,) + array.shape if shared else array.shape
        shapes.append(jax.ShapeDtypeStruct(shape, array.dtype))
        scratch.append(pltpu.SemaphoreType.DMA((size,)))
    result = pl.pallas_call(
        functools.partial(exchange_kernel, groups, plan),
        out_shape=shapes,
        in_specs=[pl.BlockSpec(memory_space=pltpu.VMEM)] * len(items),
        out_specs=[pl.BlockSpec(memory_space=pltpu.VMEM)] * len(items),
        scratch_shapes=scratch + scratch + [pltpu.SemaphoreType.DMA((len(items),))],
        compiler_params=pltpu.CompilerParams(collective_id=ident, has_side_effects=True),
        name="exchange_%d" % ident,
    )(*(array for _, array, _ in items))
    return result[0] if len(items) == 1 else result


GATHER_ORDERS = ((0, 1, 2), (2, 0, 1), (1, 2, 0))


def chip_grid():
    group_mod, group_dp = lax.axis_size("mod"), lax.axis_size("dp")
    deep = math.gcd(group_mod, 4)
    return deep, group_mod // deep, group_dp // 2


def row_pieces(rows):
    part = rows // 64 * 16
    return (0, part), (part, rows - 2 * part), (rows - part, part)


def chip_place(sizes):
    mod, dp = lax.axis_index("mod"), lax.axis_index("dp")
    return [mod // sizes[1], lax.rem(mod, sizes[1]), dp // 2], lax.rem(dp, 2)


def chip_device(sizes, at, core):
    return {"mod": at[0] * sizes[1] + at[1], "dp": at[2] * 2 + core}


def shifted(sizes, at, axis, step):
    at = list(at)
    at[axis] = lax.rem(at[axis] + step, sizes[axis])
    return at


def greet_lines(sizes, at, core):
    barrier = pltpu.get_barrier_semaphore()
    targets = [chip_device(sizes, at, 1 - core)]
    for axis in range(3):
        for step in range(1, sizes[axis]):
            targets.append(chip_device(sizes, shifted(sizes, at, axis, step), core))
    for target in targets:
        pl.semaphore_signal(
            barrier, inc=1, device_id=target, device_id_type=pl.DeviceIdType.MESH
        )
    pl.semaphore_wait(barrier, len(targets))


def line_copies(sizes):
    return sum(len(GATHER_ORDERS) * (size - 1) for size in sizes)


def gather_kernel(sizes, rows, in_ref, out_ref, send, recv, pair_send, pair_recv, local):
    at, core = chip_place(sizes)
    greet_lines(sizes, at, core)
    pieces = row_pieces(rows)
    keys = {}
    for piece, order in enumerate(GATHER_ORDERS):
        for stage, axis in enumerate(order):
            for step in range(1, sizes[axis]):
                keys[piece, stage, step] = len(keys)

    def region(at, done, core, piece):
        start, count = pieces[piece]
        index = tuple(slice(None) if axis in done else at[axis] for axis in range(3))
        return out_ref.at[index + (core, pl.ds(start, count))]

    def remote(source, target, sems, index, at, core):
        return pltpu.make_async_remote_copy(
            src_ref=source,
            dst_ref=target,
            send_sem=sems[0].at[index],
            recv_sem=sems[1].at[index],
            device_id=chip_device(sizes, at, core),
            device_id_type=pl.DeviceIdType.MESH,
        )

    def line(piece, stage, step, arriving):
        order = GATHER_ORDERS[piece]
        axis, done = order[stage], order[:stage]
        peer = shifted(sizes, at, axis, step)
        origin = shifted(sizes, at, axis, sizes[axis] - step)
        target = region(origin if arriving else at, done, core, piece)
        source = region(at, done, core, piece)
        if stage == 0:
            source = in_ref.at[pl.ds(*pieces[piece])]
        return remote(source, target, (send, recv), keys[piece, stage, step], peer, core)

    def pair(piece, stage, step, arriving):
        order = GATHER_ORDERS[piece]
        axis, done = order[stage], order[:stage]
        origin = shifted(sizes, at, axis, sizes[axis] - step)
        source = region(origin, done, core, piece)
        target = region(origin, done, 1 - core if arriving else core, piece)
        index = keys[piece, stage, step]
        return remote(source, target, (pair_send, pair_recv), index, at, 1 - core)

    def pair_own(arriving):
        target = out_ref.at[at[0], at[1], at[2], 1 - core if arriving else core]
        return remote(in_ref, target, (pair_send, pair_recv), len(keys), at, 1 - core)

    own = pltpu.make_async_copy(in_ref, out_ref.at[at[0], at[1], at[2], core], local)
    own.start()
    pair_own(False).start()
    for stage in range(4):
        for piece, order in enumerate(GATHER_ORDERS):
            if stage > 0:
                for step in range(1, sizes[order[stage - 1]]):
                    line(piece, stage - 1, step, True).wait_recv()
                if stage == 1 and piece == 0:
                    own.wait()
            if stage < 3:
                for step in range(1, sizes[order[stage]]):
                    line(piece, stage, step, False).start()
            if stage > 0:
                for step in range(1, sizes[order[stage - 1]]):
                    pair(piece, stage - 1, step, False).start()
    for piece, stage, step in keys:
        line(piece, stage, step, False).wait_send()
        pair(piece, stage, step, False).wait_send()
        pair(piece, stage, step, True).wait_recv()
    pair_own(False).wait_send()
    pair_own(True).wait_recv()


def gather_rows(ident, rows):
    sizes = chip_grid()
    count, width = rows.shape
    copies = line_copies(sizes)
    dma = pltpu.SemaphoreType.DMA
    gathered = pl.pallas_call(
        functools.partial(gather_kernel, sizes, count),
        out_shape=jax.ShapeDtypeStruct(sizes + (2, count, width), rows.dtype),
        in_specs=[pl.BlockSpec(memory_space=pltpu.VMEM)],
        out_specs=pl.BlockSpec(memory_space=pltpu.VMEM),
        scratch_shapes=[dma((copies,)), dma((copies,)), dma((copies + 1,)), dma((copies + 1,)), dma],
        compiler_params=pltpu.CompilerParams(collective_id=ident, has_side_effects=True),
        name="gather_rows",
    )(rows)
    return gathered.reshape(-1, width)


def scatter_kernel(sizes, rows, in_ref, out_ref, acc, arrived, *rest):
    slots, (send, recv, pair_send, pair_recv, local) = rest[:-5], rest[-5:]
    at, core = chip_place(sizes)
    greet_lines(sizes, at, core)
    pieces = row_pieces(rows)
    orders = [order[::-1] for order in GATHER_ORDERS]
    keys = {}
    for piece, order in enumerate(orders):
        for stage, axis in enumerate(order):
            for step in range(1, sizes[axis]):
                keys[piece, stage, step] = len(keys)

    def line(piece, stage, step):
        order = orders[piece]
        axis, done = order[stage], order[:stage]
        peer = shifted(sizes, at, axis, step)
        index = tuple(
            peer[a] if a == axis else at[a] if a in done else slice(None) for a in range(3)
        )
        key = keys[piece, stage, step]
        return pltpu.make_async_remote_copy(
            src_ref=acc.at[index + (pl.ds(*pieces[piece]),)],
            dst_ref=slots[3 * piece + stage].at[step - 1],
            send_sem=send.at[key],
            recv_sem=recv.at[key],
            device_id=chip_device(sizes, peer, core),
            device_id_type=pl.DeviceIdType.MESH,
        )

    loads, pairs = [], []
    for piece in range(3):
        part = pl.ds(*pieces[piece])
        pairs.append(
            pltpu.make_async_remote_copy(
                src_ref=in_ref.at[:, :, :, 1 - core, part],
                dst_ref=arrived.at[:, :, :, part],
                send_sem=pair_send.at[piece],
                recv_sem=pair_recv.at[piece],
                device_id=chip_device(sizes, at, 1 - core),
                device_id_type=pl.DeviceIdType.MESH,
            )
        )
        pairs[-1].start()
        loads.append(
            pltpu.make_async_copy(
                in_ref.at[:, :, :, core, part], acc.at[:, :, :, part], local.at[piece]
            )
        )
        loads[-1].start()

    def add(piece, stage):
        order = orders[piece]
        done = order[:stage]
        left = [axis for axis in range(3) if axis not in done]
        part = pl.ds(*pieces[piece])

        def one(index, carry):
            where, inner = list(at), []
            for axis in reversed(left):
                where[axis] = lax.rem(index, sizes[axis])
                index = index // sizes[axis]
                inner.insert(0, where[axis])
            spot = tuple(where) + (part,)
            total = acc[spot].astype(jnp.float32)
            if stage == 0:
                total = total + arrived[spot].astype(jnp.float32)
            else:
                taken = slots[3 * piece + stage - 1]
                for step in range(taken.shape[0]):
                    total = total + taken[(step,) + tuple(inner)].astype(jnp.float32)
            if stage == 3:
                out_ref[part] = total
            else:
                acc[spot] = total.astype(acc.dtype)
            return carry

        lax.fori_loop(0, math.prod(sizes[axis] for axis in left), one, 0)

    for stage in range(4):
        for piece, order in enumerate(orders):
            if stage == 0:
                loads[piece].wait()
                pairs[piece].wait_recv()
            else:
                for step in range(1, sizes[order[stage - 1]]):
                    line(piece, stage - 1, step).wait_recv()
            add(piece, stage)
            if stage < 3:
                for step in range(1, sizes[order[stage]]):
                    line(piece, stage, step).start()
    for piece in range(3):
        pairs[piece].wait_send()
    for piece, stage, step in keys:
        line(piece, stage, step).wait_send()


def scatter_rows(ident, parts):
    sizes = chip_grid()
    width = parts.shape[1]
    count = parts.shape[0] // (2 * math.prod(sizes))
    copies = line_copies(sizes)
    dma = pltpu.SemaphoreType.DMA
    slots = []
    for piece, order in enumerate(GATHER_ORDERS):
        order = order[::-1]
        for stage, axis in enumerate(order):
            left = tuple(sizes[a] for a in range(3) if a not in order[: stage + 1])
            shape = (sizes[axis] - 1,) + left + (row_pieces(count)[piece][1], width)
            slots.append(pltpu.VMEM(shape, parts.dtype))
    return pl.pallas_call(
        functools.partial(scatter_kernel, sizes, count),
        out_shape=jax.ShapeDtypeStruct((count, width), jnp.float32),
        in_specs=[pl.BlockSpec(memory_space=pl.ANY)],
        out_specs=pl.BlockSpec(memory_space=pltpu.VMEM),
        scratch_shapes=[
            pltpu.VMEM(sizes + (count, width), parts.dtype),
            pltpu.VMEM(sizes + (count, width), parts.dtype),
            *slots,
            dma((copies,)),
            dma((copies,)),
            dma((3,)),
            dma((3,)),
            dma((3,)),
        ],
        compiler_params=pltpu.CompilerParams(collective_id=ident, has_side_effects=True),
        name="scatter_rows",
    )(parts.reshape(sizes + (2, count, width)))


def totals_kernel(in_ref, out_ref, arrived, mine, send, recv, back_send, back_recv):
    group_mod, group_dp = lax.axis_size("mod"), lax.axis_size("dp")
    size = group_mod * group_dp
    place = lax.axis_index("mod") * group_dp + lax.axis_index("dp")

    def device(index):
        return {"mod": index // group_dp, "dp": lax.rem(index, group_dp)}

    barrier = pltpu.get_barrier_semaphore()

    def greet(step, carry):
        pl.semaphore_signal(
            barrier,
            inc=1,
            device_id=device(lax.rem(place + step, size)),
            device_id_type=pl.DeviceIdType.MESH,
        )
        return carry

    def ahead(step, slot):
        peer = lax.rem(place + step, size)
        return pltpu.make_async_remote_copy(
            src_ref=in_ref.at[peer],
            dst_ref=arrived.at[slot],
            send_sem=send.at[step],
            recv_sem=recv.at[step],
            device_id=device(peer),
            device_id_type=pl.DeviceIdType.MESH,
        )

    def back(step, slot):
        return pltpu.make_async_remote_copy(
            src_ref=mine,
            dst_ref=out_ref.at[slot],
            send_sem=back_send.at[step],
            recv_sem=back_recv.at[step],
            device_id=device(lax.rem(place + step, size)),
            device_id_type=pl.DeviceIdType.MESH,
        )

    def begin(copy):
        def one(step, carry):
            copy(step, place).start()
            return carry

        lax.fori_loop(1, size, one, 0)

    def finish(copy):
        def one(step, carry):
            copy(step, place).wait_send()
            copy(step, lax.rem(place + size - step, size)).wait_recv()
            return carry

        lax.fori_loop(1, size, one, 0)

    lax.fori_loop(1, size, greet, 0)
    pl.semaphore_wait(barrier, size - 1)
    begin(ahead)
    arrived[place] = in_ref[place]
    finish(ahead)
    tops = arrived[:, 0:1]
    top = jnp.max(tops, axis=0)
    total = jnp.sum(arrived[:, 1:2] * jnp.exp(tops - top[None]), axis=0)
    hit = jnp.sum(arrived[:, 2:3], axis=0)
    line = lax.broadcasted_iota(jnp.int32, mine.shape, 0)
    mine[...] = jnp.where(line == 0, top + jnp.log(total), jnp.where(line == 1, hit, 0.0))
    out_ref[place] = mine[...]
    begin(back)
    finish(back)


def totals_call(ident, stats):
    dma = pltpu.SemaphoreType.DMA((stats.shape[0],))
    return pl.pallas_call(
        totals_kernel,
        out_shape=jax.ShapeDtypeStruct(stats.shape, stats.dtype),
        in_specs=[pl.BlockSpec(memory_space=pltpu.VMEM)],
        out_specs=pl.BlockSpec(memory_space=pltpu.VMEM),
        scratch_shapes=[
            pltpu.VMEM(stats.shape, stats.dtype),
            pltpu.VMEM(stats.shape[1:], stats.dtype),
            dma,
            dma,
            dma,
            dma,
        ],
        compiler_params=pltpu.CompilerParams(collective_id=ident, has_side_effects=True),
        name="totals",
    )(stats)


def side_by_side(blocks):
    count, rows, columns = blocks.shape
    if columns % 128:
        return jnp.concatenate(list(blocks.astype(jnp.float32)), axis=1)

    def place(in_ref, out_ref):
        out_ref[...] = in_ref[0].astype(jnp.float32)

    return pl.pallas_call(
        place,
        grid=(count,),
        out_shape=jax.ShapeDtypeStruct((rows, count * columns), jnp.float32),
        in_specs=[pl.BlockSpec((1, rows, columns), lambda i: (i, 0, 0))],
        out_specs=pl.BlockSpec((rows, columns), lambda i: (0, i)),
        name="side_by_side",
    )(blocks)


HEAD_ROWS = 256


def scores_kernel(rows_ref, table_ref, wanted_ref, out_ref, logits_ref):
    logits = right_product(table_ref[...], rows_ref[...])
    logits_ref[...] = logits
    hits = lax.broadcasted_iota(jnp.int32, logits.shape, 0) == wanted_ref[...]
    top = jnp.max(logits, axis=0, keepdims=True)
    total = jnp.sum(jnp.exp(logits - top), axis=0, keepdims=True)
    hit = jnp.sum(jnp.where(hits, logits, 0.0), axis=0, keepdims=True)
    count, lines, part = out_ref.shape
    line = lax.broadcasted_iota(jnp.int32, (lines, part), 0)
    for block in range(count):
        at = slice(block * part, (block + 1) * part)
        out_ref[block] = jnp.where(
            line == 0, top[:, at], jnp.where(line == 1, total[:, at], hit[:, at])
        )


def scores_call(rows, table, wanted, part):
    step = math.gcd(HEAD_ROWS, rows.shape[0])
    return pl.pallas_call(
        scores_kernel,
        grid=(rows.shape[0] // step,),
        out_shape=[
            jax.ShapeDtypeStruct((rows.shape[0] // part, 8, part), jnp.float32),
            jax.ShapeDtypeStruct((table.shape[0], rows.shape[0]), jnp.float32),
        ],
        in_specs=[
            pl.BlockSpec((step, rows.shape[1]), lambda i: (i, 0)),
            pl.BlockSpec(table.shape, lambda i: (0, 0)),
            pl.BlockSpec((1, step), lambda i: (0, i)),
        ],
        out_specs=[
            pl.BlockSpec((step // part, 8, part), lambda i: (i, 0, 0)),
            pl.BlockSpec((table.shape[0], step), lambda i: (0, i)),
        ],
        name="scores",
    )(rows, table, wanted[None])


def norm_kernel(group_mod, group_dp, final_lines, in_ref, out_ref, gathered, send, recv, local):
    exchange_kernel([("mod", "dp")], [(0, True)], in_ref, gathered, send, recv, local)
    final = gathered[0]
    for mod in range(1, group_mod):
        final = final + gathered[mod * group_dp]
    line = lax.broadcasted_iota(jnp.int32, final.shape, 0)
    final = jnp.where(line < final_lines, final, 0.0)
    squares = jnp.sum(jnp.sum(final * final, axis=1, keepdims=True), axis=0, keepdims=True)
    total = jnp.sum(gathered[...], axis=0) + squares
    out_ref[...] = jnp.where(line < final_lines, final, total)


def norm_call(ident, last, final_lines):
    group_mod, group_dp = lax.axis_size("mod"), lax.axis_size("dp")
    size = group_mod * group_dp
    dma = pltpu.SemaphoreType.DMA
    return pl.pallas_call(
        functools.partial(norm_kernel, group_mod, group_dp, final_lines),
        out_shape=jax.ShapeDtypeStruct(last.shape, last.dtype),
        in_specs=[pl.BlockSpec(memory_space=pltpu.VMEM)],
        out_specs=pl.BlockSpec(memory_space=pltpu.VMEM),
        scratch_shapes=[
            pltpu.VMEM((size,) + last.shape, last.dtype),
            dma((size,)),
            dma((size,)),
            dma((1,)),
        ],
        compiler_params=pltpu.CompilerParams(collective_id=ident, has_side_effects=True),
        name="norm",
    )(last)


GROUP_SEQS = 4


def wide_table(table_ref, tokens, width):
    table = table_ref[...]
    table = jnp.concatenate([table] * (tokens // table.shape[0]), axis=0)
    return jnp.concatenate([table] * (width // table.shape[1]), axis=1)


def turned(values, cosine, sine):
    width = values.shape[-1]
    half = HEAD_DIM // 2
    lane = lax.broadcasted_iota(jnp.int32, values.shape, 1)
    other = jnp.where(
        lane % HEAD_DIM < half,
        pltpu.roll(values, width - half, 1),
        pltpu.roll(values, half, 1),
    )
    return values * cosine + other * sine


def head_spread(values, heads):
    rows, width = values.shape
    lane = lax.broadcasted_iota(jnp.int32, (heads, rows, width), 2)
    head = lax.broadcasted_iota(jnp.int32, (heads, rows, width), 0)
    return jnp.where(lane // HEAD_DIM == head, values[None], jnp.zeros((), values.dtype))


def head_fold(values, heads):
    rows, width = values.shape
    values = values.reshape(heads, rows // heads, width)
    lane = lax.broadcasted_iota(jnp.int32, values.shape, 2)
    head = lax.broadcasted_iota(jnp.int32, values.shape, 0)
    return jnp.sum(jnp.where(lane // HEAD_DIM == head, values, 0.0), axis=0)


def attention_parts(length, spots_ref, mixed_ref, cosine_ref, sine_ref):
    tokens, width = mixed_ref.shape[0], mixed_ref.shape[1] // 3
    heads = width // HEAD_DIM
    cosine = wide_table(cosine_ref, tokens, width)
    sine = wide_table(sine_ref, tokens, width)
    spot = spots_ref[...]
    key = lax.broadcasted_iota(jnp.int32, (spot.shape[0], tokens), 1)
    chosen = key == spot
    seen = (key <= spot) & (key >= spot - spot % length)
    queries = turned(mixed_ref[:, :width], cosine, sine).astype(jnp.bfloat16)
    queries = product(chosen.astype(jnp.bfloat16), queries)
    queries = head_spread(queries, heads).reshape(-1, width).astype(jnp.bfloat16)
    keys_in = turned(mixed_ref[:, width : 2 * width], cosine, sine).astype(jnp.bfloat16)
    values = mixed_ref[:, 2 * width :].astype(jnp.bfloat16)
    raw = right_product(queries, keys_in).reshape(heads, -1, tokens)
    scores = jnp.where(seen[None], raw * HEAD_DIM ** (-0.5), -1e30).reshape(-1, tokens)
    top = jnp.max(scores, axis=1, keepdims=True)
    terms = jnp.exp(scores - top)
    chances = terms / jnp.sum(terms, axis=1, keepdims=True)
    return chosen, queries, keys_in, values, chances, cosine, sine


def attention_kernel(
    length, spots_ref, mixed_ref, inputs_ref, cosine_ref, sine_ref, heads_ref, picked_ref
):
    heads = inputs_ref.shape[1] // HEAD_DIM
    chosen, _, _, values, chances, _, _ = attention_parts(
        length, spots_ref, mixed_ref, cosine_ref, sine_ref
    )
    spread = product(chances.astype(jnp.bfloat16), values)
    heads_ref[...] = head_fold(spread, heads).astype(jnp.bfloat16)
    picked_ref[...] = product(chosen.astype(jnp.bfloat16), inputs_ref[...])


def attention_back_kernel(
    length, spots_ref, mixed_ref, grad_ref, cosine_ref, sine_ref, out_ref
):
    width = grad_ref.shape[1]
    heads = width // HEAD_DIM
    chosen, queries, keys_in, values, chances, cosine, sine = attention_parts(
        length, spots_ref, mixed_ref, cosine_ref, sine_ref
    )
    grad_heads = head_spread(grad_ref[...].astype(jnp.float32), heads)
    grad_heads = grad_heads.reshape(-1, width).astype(jnp.bfloat16)
    grad_values = left_product(chances.astype(jnp.bfloat16), grad_heads)
    grad_chances = right_product(grad_heads, values)
    delta = jnp.sum(chances * grad_chances, axis=1, keepdims=True)
    grad_raw = (chances * (grad_chances - delta) * HEAD_DIM ** (-0.5)).astype(jnp.bfloat16)
    grad_queries = head_fold(product(grad_raw, keys_in), heads)
    grad_queries = lax.dot_general(
        chosen.astype(jnp.float32),
        grad_queries,
        (((0,), (0,)), ((), ())),
        precision=lax.Precision.HIGHEST,
        preferred_element_type=jnp.float32,
    )
    grad_keys = left_product(grad_raw, queries)
    out_ref[:, :width] = turned(grad_queries, cosine, -sine).astype(jnp.bfloat16)
    out_ref[:, width : 2 * width] = turned(grad_keys, cosine, -sine).astype(jnp.bfloat16)
    out_ref[:, 2 * width :] = grad_values.astype(jnp.bfloat16)


def attention_call(body, length, operands, tables, outs, name, microseconds):
    sequences = operands[1].shape[0] // length
    steps = sequences // math.gcd(GROUP_SEQS, sequences)

    def block(array):
        return pl.BlockSpec((array.shape[0] // steps, array.shape[1]), lambda i: (i, 0))

    fixed = [pl.BlockSpec(table.shape, lambda i: (0, 0)) for table in tables]
    return pl.pallas_call(
        functools.partial(body, length),
        grid=(steps,),
        out_shape=outs,
        in_specs=[block(array) for array in operands] + fixed,
        out_specs=[block(array) for array in outs],
        cost_estimate=pl.CostEstimate(
            flops=0, bytes_accessed=microseconds * 3_000_000, transcendentals=0
        ),
        name=name,
    )(*operands, *tables)


def on_device(
    token_ids,
    targets,
    positions,
    loss_mask,
    paths,
    attend,
    output,
    widen,
    narrow,
    gains,
    table,
    final_gain,
    first_attend,
    first_output,
    first_widen,
    first_narrow,
    first_gains,
    first_table,
    first_final,
    second_attend,
    second_output,
    second_widen,
    second_narrow,
    second_gains,
    second_table,
    second_final,
):
    group_dp = lax.axis_size("dp")
    group_mod = lax.axis_size("mod")
    dp_place = lax.axis_index("dp")
    mod_place = lax.axis_index("mod")
    everyone = ("mod", "dp")
    place = mod_place * group_dp + dp_place
    sources = group_mod * group_dp
    micro, per_mod, length = token_ids.shape
    spots_seq = positions.shape[2]
    seq_dev = per_mod // group_dp
    shard_rows, width = table.shape
    heads = width // HEAD_DIM
    slots = micro * sources
    slots_local = slots // group_dp
    low = jnp.bfloat16

    mixing = lax.all_gather(
        jnp.concatenate([attend[0], output[0]], axis=1).astype(low), "dp", axis=0, tiled=True
    )
    attend_low, output_low = mixing[:, : 3 * width], mixing[:, 3 * width :]
    hidden = narrow.shape[1]
    widen_low = jnp.stack(
        [widen[0, :, i * hidden : (i + 1) * hidden].astype(low) for i in range(group_dp)]
    )
    widen_low = lax.all_to_all(widen_low, "dp", split_axis=0, concat_axis=0, tiled=True)
    widen_low = widen_low.reshape(width, hidden)
    narrow_low = narrow[0].astype(low)
    table_low = table.astype(low)

    fields = jnp.concatenate(
        [token_ids, positions, targets, loss_mask, paths[..., None]], axis=-1
    )
    fields, gain_parts, final_parts = exchange(
        0,
        (("mod",), fields.reshape(micro * per_mod, -1), True),
        (("dp",), jnp.broadcast_to(gains.astype(low), (16, gains.shape[1])), True),
        (("mod",), jnp.broadcast_to(final_gain.astype(low)[None], (16, final_gain.shape[0])), True),
    )
    own_gains = gain_parts[:, 0].reshape(-1).astype(jnp.float32)
    gain_one, gain_two = own_gains[:width], own_gains[width:]
    gain_final = final_parts[:, 0].reshape(-1).astype(jnp.float32)
    fields = fields.reshape(group_mod, micro, per_mod, -1).transpose(1, 0, 2, 3)
    fields = fields.reshape(slots, seq_dev, -1)
    own = lax.dynamic_slice_in_dim(fields, dp_place * slots_local, slots_local)
    own_match = own[..., -1] == mod_place
    own = jnp.sum(jnp.where(own_match[..., None], own[..., : length + spots_seq], 0), axis=1)
    own_tokens = own[:, :length].reshape(-1)
    spots = own[:, length:]
    held = jnp.repeat(jnp.any(own_match, axis=1), length)
    match = fields[None, ..., -1] == jnp.arange(group_mod, dtype=jnp.int32)[:, None, None]
    scoring = jnp.sum(
        jnp.where(match[..., None], fields[None, ..., length + spots_seq : -1], 0), axis=2
    )
    wanted = scoring[..., :spots_seq].reshape(-1)
    counted = scoring[..., spots_seq:].reshape(-1).astype(jnp.float32)
    count_total = jnp.sum(counted)

    shard = own_tokens // shard_rows
    row = own_tokens % shard_rows
    key = jnp.where(held, own_tokens, -1)
    order = jnp.arange(key.shape[0], dtype=jnp.int32)
    repeated = jnp.any((key[:, None] == key[None, :]) & (order[None, :] < order[:, None]), axis=1)
    leading = held & ~repeated
    rank = jnp.sum(
        (
            leading[None, :] & (shard[None, :] == shard[:, None]) & (key[None, :] < key[:, None])
        ).astype(jnp.int32),
        axis=1,
    )
    expected = -(-slots_local * length // sources)
    cap = -(-3 * expected // 16) * 8
    cap = min(max(cap, 16), -(-shard_rows // 8) * 8, 112)
    own_rounds = jnp.max(jnp.where(leading, rank // cap, 0)) + 1

    def ask(turn):
        slot = rank - turn * cap
        inside = held & (slot >= 0) & (slot < cap)
        slot = jnp.where(inside, shard * cap + slot, -1)
        asked = jnp.sum(
            jnp.where(
                leading[None, :]
                & (slot[None, :] == jnp.arange(sources * cap, dtype=jnp.int32)[:, None]),
                row[None, :] + 1,
                0,
            ),
            axis=1,
        ).reshape(sources, cap)
        return slot, asked

    slot, asked = ask(0)
    message = jnp.concatenate(
        [asked, jnp.broadcast_to(own_rounds, (sources, 128 - cap))], axis=1
    )
    message = exchange(
        1, (everyone, jnp.broadcast_to(message[:, None], (sources, 8, 128)), False)
    )
    rounds = jnp.max(message[:, 0, cap])
    spread = one_hot(slot, sources * cap)
    pick = one_hot(message[:, 0, :cap].reshape(-1) - 1, shard_rows)

    def other_plan(turn):
        slot, asked = ask(turn)
        asked = lax.all_to_all(asked, everyone, split_axis=0, concat_axis=0, tiled=True)
        return one_hot(slot, sources * cap), one_hot(asked.reshape(-1) - 1, shard_rows)

    def other_rows(state):
        turn, rows = state
        spread, pick = other_plan(turn)
        sent = product(pick, table_low).astype(low).reshape(sources, cap, width)
        got = lax.all_to_all(sent, everyone, split_axis=0, concat_axis=0, tiled=True)
        return turn + 1, rows + product(spread, got.reshape(-1, width)).astype(low)

    sent = product(pick, table_low).astype(low).reshape(sources, cap, width)
    got = exchange(2, (everyone, sent, False))
    inputs = product(spread, got.reshape(-1, width)).astype(low)
    inputs = lax.while_loop(
        lambda state: state[0] < rounds, other_rows, (jnp.int32(1), inputs)
    )[1]

    group = math.gcd(GROUP_SEQS, slots_local)
    tables = rotary_tables(length)
    flat_spots = spots + (jnp.arange(slots_local, dtype=jnp.int32) % group)[:, None] * length
    flat_spots = flat_spots.reshape(-1, 1)
    inputs_wide = inputs.astype(jnp.float32)
    normed_one = rms_scale(inputs_wide, gain_one).astype(low)
    mixed = product(normed_one, attend_low)
    picked_rows = slots_local * spots_seq
    heads_out, picked_inputs = attention_call(
        attention_kernel,
        length,
        (flat_spots, mixed, inputs),
        tables,
        [
            jax.ShapeDtypeStruct((picked_rows, width), low),
            jax.ShapeDtypeStruct((picked_rows, width), jnp.float32),
        ],
        "attention",
        7,
    )
    middle = picked_inputs + product(heads_out, output_low)

    def sum_parts(ident, parts):
        parts = parts.astype(low).reshape(group_dp, picked_rows, width)
        return jnp.sum(exchange(ident, (("dp",), parts, False)).astype(jnp.float32), axis=0)

    normed_two = rms_scale(middle, gain_two).astype(low)
    normed_all = exchange(3, (("dp",), normed_two, True)).reshape(-1, width)
    upper = product(normed_all, widen_low)
    gelu = lambda value: jax.nn.gelu(value, approximate=True)
    activated = gelu(upper).astype(low)
    lifted = sum_parts(4, product(activated, narrow_low))
    returned = (middle + lifted).astype(low).astype(jnp.float32)

    final, final_back = jax.vjp(rms_scale, returned, gain_final)
    scored = gather_rows(12, final.astype(low))
    target_row = wanted - place * shard_rows
    stats, logits = scores_call(scored, table_low, target_row, picked_rows)
    totals = totals_call(5, stats)
    log_total = totals[:, 0].reshape(-1)
    loss_total = jnp.sum(counted * (log_total - totals[:, 1].reshape(-1)))
    hits = target_row[None, :] == jnp.arange(shard_rows, dtype=jnp.int32)[:, None]
    grad_logits = (
        counted[None] * (jnp.exp(logits - log_total[None]) - hits.astype(jnp.float32))
    ).astype(low)
    grad_picked = scatter_rows(13, left_product(grad_logits, table_low).astype(low))

    grad_returned, grad_final = final_back(grad_picked)
    incoming = grad_returned.astype(low)
    incoming_all = exchange(7, (("dp",), incoming, True)).reshape(-1, width)
    grad_narrow = left_product(activated, incoming_all)
    grad_act = right_product(incoming_all, narrow_low)
    grad_upper = jax.vjp(gelu, upper)[1](grad_act)[0].astype(low)
    grad_widen = left_product(normed_all, grad_upper).astype(low)
    grad_widen = lax.all_to_all(
        grad_widen.reshape(group_dp, -1, hidden), "dp", split_axis=0, concat_axis=0, tiled=True
    )
    grad_normed_two = sum_parts(8, right_product(grad_upper, widen_low))
    grad_middle, grad_gain_two = jax.vjp(rms_scale, middle, gain_two)[1](grad_normed_two)
    grad_middle = grad_middle + incoming.astype(jnp.float32)

    branch_grad = grad_middle.astype(low)
    grad_output = lax.psum_scatter(
        left_product(heads_out, branch_grad).astype(low), "dp", scatter_dimension=0, tiled=True
    ).astype(jnp.float32)
    grad_heads = right_product(branch_grad, output_low).astype(low)
    (grad_mixed,) = attention_call(
        attention_back_kernel,
        length,
        (flat_spots, mixed, grad_heads),
        tables,
        [jax.ShapeDtypeStruct(mixed.shape, low)],
        "attention_back",
        12,
    )
    grad_widen, grad_mixed = lax.optimization_barrier((grad_widen, grad_mixed))
    grad_attend = left_product(normed_one, grad_mixed)
    grad_normed = right_product(grad_mixed, attend_low)
    grad_inputs, grad_gain_one = jax.vjp(rms_scale, inputs_wide, gain_one)[1](grad_normed)
    here = spots[:, :, None] == jnp.arange(length, dtype=jnp.int32)
    grad_skip = jnp.sum(
        jnp.where(
            here[..., None], grad_middle.reshape(slots_local, spots_seq, 1, width), 0.0
        ),
        axis=1,
    ).reshape(-1, width)
    leaving = (grad_skip + grad_inputs).astype(low)

    grad_attend = lax.psum_scatter(
        grad_attend.astype(low), "dp", scatter_dimension=0, tiled=True
    ).astype(jnp.float32)

    def other_grads(state):
        turn, total = state
        spread, pick = other_plan(turn)
        sent = left_product(spread, leaving).astype(low).reshape(sources, cap, width)
        got = lax.all_to_all(sent, everyone, split_axis=0, concat_axis=0, tiled=True)
        return turn + 1, total + left_product(pick, got.reshape(-1, width))

    given = left_product(spread, leaving).astype(low).reshape(sources, cap, width)
    gain_grads = jnp.concatenate([grad_gain_one, grad_gain_two, grad_final])
    gain_grads = jnp.pad(gain_grads.reshape(-1, 128), ((0, -gain_grads.shape[0] // 128 % 8), (0, 0)))
    given, gain_grads = exchange(
        9, (everyone, given, False), (("dp",), gain_grads, True)
    )
    given, scored = lax.optimization_barrier((given, scored))
    table_grad = product(grad_logits, scored)
    table_grad = table_grad + left_product(pick, given.reshape(-1, width))
    table_grad = lax.while_loop(
        lambda state: state[0] < rounds, other_grads, (jnp.int32(1), table_grad)
    )[1]
    gain_grads = jnp.sum(gain_grads, axis=0).reshape(-1)
    own_gain_grads = gain_grads[: 2 * width]
    final_rows = gain_grads[2 * width : 3 * width].reshape(-1, 128)
    gain_part = gains.shape[1]
    grad_gains = lax.dynamic_slice_in_dim(own_gain_grads, dp_place * gain_part, gain_part)
    widen_squares = jnp.sum(jnp.square(grad_widen.astype(jnp.float32)))
    grad_widen = side_by_side(grad_widen)
    matrix_grads = (grad_attend[None], grad_output[None], grad_widen[None], grad_narrow[None])
    squares = sum((jnp.sum(g * g) for g in (grad_attend, grad_output, grad_narrow, table_grad)))
    squares = squares + widen_squares
    squares = squares + jnp.sum(grad_gains * grad_gains)
    last = jnp.concatenate(
        [final_rows, jnp.broadcast_to(squares, (16 - final_rows.shape[0] % 8 - 8, 128))], axis=0
    )
    final_count = final_rows.shape[0]
    last = norm_call(11, last, final_count)
    grad_final = last[:final_count].reshape(-1)
    squares = last[final_count, 0]
    final_part = final_gain.shape[0]
    grad_final = lax.dynamic_slice_in_dim(grad_final, mod_place * final_part, final_part)
    gradient_norm = jnp.sqrt(squares) / count_total
    factor = CLIP_LIMIT / jnp.maximum(gradient_norm, CLIP_LIMIT) / count_total
    params = (attend, output, widen, narrow, gains, table, final_gain)
    grads = matrix_grads + (grad_gains[None], table_grad, grad_final)
    firsts = (
        first_attend,
        first_output,
        first_widen,
        first_narrow,
        first_gains,
        first_table,
        first_final,
    )
    seconds = (
        second_attend,
        second_output,
        second_widen,
        second_narrow,
        second_gains,
        second_table,
        second_final,
    )
    rates = (RATE_MATRIX, RATE_MATRIX, RATE_MATRIX, RATE_MATRIX, RATE_GAIN, RATE_MATRIX, RATE_GAIN)
    decays = (DECAY_MATRIX, DECAY_MATRIX, DECAY_MATRIX, DECAY_MATRIX, 0.0, DECAY_MATRIX, 0.0)
    updated = [
        adam_step(w, g * factor, f, s, r, c)
        for w, g, f, s, r, c in zip(params, grads, firsts, seconds, rates, decays)
    ]
    return (
        loss_total / count_total,
        gradient_norm,
        *(entry[0] for entry in updated),
        *(entry[1] for entry in updated),
        *(entry[2] for entry in updated),
    )


def solution(mesh):
    placed = (
        P(None, "mod", None),
        P(None, "mod", None),
        P(None, "mod", None),
        P(None, "mod", None),
        P(None, "mod"),
        P("mod", "dp", None),
        P("mod", "dp", None),
        P("mod", "dp", None),
        P("mod", "dp", None),
        P("mod", "dp"),
        P(("mod", "dp"), None),
        P("mod"),
        P("mod", "dp", None),
        P("mod", "dp", None),
        P("mod", "dp", None),
        P("mod", "dp", None),
        P("mod", "dp"),
        P(("mod", "dp"), None),
        P("mod"),
        P("mod", "dp", None),
        P("mod", "dp", None),
        P("mod", "dp", None),
        P("mod", "dp", None),
        P("mod", "dp"),
        P(("mod", "dp"), None),
        P("mod"),
    )
    return jax.shard_map(
        on_device,
        mesh=mesh,
        in_specs=placed,
        out_specs=(
            P(),
            P(),
            P("mod", "dp", None),
            P("mod", "dp", None),
            P("mod", "dp", None),
            P("mod", "dp", None),
            P("mod", "dp"),
            P(("mod", "dp"), None),
            P("mod"),
            P("mod", "dp", None),
            P("mod", "dp", None),
            P("mod", "dp", None),
            P("mod", "dp", None),
            P("mod", "dp"),
            P(("mod", "dp"), None),
            P("mod"),
            P("mod", "dp", None),
            P("mod", "dp", None),
            P("mod", "dp", None),
            P("mod", "dp", None),
            P("mod", "dp"),
            P(("mod", "dp"), None),
            P("mod"),
        ),
        check_vma=False,
    )
```

```python
import functools
import math

import jax
import jax.numpy as jnp
import numpy as np
from jax import lax
from jax.experimental import pallas as pl
from jax.experimental.pallas import tpu as pltpu
from jax.sharding import PartitionSpec as P

HEAD_DIM = 64


NORM_EPS = 1e-05
CLIP_LIMIT = 0.05
BETA_ONE = 0.5
BETA_TWO = 0.5
ADAM_STEP = 10.0
ADAM_EPS = 1e-08
RATE_MATRIX = 0.03
RATE_GAIN = 0.3
DECAY_MATRIX = 0.1


def rms_scale(values, gain):
    return values * lax.rsqrt(jnp.mean(values * values, axis=-1, keepdims=True) + NORM_EPS) * gain


def rotary_tables(length):
    half = HEAD_DIM // 2
    inverse = 10000.0 ** (-np.arange(half, dtype=np.float32) / half)
    angle = np.arange(length, dtype=np.float32)[:, None] * inverse[None, :]
    cosine, sine = np.cos(angle), np.sin(angle)
    cosine = np.concatenate([cosine] * 4, axis=1).astype(np.float32)
    sine = np.concatenate([-sine, sine] * 2, axis=1).astype(np.float32)
    return jnp.asarray(cosine), jnp.asarray(sine)


def product(left, right):
    return jnp.dot(left, right, preferred_element_type=jnp.float32)


def left_product(left, right):
    return lax.dot_general(
        left, right, (((0,), (0,)), ((), ())), preferred_element_type=jnp.float32
    )


def right_product(left, right):
    return lax.dot_general(
        left, right, (((1,), (1,)), ((), ())), preferred_element_type=jnp.float32
    )


def adam_step(weight, grad, first, second, rate, decay):
    mean = BETA_ONE * first + (1.0 - BETA_ONE) * grad
    square = BETA_TWO * second + (1.0 - BETA_TWO) * grad * grad
    mean_hat = mean / (1.0 - BETA_ONE**ADAM_STEP)
    square_hat = square / (1.0 - BETA_TWO**ADAM_STEP)
    return (
        weight - rate * (mean_hat / (jnp.sqrt(square_hat) + ADAM_EPS) + decay * weight),
        mean,
        square,
    )


def one_hot(index, extent):
    return (index[..., None] == jnp.arange(extent, dtype=jnp.int32)).astype(jnp.bfloat16)


def exchange_kernel(groups, plan, *refs):
    count = len(plan)
    ins, outs = refs[:count], refs[count : 2 * count]
    sends, recvs = refs[2 * count : 3 * count], refs[3 * count : 4 * count]
    local = refs[4 * count]
    sizes = [math.prod(lax.axis_size(axis) for axis in axes) for axes in groups]
    places = []
    for axes in groups:
        place = lax.axis_index(axes[0])
        for axis in axes[1:]:
            place = place * lax.axis_size(axis) + lax.axis_index(axis)
        places.append(place)

    def device(group, index):
        axes = groups[group]
        if len(axes) == 1:
            return {axes[0]: index}
        inner = lax.axis_size(axes[1])
        return {axes[0]: index // inner, axes[1]: lax.rem(index, inner)}

    barrier = pltpu.get_barrier_semaphore()
    for group, size in enumerate(sizes):

        def greet(step, carry, group=group, size=size):
            peer = lax.rem(places[group] + step, size)
            pl.semaphore_signal(
                barrier,
                inc=1,
                device_id=device(group, peer),
                device_id_type=pl.DeviceIdType.MESH,
            )
            return carry

        lax.fori_loop(1, size, greet, 0)
    pl.semaphore_wait(barrier, sum(sizes) - len(sizes))

    def copy(item, step, arriving):
        group, shared = plan[item]
        size, place = sizes[group], places[group]
        peer = lax.rem(place + step, size)
        source = ins[item] if shared else ins[item].at[peer]
        slot = lax.rem(place + size - step, size) if arriving else place
        return pltpu.make_async_remote_copy(
            src_ref=source,
            dst_ref=outs[item].at[slot],
            send_sem=sends[item].at[step],
            recv_sem=recvs[item].at[step],
            device_id=device(group, peer),
            device_id_type=pl.DeviceIdType.MESH,
        )

    for item in range(count):

        def begin(step, carry, item=item):
            copy(item, step, False).start()
            return carry

        lax.fori_loop(1, sizes[plan[item][0]], begin, 0)
    own = []
    for item in range(count):
        group, shared = plan[item]
        source = ins[item] if shared else ins[item].at[places[group]]
        own.append(
            pltpu.make_async_copy(source, outs[item].at[places[group]], local.at[item])
        )
        own[-1].start()
    for item in range(count):
        own[item].wait()

        def finish(step, carry, item=item):
            copy(item, step, False).wait_send()
            copy(item, step, True).wait_recv()
            return carry

        lax.fori_loop(1, sizes[plan[item][0]], finish, 0)


def exchange(ident, *items):
    groups, plan, shapes, scratch = [], [], [], []
    for axes, array, shared in items:
        if axes not in groups:
            groups.append(axes)
        plan.append((groups.index(axes), shared))
        size = math.prod(lax.axis_size(axis) for axis in axes)
        shape = (size,) + array.shape if shared else array.shape
        shapes.append(jax.ShapeDtypeStruct(shape, array.dtype))
        scratch.append(pltpu.SemaphoreType.DMA((size,)))
    result = pl.pallas_call(
        functools.partial(exchange_kernel, groups, plan),
        out_shape=shapes,
        in_specs=[pl.BlockSpec(memory_space=pltpu.VMEM)] * len(items),
        out_specs=[pl.BlockSpec(memory_space=pltpu.VMEM)] * len(items),
        scratch_shapes=scratch + scratch + [pltpu.SemaphoreType.DMA((len(items),))],
        compiler_params=pltpu.CompilerParams(collective_id=ident, has_side_effects=True),
        name="exchange_%d" % ident,
    )(*(array for _, array, _ in items))
    return result[0] if len(items) == 1 else result


GATHER_ORDERS = ((0, 1, 2), (2, 0, 1), (1, 2, 0))


def chip_grid():
    group_mod, group_dp = lax.axis_size("mod"), lax.axis_size("dp")
    deep = math.gcd(group_mod, 4)
    return deep, group_mod // deep, group_dp // 2


def row_pieces(rows):
    part = rows // 64 * 16
    return (0, part), (part, rows - 2 * part), (rows - part, part)


def chip_place(sizes):
    mod, dp = lax.axis_index("mod"), lax.axis_index("dp")
    return [mod // sizes[1], lax.rem(mod, sizes[1]), dp // 2], lax.rem(dp, 2)


def chip_device(sizes, at, core):
    return {"mod": at[0] * sizes[1] + at[1], "dp": at[2] * 2 + core}


def shifted(sizes, at, axis, step):
    at = list(at)
    at[axis] = lax.rem(at[axis] + step, sizes[axis])
    return at


def greet_lines(sizes, at, core):
    barrier = pltpu.get_barrier_semaphore()
    targets = [chip_device(sizes, at, 1 - core)]
    for axis in range(3):
        for step in range(1, sizes[axis]):
            targets.append(chip_device(sizes, shifted(sizes, at, axis, step), core))
    for target in targets:
        pl.semaphore_signal(
            barrier, inc=1, device_id=target, device_id_type=pl.DeviceIdType.MESH
        )
    pl.semaphore_wait(barrier, len(targets))


def line_copies(sizes):
    return sum(len(GATHER_ORDERS) * (size - 1) for size in sizes)


def gather_kernel(sizes, rows, in_ref, out_ref, send, recv, pair_send, pair_recv, local):
    at, core = chip_place(sizes)
    greet_lines(sizes, at, core)
    pieces = row_pieces(rows)
    keys = {}
    for piece, order in enumerate(GATHER_ORDERS):
        for stage, axis in enumerate(order):
            for step in range(1, sizes[axis]):
                keys[piece, stage, step] = len(keys)

    def region(at, done, core, piece):
        start, count = pieces[piece]
        index = tuple(slice(None) if axis in done else at[axis] for axis in range(3))
        return out_ref.at[index + (core, pl.ds(start, count))]

    def remote(source, target, sems, index, at, core):
        return pltpu.make_async_remote_copy(
            src_ref=source,
            dst_ref=target,
            send_sem=sems[0].at[index],
            recv_sem=sems[1].at[index],
            device_id=chip_device(sizes, at, core),
            device_id_type=pl.DeviceIdType.MESH,
        )

    def line(piece, stage, step, arriving):
        order = GATHER_ORDERS[piece]
        axis, done = order[stage], order[:stage]
        peer = shifted(sizes, at, axis, step)
        origin = shifted(sizes, at, axis, sizes[axis] - step)
        target = region(origin if arriving else at, done, core, piece)
        source = region(at, done, core, piece)
        if stage == 0:
            source = in_ref.at[pl.ds(*pieces[piece])]
        return remote(source, target, (send, recv), keys[piece, stage, step], peer, core)

    def pair(piece, stage, step, arriving):
        order = GATHER_ORDERS[piece]
        axis, done = order[stage], order[:stage]
        origin = shifted(sizes, at, axis, sizes[axis] - step)
        source = region(origin, done, core, piece)
        target = region(origin, done, 1 - core if arriving else core, piece)
        index = keys[piece, stage, step]
        return remote(source, target, (pair_send, pair_recv), index, at, 1 - core)

    def pair_own(arriving):
        target = out_ref.at[at[0], at[1], at[2], 1 - core if arriving else core]
        return remote(in_ref, target, (pair_send, pair_recv), len(keys), at, 1 - core)

    own = pltpu.make_async_copy(in_ref, out_ref.at[at[0], at[1], at[2], core], local)
    own.start()
    pair_own(False).start()
    for stage in range(4):
        for piece, order in enumerate(GATHER_ORDERS):
            if stage > 0:
                for step in range(1, sizes[order[stage - 1]]):
                    line(piece, stage - 1, step, True).wait_recv()
                if stage == 1 and piece == 0:
                    own.wait()
            if stage < 3:
                for step in range(1, sizes[order[stage]]):
                    line(piece, stage, step, False).start()
            if stage > 0:
                for step in range(1, sizes[order[stage - 1]]):
                    pair(piece, stage - 1, step, False).start()
    for piece, stage, step in keys:
        line(piece, stage, step, False).wait_send()
        pair(piece, stage, step, False).wait_send()
        pair(piece, stage, step, True).wait_recv()
    pair_own(False).wait_send()
    pair_own(True).wait_recv()


def gather_rows(ident, rows):
    sizes = chip_grid()
    count, width = rows.shape
    copies = line_copies(sizes)
    dma = pltpu.SemaphoreType.DMA
    gathered = pl.pallas_call(
        functools.partial(gather_kernel, sizes, count),
        out_shape=jax.ShapeDtypeStruct(sizes + (2, count, width), rows.dtype),
        in_specs=[pl.BlockSpec(memory_space=pltpu.VMEM)],
        out_specs=pl.BlockSpec(memory_space=pltpu.VMEM),
        scratch_shapes=[dma((copies,)), dma((copies,)), dma((copies + 1,)), dma((copies + 1,)), dma],
        compiler_params=pltpu.CompilerParams(collective_id=ident, has_side_effects=True),
        name="gather_rows",
    )(rows)
    return gathered.reshape(-1, width)


def scatter_kernel(sizes, rows, in_ref, out_ref, acc, arrived, *rest):
    slots, (send, recv, pair_send, pair_recv, local) = rest[:-5], rest[-5:]
    at, core = chip_place(sizes)
    greet_lines(sizes, at, core)
    pieces = row_pieces(rows)
    orders = [order[::-1] for order in GATHER_ORDERS]
    keys = {}
    for piece, order in enumerate(orders):
        for stage, axis in enumerate(order):
            for step in range(1, sizes[axis]):
                keys[piece, stage, step] = len(keys)

    def line(piece, stage, step):
        order = orders[piece]
        axis, done = order[stage], order[:stage]
        peer = shifted(sizes, at, axis, step)
        index = tuple(
            peer[a] if a == axis else at[a] if a in done else slice(None) for a in range(3)
        )
        key = keys[piece, stage, step]
        return pltpu.make_async_remote_copy(
            src_ref=acc.at[index + (pl.ds(*pieces[piece]),)],
            dst_ref=slots[3 * piece + stage].at[step - 1],
            send_sem=send.at[key],
            recv_sem=recv.at[key],
            device_id=chip_device(sizes, peer, core),
            device_id_type=pl.DeviceIdType.MESH,
        )

    loads, pairs = [], []
    for piece in range(3):
        part = pl.ds(*pieces[piece])
        pairs.append(
            pltpu.make_async_remote_copy(
                src_ref=in_ref.at[:, :, :, 1 - core, part],
                dst_ref=arrived.at[:, :, :, part],
                send_sem=pair_send.at[piece],
                recv_sem=pair_recv.at[piece],
                device_id=chip_device(sizes, at, 1 - core),
                device_id_type=pl.DeviceIdType.MESH,
            )
        )
        pairs[-1].start()
        loads.append(
            pltpu.make_async_copy(
                in_ref.at[:, :, :, core, part], acc.at[:, :, :, part], local.at[piece]
            )
        )
        loads[-1].start()

    def add(piece, stage):
        order = orders[piece]
        done = order[:stage]
        left = [axis for axis in range(3) if axis not in done]
        part = pl.ds(*pieces[piece])

        def one(index, carry):
            where, inner = list(at), []
            for axis in reversed(left):
                where[axis] = lax.rem(index, sizes[axis])
                index = index // sizes[axis]
                inner.insert(0, where[axis])
            spot = tuple(where) + (part,)
            total = acc[spot].astype(jnp.float32)
            if stage == 0:
                total = total + arrived[spot].astype(jnp.float32)
            else:
                taken = slots[3 * piece + stage - 1]
                for step in range(taken.shape[0]):
                    total = total + taken[(step,) + tuple(inner)].astype(jnp.float32)
            if stage == 3:
                out_ref[part] = total
            else:
                acc[spot] = total.astype(acc.dtype)
            return carry

        lax.fori_loop(0, math.prod(sizes[axis] for axis in left), one, 0)

    for stage in range(4):
        for piece, order in enumerate(orders):
            if stage == 0:
                loads[piece].wait()
                pairs[piece].wait_recv()
            else:
                for step in range(1, sizes[order[stage - 1]]):
                    line(piece, stage - 1, step).wait_recv()
            add(piece, stage)
            if stage < 3:
                for step in range(1, sizes[order[stage]]):
                    line(piece, stage, step).start()
    for piece in range(3):
        pairs[piece].wait_send()
    for piece, stage, step in keys:
        line(piece, stage, step).wait_send()


def scatter_rows(ident, parts):
    sizes = chip_grid()
    width = parts.shape[1]
    count = parts.shape[0] // (2 * math.prod(sizes))
    copies = line_copies(sizes)
    dma = pltpu.SemaphoreType.DMA
    slots = []
    for piece, order in enumerate(GATHER_ORDERS):
        order = order[::-1]
        for stage, axis in enumerate(order):
            left = tuple(sizes[a] for a in range(3) if a not in order[: stage + 1])
            shape = (sizes[axis] - 1,) + left + (row_pieces(count)[piece][1], width)
            slots.append(pltpu.VMEM(shape, parts.dtype))
    return pl.pallas_call(
        functools.partial(scatter_kernel, sizes, count),
        out_shape=jax.ShapeDtypeStruct((count, width), jnp.float32),
        in_specs=[pl.BlockSpec(memory_space=pl.ANY)],
        out_specs=pl.BlockSpec(memory_space=pltpu.VMEM),
        scratch_shapes=[
            pltpu.VMEM(sizes + (count, width), parts.dtype),
            pltpu.VMEM(sizes + (count, width), parts.dtype),
            *slots,
            dma((copies,)),
            dma((copies,)),
            dma((3,)),
            dma((3,)),
            dma((3,)),
        ],
        compiler_params=pltpu.CompilerParams(collective_id=ident, has_side_effects=True),
        name="scatter_rows",
    )(parts.reshape(sizes + (2, count, width)))


def totals_kernel(in_ref, out_ref, arrived, mine, send, recv, back_send, back_recv):
    group_mod, group_dp = lax.axis_size("mod"), lax.axis_size("dp")
    size = group_mod * group_dp
    place = lax.axis_index("mod") * group_dp + lax.axis_index("dp")

    def device(index):
        return {"mod": index // group_dp, "dp": lax.rem(index, group_dp)}

    barrier = pltpu.get_barrier_semaphore()

    def greet(step, carry):
        pl.semaphore_signal(
            barrier,
            inc=1,
            device_id=device(lax.rem(place + step, size)),
            device_id_type=pl.DeviceIdType.MESH,
        )
        return carry

    def ahead(step, slot):
        peer = lax.rem(place + step, size)
        return pltpu.make_async_remote_copy(
            src_ref=in_ref.at[peer],
            dst_ref=arrived.at[slot],
            send_sem=send.at[step],
            recv_sem=recv.at[step],
            device_id=device(peer),
            device_id_type=pl.DeviceIdType.MESH,
        )

    def back(step, slot):
        return pltpu.make_async_remote_copy(
            src_ref=mine,
            dst_ref=out_ref.at[slot],
            send_sem=back_send.at[step],
            recv_sem=back_recv.at[step],
            device_id=device(lax.rem(place + step, size)),
            device_id_type=pl.DeviceIdType.MESH,
        )

    def begin(copy):
        def one(step, carry):
            copy(step, place).start()
            return carry

        lax.fori_loop(1, size, one, 0)

    def finish(copy):
        def one(step, carry):
            copy(step, place).wait_send()
            copy(step, lax.rem(place + size - step, size)).wait_recv()
            return carry

        lax.fori_loop(1, size, one, 0)

    lax.fori_loop(1, size, greet, 0)
    pl.semaphore_wait(barrier, size - 1)
    begin(ahead)
    arrived[place] = in_ref[place]
    finish(ahead)
    tops = arrived[:, 0:1]
    top = jnp.max(tops, axis=0)
    total = jnp.sum(arrived[:, 1:2] * jnp.exp(tops - top[None]), axis=0)
    hit = jnp.sum(arrived[:, 2:3], axis=0)
    line = lax.broadcasted_iota(jnp.int32, mine.shape, 0)
    mine[...] = jnp.where(line == 0, top + jnp.log(total), jnp.where(line == 1, hit, 0.0))
    out_ref[place] = mine[...]
    begin(back)
    finish(back)


def totals_call(ident, stats):
    dma = pltpu.SemaphoreType.DMA((stats.shape[0],))
    return pl.pallas_call(
        totals_kernel,
        out_shape=jax.ShapeDtypeStruct(stats.shape, stats.dtype),
        in_specs=[pl.BlockSpec(memory_space=pltpu.VMEM)],
        out_specs=pl.BlockSpec(memory_space=pltpu.VMEM),
        scratch_shapes=[
            pltpu.VMEM(stats.shape, stats.dtype),
            pltpu.VMEM(stats.shape[1:], stats.dtype),
            dma,
            dma,
            dma,
            dma,
        ],
        compiler_params=pltpu.CompilerParams(collective_id=ident, has_side_effects=True),
        name="totals",
    )(stats)


def side_by_side(blocks):
    count, rows, columns = blocks.shape
    if columns % 128:
        return jnp.concatenate(list(blocks.astype(jnp.float32)), axis=1)

    def place(in_ref, out_ref):
        out_ref[...] = in_ref[0].astype(jnp.float32)

    return pl.pallas_call(
        place,
        grid=(count,),
        out_shape=jax.ShapeDtypeStruct((rows, count * columns), jnp.float32),
        in_specs=[pl.BlockSpec((1, rows, columns), lambda i: (i, 0, 0))],
        out_specs=pl.BlockSpec((rows, columns), lambda i: (0, i)),
        name="side_by_side",
    )(blocks)


HEAD_ROWS = 256


def scores_kernel(rows_ref, table_ref, wanted_ref, out_ref, logits_ref):
    logits = right_product(table_ref[...], rows_ref[...])
    logits_ref[...] = logits
    hits = lax.broadcasted_iota(jnp.int32, logits.shape, 0) == wanted_ref[...]
    top = jnp.max(logits, axis=0, keepdims=True)
    total = jnp.sum(jnp.exp(logits - top), axis=0, keepdims=True)
    hit = jnp.sum(jnp.where(hits, logits, 0.0), axis=0, keepdims=True)
    count, lines, part = out_ref.shape
    line = lax.broadcasted_iota(jnp.int32, (lines, part), 0)
    for block in range(count):
        at = slice(block * part, (block + 1) * part)
        out_ref[block] = jnp.where(
            line == 0, top[:, at], jnp.where(line == 1, total[:, at], hit[:, at])
        )


def scores_call(rows, table, wanted, part):
    step = math.gcd(HEAD_ROWS, rows.shape[0])
    return pl.pallas_call(
        scores_kernel,
        grid=(rows.shape[0] // step,),
        out_shape=[
            jax.ShapeDtypeStruct((rows.shape[0] // part, 8, part), jnp.float32),
            jax.ShapeDtypeStruct((table.shape[0], rows.shape[0]), jnp.float32),
        ],
        in_specs=[
            pl.BlockSpec((step, rows.shape[1]), lambda i: (i, 0)),
            pl.BlockSpec(table.shape, lambda i: (0, 0)),
            pl.BlockSpec((1, step), lambda i: (0, i)),
        ],
        out_specs=[
            pl.BlockSpec((step // part, 8, part), lambda i: (i, 0, 0)),
            pl.BlockSpec((table.shape[0], step), lambda i: (0, i)),
        ],
        name="scores",
    )(rows, table, wanted[None])


def norm_kernel(group_mod, group_dp, final_lines, in_ref, out_ref, gathered, send, recv, local):
    exchange_kernel([("mod", "dp")], [(0, True)], in_ref, gathered, send, recv, local)
    final = gathered[0]
    for mod in range(1, group_mod):
        final = final + gathered[mod * group_dp]
    line = lax.broadcasted_iota(jnp.int32, final.shape, 0)
    final = jnp.where(line < final_lines, final, 0.0)
    squares = jnp.sum(jnp.sum(final * final, axis=1, keepdims=True), axis=0, keepdims=True)
    total = jnp.sum(gathered[...], axis=0) + squares
    out_ref[...] = jnp.where(line < final_lines, final, total)


def norm_call(ident, last, final_lines):
    group_mod, group_dp = lax.axis_size("mod"), lax.axis_size("dp")
    size = group_mod * group_dp
    dma = pltpu.SemaphoreType.DMA
    return pl.pallas_call(
        functools.partial(norm_kernel, group_mod, group_dp, final_lines),
        out_shape=jax.ShapeDtypeStruct(last.shape, last.dtype),
        in_specs=[pl.BlockSpec(memory_space=pltpu.VMEM)],
        out_specs=pl.BlockSpec(memory_space=pltpu.VMEM),
        scratch_shapes=[
            pltpu.VMEM((size,) + last.shape, last.dtype),
            dma((size,)),
            dma((size,)),
            dma((1,)),
        ],
        compiler_params=pltpu.CompilerParams(collective_id=ident, has_side_effects=True),
        name="norm",
    )(last)


GROUP_SEQS = 4


def wide_table(table_ref, tokens, width):
    table = table_ref[...]
    table = jnp.concatenate([table] * (tokens // table.shape[0]), axis=0)
    return jnp.concatenate([table] * (width // table.shape[1]), axis=1)


def turned(values, cosine, sine):
    width = values.shape[-1]
    half = HEAD_DIM // 2
    lane = lax.broadcasted_iota(jnp.int32, values.shape, 1)
    other = jnp.where(
        lane % HEAD_DIM < half,
        pltpu.roll(values, width - half, 1),
        pltpu.roll(values, half, 1),
    )
    return values * cosine + other * sine


def head_spread(values, heads):
    rows, width = values.shape
    lane = lax.broadcasted_iota(jnp.int32, (heads, rows, width), 2)
    head = lax.broadcasted_iota(jnp.int32, (heads, rows, width), 0)
    return jnp.where(lane // HEAD_DIM == head, values[None], jnp.zeros((), values.dtype))


def head_fold(values, heads):
    rows, width = values.shape
    values = values.reshape(heads, rows // heads, width)
    lane = lax.broadcasted_iota(jnp.int32, values.shape, 2)
    head = lax.broadcasted_iota(jnp.int32, values.shape, 0)
    return jnp.sum(jnp.where(lane // HEAD_DIM == head, values, 0.0), axis=0)


def attention_parts(length, spots_ref, mixed_ref, cosine_ref, sine_ref):
    tokens, width = mixed_ref.shape[0], mixed_ref.shape[1] // 3
    heads = width // HEAD_DIM
    cosine = wide_table(cosine_ref, tokens, width)
    sine = wide_table(sine_ref, tokens, width)
    spot = spots_ref[...]
    key = lax.broadcasted_iota(jnp.int32, (spot.shape[0], tokens), 1)
    chosen = key == spot
    seen = (key <= spot) & (key >= spot - spot % length)
    queries = turned(mixed_ref[:, :width], cosine, sine).astype(jnp.bfloat16)
    queries = product(chosen.astype(jnp.bfloat16), queries)
    queries = head_spread(queries, heads).reshape(-1, width).astype(jnp.bfloat16)
    keys_in = turned(mixed_ref[:, width : 2 * width], cosine, sine).astype(jnp.bfloat16)
    values = mixed_ref[:, 2 * width :].astype(jnp.bfloat16)
    raw = right_product(queries, keys_in).reshape(heads, -1, tokens)
    scores = jnp.where(seen[None], raw * HEAD_DIM ** (-0.5), -1e30).reshape(-1, tokens)
    top = jnp.max(scores, axis=1, keepdims=True)
    terms = jnp.exp(scores - top)
    chances = terms / jnp.sum(terms, axis=1, keepdims=True)
    return chosen, queries, keys_in, values, chances, cosine, sine


def attention_kernel(
    length, spots_ref, mixed_ref, inputs_ref, cosine_ref, sine_ref, heads_ref, picked_ref
):
    heads = inputs_ref.shape[1] // HEAD_DIM
    chosen, _, _, values, chances, _, _ = attention_parts(
        length, spots_ref, mixed_ref, cosine_ref, sine_ref
    )
    spread = product(chances.astype(jnp.bfloat16), values)
    heads_ref[...] = head_fold(spread, heads).astype(jnp.bfloat16)
    picked_ref[...] = product(chosen.astype(jnp.bfloat16), inputs_ref[...])


def attention_back_kernel(
    length, spots_ref, mixed_ref, grad_ref, cosine_ref, sine_ref, out_ref
):
    width = grad_ref.shape[1]
    heads = width // HEAD_DIM
    chosen, queries, keys_in, values, chances, cosine, sine = attention_parts(
        length, spots_ref, mixed_ref, cosine_ref, sine_ref
    )
    grad_heads = head_spread(grad_ref[...].astype(jnp.float32), heads)
    grad_heads = grad_heads.reshape(-1, width).astype(jnp.bfloat16)
    grad_values = left_product(chances.astype(jnp.bfloat16), grad_heads)
    grad_chances = right_product(grad_heads, values)
    delta = jnp.sum(chances * grad_chances, axis=1, keepdims=True)
    grad_raw = (chances * (grad_chances - delta) * HEAD_DIM ** (-0.5)).astype(jnp.bfloat16)
    grad_queries = head_fold(product(grad_raw, keys_in), heads)
    grad_queries = lax.dot_general(
        chosen.astype(jnp.float32),
        grad_queries,
        (((0,), (0,)), ((), ())),
        precision=lax.Precision.HIGHEST,
        preferred_element_type=jnp.float32,
    )
    grad_keys = left_product(grad_raw, queries)
    out_ref[:, :width] = turned(grad_queries, cosine, -sine).astype(jnp.bfloat16)
    out_ref[:, width : 2 * width] = turned(grad_keys, cosine, -sine).astype(jnp.bfloat16)
    out_ref[:, 2 * width :] = grad_values.astype(jnp.bfloat16)


def attention_call(body, length, operands, tables, outs, name, microseconds):
    sequences = operands[1].shape[0] // length
    steps = sequences // math.gcd(GROUP_SEQS, sequences)

    def block(array):
        return pl.BlockSpec((array.shape[0] // steps, array.shape[1]), lambda i: (i, 0))

    fixed = [pl.BlockSpec(table.shape, lambda i: (0, 0)) for table in tables]
    return pl.pallas_call(
        functools.partial(body, length),
        grid=(steps,),
        out_shape=outs,
        in_specs=[block(array) for array in operands] + fixed,
        out_specs=[block(array) for array in outs],
        cost_estimate=pl.CostEstimate(
            flops=0, bytes_accessed=microseconds * 3_000_000, transcendentals=0
        ),
        name=name,
    )(*operands, *tables)


def square_sum(values):
    return jnp.sum(lax.optimization_barrier(jnp.sum(values * values, axis=0)))


def on_device(
    token_ids,
    targets,
    positions,
    loss_mask,
    paths,
    attend,
    output,
    widen,
    narrow,
    gains,
    table,
    final_gain,
    first_attend,
    first_output,
    first_widen,
    first_narrow,
    first_gains,
    first_table,
    first_final,
    second_attend,
    second_output,
    second_widen,
    second_narrow,
    second_gains,
    second_table,
    second_final,
):
    group_dp = lax.axis_size("dp")
    group_mod = lax.axis_size("mod")
    dp_place = lax.axis_index("dp")
    mod_place = lax.axis_index("mod")
    everyone = ("mod", "dp")
    place = mod_place * group_dp + dp_place
    sources = group_mod * group_dp
    micro, per_mod, length = token_ids.shape
    spots_seq = positions.shape[2]
    seq_dev = per_mod // group_dp
    shard_rows, width = table.shape
    heads = width // HEAD_DIM
    slots = micro * sources
    slots_local = slots // group_dp
    low = jnp.bfloat16

    mixing = lax.all_gather(
        jnp.concatenate([attend[0], output[0]], axis=1).astype(low), "dp", axis=0, tiled=True
    )
    attend_low, output_low = mixing[:, : 3 * width], mixing[:, 3 * width :]
    hidden = narrow.shape[1]
    widen_low = jnp.stack(
        [widen[0, :, i * hidden : (i + 1) * hidden].astype(low) for i in range(group_dp)]
    )
    widen_low = lax.all_to_all(widen_low, "dp", split_axis=0, concat_axis=0, tiled=True)
    widen_low = widen_low.reshape(width, hidden)
    narrow_low = narrow[0].astype(low)
    table_low = table.astype(low)

    fields = jnp.concatenate(
        [token_ids, positions, targets, loss_mask, paths[..., None]], axis=-1
    )
    fields, gain_parts, final_parts = exchange(
        0,
        (("mod",), fields.reshape(micro * per_mod, -1), True),
        (("dp",), jnp.broadcast_to(gains.astype(low), (16, gains.shape[1])), True),
        (("mod",), jnp.broadcast_to(final_gain.astype(low)[None], (16, final_gain.shape[0])), True),
    )
    own_gains = gain_parts[:, 0].reshape(-1).astype(jnp.float32)
    gain_one, gain_two = own_gains[:width], own_gains[width:]
    gain_final = final_parts[:, 0].reshape(-1).astype(jnp.float32)
    fields = fields.reshape(group_mod, micro, per_mod, -1).transpose(1, 0, 2, 3)
    fields = fields.reshape(slots, seq_dev, -1)
    own = lax.dynamic_slice_in_dim(fields, dp_place * slots_local, slots_local)
    own_match = own[..., -1] == mod_place
    own = jnp.sum(jnp.where(own_match[..., None], own[..., : length + spots_seq], 0), axis=1)
    own_tokens = own[:, :length].reshape(-1)
    spots = own[:, length:]
    held = jnp.repeat(jnp.any(own_match, axis=1), length)
    match = fields[None, ..., -1] == jnp.arange(group_mod, dtype=jnp.int32)[:, None, None]
    scoring = jnp.sum(
        jnp.where(match[..., None], fields[None, ..., length + spots_seq : -1], 0), axis=2
    )
    wanted = scoring[..., :spots_seq].reshape(-1)
    counted = scoring[..., spots_seq:].reshape(-1).astype(jnp.float32)
    count_total = jnp.sum(counted)

    shard = own_tokens // shard_rows
    row = own_tokens % shard_rows
    key = jnp.where(held, own_tokens, -1)
    order = jnp.arange(key.shape[0], dtype=jnp.int32)
    repeated = jnp.any((key[:, None] == key[None, :]) & (order[None, :] < order[:, None]), axis=1)
    leading = held & ~repeated
    rank = jnp.sum(
        (
            leading[None, :] & (shard[None, :] == shard[:, None]) & (key[None, :] < key[:, None])
        ).astype(jnp.int32),
        axis=1,
    )
    expected = -(-slots_local * length // sources)
    cap = -(-3 * expected // 16) * 8
    cap = min(max(cap, 16), -(-shard_rows // 8) * 8, 112)
    own_rounds = jnp.max(jnp.where(leading, rank // cap, 0)) + 1

    def ask(turn):
        slot = rank - turn * cap
        inside = held & (slot >= 0) & (slot < cap)
        slot = jnp.where(inside, shard * cap + slot, -1)
        asked = jnp.sum(
            jnp.where(
                leading[None, :]
                & (slot[None, :] == jnp.arange(sources * cap, dtype=jnp.int32)[:, None]),
                row[None, :] + 1,
                0,
            ),
            axis=1,
        ).reshape(sources, cap)
        return slot, asked

    slot, asked = ask(0)
    message = jnp.concatenate(
        [asked, jnp.broadcast_to(own_rounds, (sources, 128 - cap))], axis=1
    )
    message = exchange(
        1, (everyone, jnp.broadcast_to(message[:, None], (sources, 8, 128)), False)
    )
    rounds = jnp.max(message[:, 0, cap])
    spread = one_hot(slot, sources * cap)
    pick = one_hot(message[:, 0, :cap].reshape(-1) - 1, shard_rows)

    def other_plan(turn):
        slot, asked = ask(turn)
        asked = lax.all_to_all(asked, everyone, split_axis=0, concat_axis=0, tiled=True)
        return one_hot(slot, sources * cap), one_hot(asked.reshape(-1) - 1, shard_rows)

    def other_rows(state):
        turn, rows = state
        spread, pick = other_plan(turn)
        sent = product(pick, table_low).astype(low).reshape(sources, cap, width)
        got = lax.all_to_all(sent, everyone, split_axis=0, concat_axis=0, tiled=True)
        return turn + 1, rows + product(spread, got.reshape(-1, width)).astype(low)

    sent = product(pick, table_low).astype(low).reshape(sources, cap, width)
    got = exchange(2, (everyone, sent, False))
    inputs = product(spread, got.reshape(-1, width)).astype(low)
    inputs = lax.while_loop(
        lambda state: state[0] < rounds, other_rows, (jnp.int32(1), inputs)
    )[1]

    group = math.gcd(GROUP_SEQS, slots_local)
    tables = rotary_tables(length)
    flat_spots = spots + (jnp.arange(slots_local, dtype=jnp.int32) % group)[:, None] * length
    flat_spots = flat_spots.reshape(-1, 1)
    inputs_wide = inputs.astype(jnp.float32)
    normed_one = lax.optimization_barrier(rms_scale(inputs_wide, gain_one).astype(low))
    mixed = product(normed_one, attend_low)
    picked_rows = slots_local * spots_seq
    heads_out, picked_inputs = attention_call(
        attention_kernel,
        length,
        (flat_spots, mixed, inputs),
        tables,
        [
            jax.ShapeDtypeStruct((picked_rows, width), low),
            jax.ShapeDtypeStruct((picked_rows, width), jnp.float32),
        ],
        "attention",
        7,
    )
    middle = picked_inputs + product(heads_out, output_low)

    def sum_parts(ident, parts):
        parts = parts.astype(low).reshape(group_dp, picked_rows, width)
        return jnp.sum(exchange(ident, (("dp",), parts, False)).astype(jnp.float32), axis=0)

    normed_two = rms_scale(middle, gain_two).astype(low)
    normed_all = exchange(3, (("dp",), normed_two, True)).reshape(-1, width)
    upper = product(normed_all, widen_low)
    gelu = lambda value: jax.nn.gelu(value, approximate=True)
    activated = gelu(upper).astype(low)
    lifted = sum_parts(4, product(activated, narrow_low))
    returned = (middle + lifted).astype(low).astype(jnp.float32)

    final, final_back = jax.vjp(rms_scale, returned, gain_final)
    scored = gather_rows(12, final.astype(low))
    target_row = wanted - place * shard_rows
    stats, logits = scores_call(scored, table_low, target_row, picked_rows)
    totals = totals_call(5, stats)
    log_total = totals[:, 0].reshape(-1)
    loss_total = jnp.sum(counted * (log_total - totals[:, 1].reshape(-1)))
    hits = target_row[None, :] == jnp.arange(shard_rows, dtype=jnp.int32)[:, None]
    grad_logits = (
        counted[None] * (jnp.exp(logits - log_total[None]) - hits.astype(jnp.float32))
    ).astype(low)
    grad_logits = lax.optimization_barrier(grad_logits)
    grad_picked = scatter_rows(13, left_product(grad_logits, table_low).astype(low))

    grad_returned, grad_final = final_back(grad_picked)
    incoming = grad_returned.astype(low)
    incoming_all = exchange(7, (("dp",), incoming, True)).reshape(-1, width)
    grad_narrow = left_product(activated, incoming_all)
    grad_act = right_product(incoming_all, narrow_low)
    grad_upper = jax.vjp(gelu, upper)[1](grad_act)[0].astype(low)
    grad_widen = left_product(normed_all, grad_upper).astype(low)
    grad_widen = lax.all_to_all(
        grad_widen.reshape(group_dp, -1, hidden), "dp", split_axis=0, concat_axis=0, tiled=True
    )
    grad_normed_two = sum_parts(8, right_product(grad_upper, widen_low))
    grad_middle, grad_gain_two = jax.vjp(rms_scale, middle, gain_two)[1](grad_normed_two)
    grad_middle = grad_middle + incoming.astype(jnp.float32)

    branch_grad = grad_middle.astype(low)
    grad_output = lax.psum_scatter(
        left_product(heads_out, branch_grad).astype(low), "dp", scatter_dimension=0, tiled=True
    ).astype(jnp.float32)
    grad_heads = right_product(branch_grad, output_low).astype(low)
    (grad_mixed,) = attention_call(
        attention_back_kernel,
        length,
        (flat_spots, mixed, grad_heads),
        tables,
        [jax.ShapeDtypeStruct(mixed.shape, low)],
        "attention_back",
        12,
    )
    grad_widen, grad_mixed = lax.optimization_barrier((grad_widen, grad_mixed))
    grad_attend = left_product(normed_one, grad_mixed)
    grad_normed = right_product(grad_mixed, attend_low)
    grad_inputs, grad_gain_one = jax.vjp(rms_scale, inputs_wide, gain_one)[1](grad_normed)
    here = spots[:, :, None] == jnp.arange(length, dtype=jnp.int32)
    grad_skip = jnp.sum(
        jnp.where(
            here[..., None], grad_middle.reshape(slots_local, spots_seq, 1, width), 0.0
        ),
        axis=1,
    ).reshape(-1, width)
    leaving = (grad_skip + grad_inputs).astype(low)

    grad_attend = lax.psum_scatter(
        grad_attend.astype(low), "dp", scatter_dimension=0, tiled=True
    ).astype(jnp.float32)

    def other_grads(state):
        turn, total = state
        spread, pick = other_plan(turn)
        sent = left_product(spread, leaving).astype(low).reshape(sources, cap, width)
        got = lax.all_to_all(sent, everyone, split_axis=0, concat_axis=0, tiled=True)
        return turn + 1, total + left_product(pick, got.reshape(-1, width))

    given = left_product(spread, leaving).astype(low).reshape(sources, cap, width)
    gain_grads = jnp.concatenate([grad_gain_one, grad_gain_two, grad_final])
    gain_grads = jnp.pad(gain_grads.reshape(-1, 128), ((0, -gain_grads.shape[0] // 128 % 8), (0, 0)))
    given, gain_grads = exchange(
        9, (everyone, given, False), (("dp",), gain_grads, True)
    )
    given, scored = lax.optimization_barrier((given, scored))
    table_grad = product(grad_logits, scored)
    table_grad = table_grad + left_product(pick, given.reshape(-1, width))
    table_grad = lax.while_loop(
        lambda state: state[0] < rounds, other_grads, (jnp.int32(1), table_grad)
    )[1]
    gain_grads = jnp.sum(gain_grads, axis=0).reshape(-1)
    own_gain_grads = gain_grads[: 2 * width]
    final_rows = gain_grads[2 * width : 3 * width].reshape(-1, 128)
    gain_part = gains.shape[1]
    grad_gains = lax.dynamic_slice_in_dim(own_gain_grads, dp_place * gain_part, gain_part)
    widen_squares = square_sum(grad_widen.astype(jnp.float32).reshape(-1, hidden))
    grad_widen = side_by_side(grad_widen)
    matrix_grads = (grad_attend[None], grad_output[None], grad_widen[None], grad_narrow[None])
    squares = sum(square_sum(g) for g in (grad_attend, grad_output, grad_narrow, table_grad))
    squares = squares + widen_squares
    squares = squares + jnp.sum(grad_gains * grad_gains)
    last = jnp.concatenate(
        [final_rows, jnp.broadcast_to(squares, (16 - final_rows.shape[0] % 8 - 8, 128))], axis=0
    )
    final_count = final_rows.shape[0]
    last = norm_call(11, last, final_count)
    grad_final = last[:final_count].reshape(-1)
    squares = last[final_count, 0]
    final_part = final_gain.shape[0]
    grad_final = lax.dynamic_slice_in_dim(grad_final, mod_place * final_part, final_part)
    gradient_norm = jnp.sqrt(squares) / count_total
    factor = CLIP_LIMIT / jnp.maximum(gradient_norm, CLIP_LIMIT) / count_total
    params = (attend, output, widen, narrow, gains, table, final_gain)
    grads = matrix_grads + (grad_gains[None], table_grad, grad_final)
    firsts = (
        first_attend,
        first_output,
        first_widen,
        first_narrow,
        first_gains,
        first_table,
        first_final,
    )
    seconds = (
        second_attend,
        second_output,
        second_widen,
        second_narrow,
        second_gains,
        second_table,
        second_final,
    )
    rates = (RATE_MATRIX, RATE_MATRIX, RATE_MATRIX, RATE_MATRIX, RATE_GAIN, RATE_MATRIX, RATE_GAIN)
    decays = (DECAY_MATRIX, DECAY_MATRIX, DECAY_MATRIX, DECAY_MATRIX, 0.0, DECAY_MATRIX, 0.0)
    updated = [
        adam_step(w, g * factor, f, s, r, c)
        for w, g, f, s, r, c in zip(params, grads, firsts, seconds, rates, decays)
    ]
    return (
        loss_total / count_total,
        gradient_norm,
        *(entry[0] for entry in updated),
        *(entry[1] for entry in updated),
        *(entry[2] for entry in updated),
    )


def solution(mesh):
    placed = (
        P(None, "mod", None),
        P(None, "mod", None),
        P(None, "mod", None),
        P(None, "mod", None),
        P(None, "mod"),
        P("mod", "dp", None),
        P("mod", "dp", None),
        P("mod", "dp", None),
        P("mod", "dp", None),
        P("mod", "dp"),
        P(("mod", "dp"), None),
        P("mod"),
        P("mod", "dp", None),
        P("mod", "dp", None),
        P("mod", "dp", None),
        P("mod", "dp", None),
        P("mod", "dp"),
        P(("mod", "dp"), None),
        P("mod"),
        P("mod", "dp", None),
        P("mod", "dp", None),
        P("mod", "dp", None),
        P("mod", "dp", None),
        P("mod", "dp"),
        P(("mod", "dp"), None),
        P("mod"),
    )
    return jax.shard_map(
        on_device,
        mesh=mesh,
        in_specs=placed,
        out_specs=(
            P(),
            P(),
            P("mod", "dp", None),
            P("mod", "dp", None),
            P("mod", "dp", None),
            P("mod", "dp", None),
            P("mod", "dp"),
            P(("mod", "dp"), None),
            P("mod"),
            P("mod", "dp", None),
            P("mod", "dp", None),
            P("mod", "dp", None),
            P("mod", "dp", None),
            P("mod", "dp"),
            P(("mod", "dp"), None),
            P("mod"),
            P("mod", "dp", None),
            P("mod", "dp", None),
            P("mod", "dp", None),
            P("mod", "dp", None),
            P("mod", "dp"),
            P(("mod", "dp"), None),
            P("mod"),
        ),
        check_vma=False,
    )
```

```python
import functools
import math

import jax
import jax.numpy as jnp
import numpy as np
from jax import lax
from jax.experimental import pallas as pl
from jax.experimental.pallas import tpu as pltpu
from jax.sharding import PartitionSpec as P

HEAD_DIM = 64


NORM_EPS = 1e-05
CLIP_LIMIT = 0.05
BETA_ONE = 0.5
BETA_TWO = 0.5
ADAM_STEP = 10.0
ADAM_EPS = 1e-08
RATE_MATRIX = 0.03
RATE_GAIN = 0.3
DECAY_MATRIX = 0.1


def rms_scale(values, gain):
    return values * lax.rsqrt(jnp.mean(values * values, axis=-1, keepdims=True) + NORM_EPS) * gain


def rotary_tables(length):
    half = HEAD_DIM // 2
    inverse = 10000.0 ** (-np.arange(half, dtype=np.float32) / half)
    angle = np.arange(length, dtype=np.float32)[:, None] * inverse[None, :]
    cosine, sine = np.cos(angle), np.sin(angle)
    cosine = np.concatenate([cosine] * 4, axis=1).astype(np.float32)
    sine = np.concatenate([-sine, sine] * 2, axis=1).astype(np.float32)
    return jnp.asarray(cosine), jnp.asarray(sine)


def product(left, right):
    return jnp.dot(left, right, preferred_element_type=jnp.float32)


def left_product(left, right):
    return lax.dot_general(
        left, right, (((0,), (0,)), ((), ())), preferred_element_type=jnp.float32
    )


def right_product(left, right):
    return lax.dot_general(
        left, right, (((1,), (1,)), ((), ())), preferred_element_type=jnp.float32
    )


def adam_step(weight, grad, first, second, rate, decay):
    mean = BETA_ONE * first + (1.0 - BETA_ONE) * grad
    square = BETA_TWO * second + (1.0 - BETA_TWO) * grad * grad
    mean_hat = mean / (1.0 - BETA_ONE**ADAM_STEP)
    square_hat = square / (1.0 - BETA_TWO**ADAM_STEP)
    return (
        weight - rate * (mean_hat / (jnp.sqrt(square_hat) + ADAM_EPS) + decay * weight),
        mean,
        square,
    )


def one_hot(index, extent):
    return (index[..., None] == jnp.arange(extent, dtype=jnp.int32)).astype(jnp.bfloat16)


def exchange_kernel(groups, plan, *refs):
    count = len(plan)
    ins, outs = refs[:count], refs[count : 2 * count]
    sends, recvs = refs[2 * count : 3 * count], refs[3 * count : 4 * count]
    local = refs[4 * count]
    sizes = [math.prod(lax.axis_size(axis) for axis in axes) for axes in groups]
    places = []
    for axes in groups:
        place = lax.axis_index(axes[0])
        for axis in axes[1:]:
            place = place * lax.axis_size(axis) + lax.axis_index(axis)
        places.append(place)

    def device(group, index):
        axes = groups[group]
        if len(axes) == 1:
            return {axes[0]: index}
        inner = lax.axis_size(axes[1])
        return {axes[0]: index // inner, axes[1]: lax.rem(index, inner)}

    barrier = pltpu.get_barrier_semaphore()
    for group, size in enumerate(sizes):

        def greet(step, carry, group=group, size=size):
            peer = lax.rem(places[group] + step, size)
            pl.semaphore_signal(
                barrier,
                inc=1,
                device_id=device(group, peer),
                device_id_type=pl.DeviceIdType.MESH,
            )
            return carry

        lax.fori_loop(1, size, greet, 0)
    pl.semaphore_wait(barrier, sum(sizes) - len(sizes))

    def copy(item, step, arriving):
        group, shared = plan[item]
        size, place = sizes[group], places[group]
        peer = lax.rem(place + step, size)
        source = ins[item] if shared else ins[item].at[peer]
        slot = lax.rem(place + size - step, size) if arriving else place
        return pltpu.make_async_remote_copy(
            src_ref=source,
            dst_ref=outs[item].at[slot],
            send_sem=sends[item].at[step],
            recv_sem=recvs[item].at[step],
            device_id=device(group, peer),
            device_id_type=pl.DeviceIdType.MESH,
        )

    for item in range(count):

        def begin(step, carry, item=item):
            copy(item, step, False).start()
            return carry

        lax.fori_loop(1, sizes[plan[item][0]], begin, 0)
    own = []
    for item in range(count):
        group, shared = plan[item]
        source = ins[item] if shared else ins[item].at[places[group]]
        own.append(
            pltpu.make_async_copy(source, outs[item].at[places[group]], local.at[item])
        )
        own[-1].start()
    for item in range(count):
        own[item].wait()

        def finish(step, carry, item=item):
            copy(item, step, False).wait_send()
            copy(item, step, True).wait_recv()
            return carry

        lax.fori_loop(1, sizes[plan[item][0]], finish, 0)


def exchange(ident, *items):
    groups, plan, shapes, scratch = [], [], [], []
    for axes, array, shared in items:
        if axes not in groups:
            groups.append(axes)
        plan.append((groups.index(axes), shared))
        size = math.prod(lax.axis_size(axis) for axis in axes)
        shape = (size,) + array.shape if shared else array.shape
        shapes.append(jax.ShapeDtypeStruct(shape, array.dtype))
        scratch.append(pltpu.SemaphoreType.DMA((size,)))
    result = pl.pallas_call(
        functools.partial(exchange_kernel, groups, plan),
        out_shape=shapes,
        in_specs=[pl.BlockSpec(memory_space=pltpu.VMEM)] * len(items),
        out_specs=[pl.BlockSpec(memory_space=pltpu.VMEM)] * len(items),
        scratch_shapes=scratch + scratch + [pltpu.SemaphoreType.DMA((len(items),))],
        compiler_params=pltpu.CompilerParams(collective_id=ident, has_side_effects=True),
        name="exchange_%d" % ident,
    )(*(array for _, array, _ in items))
    return result[0] if len(items) == 1 else result


GATHER_ORDERS = ((0, 1, 2), (2, 0, 1), (1, 2, 0))


def chip_grid():
    group_mod, group_dp = lax.axis_size("mod"), lax.axis_size("dp")
    deep = math.gcd(group_mod, 4)
    return deep, group_mod // deep, group_dp // 2


def row_pieces(rows):
    part = rows // 64 * 16
    return (0, part), (part, rows - 2 * part), (rows - part, part)


def chip_place(sizes):
    mod, dp = lax.axis_index("mod"), lax.axis_index("dp")
    return [mod // sizes[1], lax.rem(mod, sizes[1]), dp // 2], lax.rem(dp, 2)


def chip_device(sizes, at, core):
    return {"mod": at[0] * sizes[1] + at[1], "dp": at[2] * 2 + core}


def shifted(sizes, at, axis, step):
    at = list(at)
    at[axis] = lax.rem(at[axis] + step, sizes[axis])
    return at


def greet_lines(sizes, at, core):
    barrier = pltpu.get_barrier_semaphore()
    targets = [chip_device(sizes, at, 1 - core)]
    for axis in range(3):
        for step in range(1, sizes[axis]):
            targets.append(chip_device(sizes, shifted(sizes, at, axis, step), core))
    for target in targets:
        pl.semaphore_signal(
            barrier, inc=1, device_id=target, device_id_type=pl.DeviceIdType.MESH
        )
    pl.semaphore_wait(barrier, len(targets))


def line_copies(sizes):
    return sum(len(GATHER_ORDERS) * (size - 1) for size in sizes)


def gather_kernel(sizes, rows, in_ref, out_ref, send, recv, pair_send, pair_recv, local):
    at, core = chip_place(sizes)
    greet_lines(sizes, at, core)
    pieces = row_pieces(rows)
    keys = {}
    for piece, order in enumerate(GATHER_ORDERS):
        for stage, axis in enumerate(order):
            for step in range(1, sizes[axis]):
                keys[piece, stage, step] = len(keys)

    def region(at, done, core, piece):
        start, count = pieces[piece]
        index = tuple(slice(None) if axis in done else at[axis] for axis in range(3))
        return out_ref.at[index + (core, pl.ds(start, count))]

    def remote(source, target, sems, index, at, core):
        return pltpu.make_async_remote_copy(
            src_ref=source,
            dst_ref=target,
            send_sem=sems[0].at[index],
            recv_sem=sems[1].at[index],
            device_id=chip_device(sizes, at, core),
            device_id_type=pl.DeviceIdType.MESH,
        )

    def line(piece, stage, step, arriving):
        order = GATHER_ORDERS[piece]
        axis, done = order[stage], order[:stage]
        peer = shifted(sizes, at, axis, step)
        origin = shifted(sizes, at, axis, sizes[axis] - step)
        target = region(origin if arriving else at, done, core, piece)
        source = region(at, done, core, piece)
        if stage == 0:
            source = in_ref.at[pl.ds(*pieces[piece])]
        return remote(source, target, (send, recv), keys[piece, stage, step], peer, core)

    def pair(piece, stage, step, arriving):
        order = GATHER_ORDERS[piece]
        axis, done = order[stage], order[:stage]
        origin = shifted(sizes, at, axis, sizes[axis] - step)
        source = region(origin, done, core, piece)
        target = region(origin, done, 1 - core if arriving else core, piece)
        index = keys[piece, stage, step]
        return remote(source, target, (pair_send, pair_recv), index, at, 1 - core)

    def pair_own(arriving):
        target = out_ref.at[at[0], at[1], at[2], 1 - core if arriving else core]
        return remote(in_ref, target, (pair_send, pair_recv), len(keys), at, 1 - core)

    own = pltpu.make_async_copy(in_ref, out_ref.at[at[0], at[1], at[2], core], local)
    own.start()
    pair_own(False).start()
    for stage in range(4):
        for piece, order in enumerate(GATHER_ORDERS):
            if stage > 0:
                for step in range(1, sizes[order[stage - 1]]):
                    line(piece, stage - 1, step, True).wait_recv()
                if stage == 1 and piece == 0:
                    own.wait()
            if stage < 3:
                for step in range(1, sizes[order[stage]]):
                    line(piece, stage, step, False).start()
            if stage > 0:
                for step in range(1, sizes[order[stage - 1]]):
                    pair(piece, stage - 1, step, False).start()
    for piece, stage, step in keys:
        line(piece, stage, step, False).wait_send()
        pair(piece, stage, step, False).wait_send()
        pair(piece, stage, step, True).wait_recv()
    pair_own(False).wait_send()
    pair_own(True).wait_recv()


def gather_rows(ident, rows):
    sizes = chip_grid()
    count, width = rows.shape
    copies = line_copies(sizes)
    dma = pltpu.SemaphoreType.DMA
    gathered = pl.pallas_call(
        functools.partial(gather_kernel, sizes, count),
        out_shape=jax.ShapeDtypeStruct(sizes + (2, count, width), rows.dtype),
        in_specs=[pl.BlockSpec(memory_space=pltpu.VMEM)],
        out_specs=pl.BlockSpec(memory_space=pltpu.VMEM),
        scratch_shapes=[dma((copies,)), dma((copies,)), dma((copies + 1,)), dma((copies + 1,)), dma],
        compiler_params=pltpu.CompilerParams(collective_id=ident, has_side_effects=True),
        name="gather_rows",
    )(rows)
    return gathered.reshape(-1, width)


def scatter_kernel(sizes, rows, in_ref, out_ref, acc, arrived, *rest):
    slots, (send, recv, pair_send, pair_recv, local) = rest[:-5], rest[-5:]
    at, core = chip_place(sizes)
    greet_lines(sizes, at, core)
    pieces = row_pieces(rows)
    orders = [order[::-1] for order in GATHER_ORDERS]
    keys = {}
    for piece, order in enumerate(orders):
        for stage, axis in enumerate(order):
            for step in range(1, sizes[axis]):
                keys[piece, stage, step] = len(keys)

    def line(piece, stage, step):
        order = orders[piece]
        axis, done = order[stage], order[:stage]
        peer = shifted(sizes, at, axis, step)
        index = tuple(
            peer[a] if a == axis else at[a] if a in done else slice(None) for a in range(3)
        )
        key = keys[piece, stage, step]
        return pltpu.make_async_remote_copy(
            src_ref=acc.at[index + (pl.ds(*pieces[piece]),)],
            dst_ref=slots[3 * piece + stage].at[step - 1],
            send_sem=send.at[key],
            recv_sem=recv.at[key],
            device_id=chip_device(sizes, peer, core),
            device_id_type=pl.DeviceIdType.MESH,
        )

    loads, pairs = [], []
    for piece in range(3):
        part = pl.ds(*pieces[piece])
        pairs.append(
            pltpu.make_async_remote_copy(
                src_ref=in_ref.at[:, :, :, 1 - core, part],
                dst_ref=arrived.at[:, :, :, part],
                send_sem=pair_send.at[piece],
                recv_sem=pair_recv.at[piece],
                device_id=chip_device(sizes, at, 1 - core),
                device_id_type=pl.DeviceIdType.MESH,
            )
        )
        pairs[-1].start()
        loads.append(
            pltpu.make_async_copy(
                in_ref.at[:, :, :, core, part], acc.at[:, :, :, part], local.at[piece]
            )
        )
        loads[-1].start()

    def add(piece, stage):
        order = orders[piece]
        done = order[:stage]
        left = [axis for axis in range(3) if axis not in done]
        part = pl.ds(*pieces[piece])

        def one(index, carry):
            where, inner = list(at), []
            for axis in reversed(left):
                where[axis] = lax.rem(index, sizes[axis])
                index = index // sizes[axis]
                inner.insert(0, where[axis])
            spot = tuple(where) + (part,)
            total = acc[spot].astype(jnp.float32)
            if stage == 0:
                total = total + arrived[spot].astype(jnp.float32)
            else:
                taken = slots[3 * piece + stage - 1]
                for step in range(taken.shape[0]):
                    total = total + taken[(step,) + tuple(inner)].astype(jnp.float32)
            if stage == 3:
                out_ref[part] = total
            else:
                acc[spot] = total.astype(acc.dtype)
            return carry

        lax.fori_loop(0, math.prod(sizes[axis] for axis in left), one, 0)

    for stage in range(4):
        for piece, order in enumerate(orders):
            if stage == 0:
                loads[piece].wait()
                pairs[piece].wait_recv()
            else:
                for step in range(1, sizes[order[stage - 1]]):
                    line(piece, stage - 1, step).wait_recv()
            add(piece, stage)
            if stage < 3:
                for step in range(1, sizes[order[stage]]):
                    line(piece, stage, step).start()
    for piece in range(3):
        pairs[piece].wait_send()
    for piece, stage, step in keys:
        line(piece, stage, step).wait_send()


def scatter_rows(ident, parts):
    sizes = chip_grid()
    width = parts.shape[1]
    count = parts.shape[0] // (2 * math.prod(sizes))
    copies = line_copies(sizes)
    dma = pltpu.SemaphoreType.DMA
    slots = []
    for piece, order in enumerate(GATHER_ORDERS):
        order = order[::-1]
        for stage, axis in enumerate(order):
            left = tuple(sizes[a] for a in range(3) if a not in order[: stage + 1])
            shape = (sizes[axis] - 1,) + left + (row_pieces(count)[piece][1], width)
            slots.append(pltpu.VMEM(shape, parts.dtype))
    return pl.pallas_call(
        functools.partial(scatter_kernel, sizes, count),
        out_shape=jax.ShapeDtypeStruct((count, width), jnp.float32),
        in_specs=[pl.BlockSpec(memory_space=pl.ANY)],
        out_specs=pl.BlockSpec(memory_space=pltpu.VMEM),
        scratch_shapes=[
            pltpu.VMEM(sizes + (count, width), parts.dtype),
            pltpu.VMEM(sizes + (count, width), parts.dtype),
            *slots,
            dma((copies,)),
            dma((copies,)),
            dma((3,)),
            dma((3,)),
            dma((3,)),
        ],
        compiler_params=pltpu.CompilerParams(collective_id=ident, has_side_effects=True),
        name="scatter_rows",
    )(parts.reshape(sizes + (2, count, width)))


def totals_kernel(in_ref, out_ref, arrived, mine, send, recv, back_send, back_recv):
    group_mod, group_dp = lax.axis_size("mod"), lax.axis_size("dp")
    size = group_mod * group_dp
    place = lax.axis_index("mod") * group_dp + lax.axis_index("dp")

    def device(index):
        return {"mod": index // group_dp, "dp": lax.rem(index, group_dp)}

    barrier = pltpu.get_barrier_semaphore()

    def greet(step, carry):
        pl.semaphore_signal(
            barrier,
            inc=1,
            device_id=device(lax.rem(place + step, size)),
            device_id_type=pl.DeviceIdType.MESH,
        )
        return carry

    def ahead(step, slot):
        peer = lax.rem(place + step, size)
        return pltpu.make_async_remote_copy(
            src_ref=in_ref.at[peer],
            dst_ref=arrived.at[slot],
            send_sem=send.at[step],
            recv_sem=recv.at[step],
            device_id=device(peer),
            device_id_type=pl.DeviceIdType.MESH,
        )

    def back(step, slot):
        return pltpu.make_async_remote_copy(
            src_ref=mine,
            dst_ref=out_ref.at[slot],
            send_sem=back_send.at[step],
            recv_sem=back_recv.at[step],
            device_id=device(lax.rem(place + step, size)),
            device_id_type=pl.DeviceIdType.MESH,
        )

    def begin(copy):
        def one(step, carry):
            copy(step, place).start()
            return carry

        lax.fori_loop(1, size, one, 0)

    def finish(copy):
        def one(step, carry):
            copy(step, place).wait_send()
            copy(step, lax.rem(place + size - step, size)).wait_recv()
            return carry

        lax.fori_loop(1, size, one, 0)

    lax.fori_loop(1, size, greet, 0)
    pl.semaphore_wait(barrier, size - 1)
    begin(ahead)
    arrived[place] = in_ref[place]
    finish(ahead)
    tops = arrived[:, 0:1]
    top = jnp.max(tops, axis=0)
    total = jnp.sum(arrived[:, 1:2] * jnp.exp(tops - top[None]), axis=0)
    hit = jnp.sum(arrived[:, 2:3], axis=0)
    line = lax.broadcasted_iota(jnp.int32, mine.shape, 0)
    mine[...] = jnp.where(line == 0, top + jnp.log(total), jnp.where(line == 1, hit, 0.0))
    out_ref[place] = mine[...]
    begin(back)
    finish(back)


def totals_call(ident, stats):
    dma = pltpu.SemaphoreType.DMA((stats.shape[0],))
    return pl.pallas_call(
        totals_kernel,
        out_shape=jax.ShapeDtypeStruct(stats.shape, stats.dtype),
        in_specs=[pl.BlockSpec(memory_space=pltpu.VMEM)],
        out_specs=pl.BlockSpec(memory_space=pltpu.VMEM),
        scratch_shapes=[
            pltpu.VMEM(stats.shape, stats.dtype),
            pltpu.VMEM(stats.shape[1:], stats.dtype),
            dma,
            dma,
            dma,
            dma,
        ],
        compiler_params=pltpu.CompilerParams(collective_id=ident, has_side_effects=True),
        name="totals",
    )(stats)


def side_by_side(blocks):
    count, rows, columns = blocks.shape
    if columns % 128:
        return jnp.concatenate(list(blocks.astype(jnp.float32)), axis=1)

    def place(in_ref, out_ref):
        out_ref[...] = in_ref[0].astype(jnp.float32)

    return pl.pallas_call(
        place,
        grid=(count,),
        out_shape=jax.ShapeDtypeStruct((rows, count * columns), jnp.float32),
        in_specs=[pl.BlockSpec((1, rows, columns), lambda i: (i, 0, 0))],
        out_specs=pl.BlockSpec((rows, columns), lambda i: (0, i)),
        name="side_by_side",
    )(blocks)


HEAD_ROWS = 256


def scores_kernel(rows_ref, table_ref, wanted_ref, out_ref, logits_ref):
    logits = right_product(table_ref[...], rows_ref[...])
    logits_ref[...] = logits
    hits = lax.broadcasted_iota(jnp.int32, logits.shape, 0) == wanted_ref[...]
    top = jnp.max(logits, axis=0, keepdims=True)
    total = jnp.sum(jnp.exp(logits - top), axis=0, keepdims=True)
    hit = jnp.sum(jnp.where(hits, logits, 0.0), axis=0, keepdims=True)
    count, lines, part = out_ref.shape
    line = lax.broadcasted_iota(jnp.int32, (lines, part), 0)
    for block in range(count):
        at = slice(block * part, (block + 1) * part)
        out_ref[block] = jnp.where(
            line == 0, top[:, at], jnp.where(line == 1, total[:, at], hit[:, at])
        )


def scores_call(rows, table, wanted, part):
    step = math.gcd(HEAD_ROWS, rows.shape[0])
    return pl.pallas_call(
        scores_kernel,
        grid=(rows.shape[0] // step,),
        out_shape=[
            jax.ShapeDtypeStruct((rows.shape[0] // part, 8, part), jnp.float32),
            jax.ShapeDtypeStruct((table.shape[0], rows.shape[0]), jnp.float32),
        ],
        in_specs=[
            pl.BlockSpec((step, rows.shape[1]), lambda i: (i, 0)),
            pl.BlockSpec(table.shape, lambda i: (0, 0)),
            pl.BlockSpec((1, step), lambda i: (0, i)),
        ],
        out_specs=[
            pl.BlockSpec((step // part, 8, part), lambda i: (i, 0, 0)),
            pl.BlockSpec((table.shape[0], step), lambda i: (0, i)),
        ],
        name="scores",
    )(rows, table, wanted[None])


def norm_kernel(group_mod, group_dp, final_lines, in_ref, out_ref, gathered, send, recv, local):
    exchange_kernel([("mod", "dp")], [(0, True)], in_ref, gathered, send, recv, local)
    final = gathered[0]
    for mod in range(1, group_mod):
        final = final + gathered[mod * group_dp]
    line = lax.broadcasted_iota(jnp.int32, final.shape, 0)
    final = jnp.where(line < final_lines, final, 0.0)
    squares = jnp.sum(jnp.sum(final * final, axis=1, keepdims=True), axis=0, keepdims=True)
    total = jnp.sum(gathered[...], axis=0) + squares
    out_ref[...] = jnp.where(line < final_lines, final, total)


def norm_call(ident, last, final_lines):
    group_mod, group_dp = lax.axis_size("mod"), lax.axis_size("dp")
    size = group_mod * group_dp
    dma = pltpu.SemaphoreType.DMA
    return pl.pallas_call(
        functools.partial(norm_kernel, group_mod, group_dp, final_lines),
        out_shape=jax.ShapeDtypeStruct(last.shape, last.dtype),
        in_specs=[pl.BlockSpec(memory_space=pltpu.VMEM)],
        out_specs=pl.BlockSpec(memory_space=pltpu.VMEM),
        scratch_shapes=[
            pltpu.VMEM((size,) + last.shape, last.dtype),
            dma((size,)),
            dma((size,)),
            dma((1,)),
        ],
        compiler_params=pltpu.CompilerParams(collective_id=ident, has_side_effects=True),
        name="norm",
    )(last)


GROUP_SEQS = 4


def wide_table(table_ref, tokens, width):
    table = table_ref[...]
    table = jnp.concatenate([table] * (tokens // table.shape[0]), axis=0)
    return jnp.concatenate([table] * (width // table.shape[1]), axis=1)


def turned(values, cosine, sine):
    width = values.shape[-1]
    half = HEAD_DIM // 2
    lane = lax.broadcasted_iota(jnp.int32, values.shape, 1)
    other = jnp.where(
        lane % HEAD_DIM < half,
        pltpu.roll(values, width - half, 1),
        pltpu.roll(values, half, 1),
    )
    return values * cosine + other * sine


def head_spread(values, heads):
    rows, width = values.shape
    lane = lax.broadcasted_iota(jnp.int32, (heads, rows, width), 2)
    head = lax.broadcasted_iota(jnp.int32, (heads, rows, width), 0)
    return jnp.where(lane // HEAD_DIM == head, values[None], jnp.zeros((), values.dtype))


def head_fold(values, heads):
    rows, width = values.shape
    values = values.reshape(heads, rows // heads, width)
    lane = lax.broadcasted_iota(jnp.int32, values.shape, 2)
    head = lax.broadcasted_iota(jnp.int32, values.shape, 0)
    return jnp.sum(jnp.where(lane // HEAD_DIM == head, values, 0.0), axis=0)


def attention_parts(length, spots_ref, mixed_ref, cosine_ref, sine_ref):
    tokens, width = mixed_ref.shape[0], mixed_ref.shape[1] // 3
    heads = width // HEAD_DIM
    cosine = wide_table(cosine_ref, tokens, width)
    sine = wide_table(sine_ref, tokens, width)
    spot = spots_ref[...]
    key = lax.broadcasted_iota(jnp.int32, (spot.shape[0], tokens), 1)
    chosen = key == spot
    seen = (key <= spot) & (key >= spot - spot % length)
    queries = turned(mixed_ref[:, :width], cosine, sine).astype(jnp.bfloat16)
    queries = product(chosen.astype(jnp.bfloat16), queries)
    queries = head_spread(queries, heads).reshape(-1, width).astype(jnp.bfloat16)
    keys_in = turned(mixed_ref[:, width : 2 * width], cosine, sine).astype(jnp.bfloat16)
    values = mixed_ref[:, 2 * width :].astype(jnp.bfloat16)
    raw = right_product(queries, keys_in).reshape(heads, -1, tokens)
    scores = jnp.where(seen[None], raw * HEAD_DIM ** (-0.5), -1e30).reshape(-1, tokens)
    top = jnp.max(scores, axis=1, keepdims=True)
    terms = jnp.exp(scores - top)
    chances = terms / jnp.sum(terms, axis=1, keepdims=True)
    return chosen, queries, keys_in, values, chances, cosine, sine


def attention_kernel(
    length, spots_ref, mixed_ref, inputs_ref, cosine_ref, sine_ref, heads_ref, picked_ref
):
    heads = inputs_ref.shape[1] // HEAD_DIM
    chosen, _, _, values, chances, _, _ = attention_parts(
        length, spots_ref, mixed_ref, cosine_ref, sine_ref
    )
    spread = product(chances.astype(jnp.bfloat16), values)
    heads_ref[...] = head_fold(spread, heads).astype(jnp.bfloat16)
    picked_ref[...] = product(chosen.astype(jnp.bfloat16), inputs_ref[...])


def attention_back_kernel(
    length, spots_ref, mixed_ref, grad_ref, cosine_ref, sine_ref, out_ref
):
    width = grad_ref.shape[1]
    heads = width // HEAD_DIM
    chosen, queries, keys_in, values, chances, cosine, sine = attention_parts(
        length, spots_ref, mixed_ref, cosine_ref, sine_ref
    )
    grad_heads = head_spread(grad_ref[...].astype(jnp.float32), heads)
    grad_heads = grad_heads.reshape(-1, width).astype(jnp.bfloat16)
    grad_values = left_product(chances.astype(jnp.bfloat16), grad_heads)
    grad_chances = right_product(grad_heads, values)
    delta = jnp.sum(chances * grad_chances, axis=1, keepdims=True)
    grad_raw = (chances * (grad_chances - delta) * HEAD_DIM ** (-0.5)).astype(jnp.bfloat16)
    grad_queries = head_fold(product(grad_raw, keys_in), heads)
    grad_queries = lax.dot_general(
        chosen.astype(jnp.float32),
        grad_queries,
        (((0,), (0,)), ((), ())),
        precision=lax.Precision.HIGHEST,
        preferred_element_type=jnp.float32,
    )
    grad_keys = left_product(grad_raw, queries)
    out_ref[:, :width] = turned(grad_queries, cosine, -sine).astype(jnp.bfloat16)
    out_ref[:, width : 2 * width] = turned(grad_keys, cosine, -sine).astype(jnp.bfloat16)
    out_ref[:, 2 * width :] = grad_values.astype(jnp.bfloat16)


def attention_call(body, length, operands, tables, outs, name, microseconds):
    sequences = operands[1].shape[0] // length
    steps = sequences // math.gcd(GROUP_SEQS, sequences)

    def block(array):
        return pl.BlockSpec((array.shape[0] // steps, array.shape[1]), lambda i: (i, 0))

    fixed = [pl.BlockSpec(table.shape, lambda i: (0, 0)) for table in tables]
    return pl.pallas_call(
        functools.partial(body, length),
        grid=(steps,),
        out_shape=outs,
        in_specs=[block(array) for array in operands] + fixed,
        out_specs=[block(array) for array in outs],
        cost_estimate=pl.CostEstimate(
            flops=0, bytes_accessed=microseconds * 3_000_000, transcendentals=0
        ),
        name=name,
    )(*operands, *tables)


def square_sum(values):
    return jnp.sum(lax.optimization_barrier(jnp.sum(values * values, axis=0)))


def on_device(
    token_ids,
    targets,
    positions,
    loss_mask,
    paths,
    attend,
    output,
    widen,
    narrow,
    gains,
    table,
    final_gain,
    first_attend,
    first_output,
    first_widen,
    first_narrow,
    first_gains,
    first_table,
    first_final,
    second_attend,
    second_output,
    second_widen,
    second_narrow,
    second_gains,
    second_table,
    second_final,
):
    group_dp = lax.axis_size("dp")
    group_mod = lax.axis_size("mod")
    dp_place = lax.axis_index("dp")
    mod_place = lax.axis_index("mod")
    everyone = ("mod", "dp")
    place = mod_place * group_dp + dp_place
    sources = group_mod * group_dp
    micro, per_mod, length = token_ids.shape
    spots_seq = positions.shape[2]
    seq_dev = per_mod // group_dp
    shard_rows, width = table.shape
    heads = width // HEAD_DIM
    slots = micro * sources
    slots_local = slots // group_dp
    low = jnp.bfloat16

    mixing = lax.all_gather(
        jnp.concatenate([attend[0], output[0]], axis=1).astype(low), "dp", axis=0, tiled=True
    )
    attend_low, output_low = mixing[:, : 3 * width], mixing[:, 3 * width :]
    hidden = narrow.shape[1]
    widen_low = jnp.stack(
        [widen[0, :, i * hidden : (i + 1) * hidden].astype(low) for i in range(group_dp)]
    )
    widen_low = lax.all_to_all(widen_low, "dp", split_axis=0, concat_axis=0, tiled=True)
    widen_low = widen_low.reshape(width, hidden)
    narrow_low = narrow[0].astype(low)
    table_low = table.astype(low)

    fields = jnp.concatenate(
        [token_ids, positions, targets, loss_mask, paths[..., None]], axis=-1
    )
    fields, gain_parts, final_parts = exchange(
        0,
        (("mod",), fields.reshape(micro * per_mod, -1), True),
        (("dp",), jnp.broadcast_to(gains.astype(low), (16, gains.shape[1])), True),
        (("mod",), jnp.broadcast_to(final_gain.astype(low)[None], (16, final_gain.shape[0])), True),
    )
    own_gains = gain_parts[:, 0].reshape(-1).astype(jnp.float32)
    gain_one, gain_two = own_gains[:width], own_gains[width:]
    gain_final = final_parts[:, 0].reshape(-1).astype(jnp.float32)
    fields = fields.reshape(group_mod, micro, per_mod, -1).transpose(1, 0, 2, 3)
    fields = fields.reshape(slots, seq_dev, -1)
    own = lax.dynamic_slice_in_dim(fields, dp_place * slots_local, slots_local)
    own_match = own[..., -1] == mod_place
    own = jnp.sum(jnp.where(own_match[..., None], own[..., : length + spots_seq], 0), axis=1)
    own_tokens = own[:, :length].reshape(-1)
    spots = own[:, length:]
    held = jnp.repeat(jnp.any(own_match, axis=1), length)
    match = fields[None, ..., -1] == jnp.arange(group_mod, dtype=jnp.int32)[:, None, None]
    scoring = jnp.sum(
        jnp.where(match[..., None], fields[None, ..., length + spots_seq : -1], 0), axis=2
    )
    wanted = scoring[..., :spots_seq].reshape(-1)
    counted = scoring[..., spots_seq:].reshape(-1).astype(jnp.float32)
    count_total = jnp.sum(counted)

    shard = own_tokens // shard_rows
    row = own_tokens % shard_rows
    key = jnp.where(held, own_tokens, -1)
    order = jnp.arange(key.shape[0], dtype=jnp.int32)
    repeated = jnp.any((key[:, None] == key[None, :]) & (order[None, :] < order[:, None]), axis=1)
    leading = held & ~repeated
    rank = jnp.sum(
        (
            leading[None, :] & (shard[None, :] == shard[:, None]) & (key[None, :] < key[:, None])
        ).astype(jnp.int32),
        axis=1,
    )
    expected = -(-slots_local * length // sources)
    cap = -(-3 * expected // 16) * 8
    cap = min(max(cap, 16), -(-shard_rows // 8) * 8, 112)
    own_rounds = jnp.max(jnp.where(leading, rank // cap, 0)) + 1

    def ask(turn):
        slot = rank - turn * cap
        inside = held & (slot >= 0) & (slot < cap)
        slot = jnp.where(inside, shard * cap + slot, -1)
        asked = jnp.sum(
            jnp.where(
                leading[None, :]
                & (slot[None, :] == jnp.arange(sources * cap, dtype=jnp.int32)[:, None]),
                row[None, :] + 1,
                0,
            ),
            axis=1,
        ).reshape(sources, cap)
        return slot, asked

    slot, asked = ask(0)
    message = jnp.concatenate(
        [asked, jnp.broadcast_to(own_rounds, (sources, 128 - cap))], axis=1
    )
    message = exchange(
        1, (everyone, jnp.broadcast_to(message[:, None], (sources, 8, 128)), False)
    )
    rounds = jnp.max(message[:, 0, cap])
    spread = one_hot(slot, sources * cap)
    pick = one_hot(message[:, 0, :cap].reshape(-1) - 1, shard_rows)

    def other_plan(turn):
        slot, asked = ask(turn)
        asked = lax.all_to_all(asked, everyone, split_axis=0, concat_axis=0, tiled=True)
        return one_hot(slot, sources * cap), one_hot(asked.reshape(-1) - 1, shard_rows)

    def other_rows(state):
        turn, rows = state
        spread, pick = other_plan(turn)
        sent = product(pick, table_low).astype(low).reshape(sources, cap, width)
        got = lax.all_to_all(sent, everyone, split_axis=0, concat_axis=0, tiled=True)
        return turn + 1, rows + product(spread, got.reshape(-1, width)).astype(low)

    sent = product(pick, table_low).astype(low).reshape(sources, cap, width)
    got = exchange(2, (everyone, sent, False))
    inputs = product(spread, got.reshape(-1, width)).astype(low)
    inputs = lax.while_loop(
        lambda state: state[0] < rounds, other_rows, (jnp.int32(1), inputs)
    )[1]

    group = math.gcd(GROUP_SEQS, slots_local)
    tables = rotary_tables(length)
    flat_spots = spots + (jnp.arange(slots_local, dtype=jnp.int32) % group)[:, None] * length
    flat_spots = flat_spots.reshape(-1, 1)
    inputs_wide = inputs.astype(jnp.float32)
    normed_one = rms_scale(inputs_wide, gain_one).astype(low)
    mixed = product(normed_one, attend_low)
    picked_rows = slots_local * spots_seq
    heads_out, picked_inputs = attention_call(
        attention_kernel,
        length,
        (flat_spots, mixed, inputs),
        tables,
        [
            jax.ShapeDtypeStruct((picked_rows, width), low),
            jax.ShapeDtypeStruct((picked_rows, width), jnp.float32),
        ],
        "attention",
        7,
    )
    middle = picked_inputs + product(heads_out, output_low)

    def sum_parts(ident, parts):
        parts = parts.astype(low).reshape(group_dp, picked_rows, width)
        return jnp.sum(exchange(ident, (("dp",), parts, False)).astype(jnp.float32), axis=0)

    normed_two = rms_scale(middle, gain_two).astype(low)
    normed_all = exchange(3, (("dp",), normed_two, True)).reshape(-1, width)
    upper = product(normed_all, widen_low)
    gelu = lambda value: jax.nn.gelu(value, approximate=True)
    activated = gelu(upper).astype(low)
    lifted = sum_parts(4, product(activated, narrow_low))
    returned = (middle + lifted).astype(low).astype(jnp.float32)

    final, final_back = jax.vjp(rms_scale, returned, gain_final)
    scored = gather_rows(12, final.astype(low))
    target_row = wanted - place * shard_rows
    stats, logits = scores_call(scored, table_low, target_row, picked_rows)
    totals = totals_call(5, stats)
    log_total = totals[:, 0].reshape(-1)
    loss_total = jnp.sum(counted * (log_total - totals[:, 1].reshape(-1)))
    hits = target_row[None, :] == jnp.arange(shard_rows, dtype=jnp.int32)[:, None]
    grad_logits = (
        counted[None] * (jnp.exp(logits - log_total[None]) - hits.astype(jnp.float32))
    ).astype(low)
    grad_picked = scatter_rows(13, left_product(grad_logits, table_low).astype(low))

    grad_returned, grad_final = final_back(grad_picked)
    incoming = grad_returned.astype(low)
    incoming_all = exchange(7, (("dp",), incoming, True)).reshape(-1, width)
    grad_narrow = left_product(activated, incoming_all)
    grad_act = right_product(incoming_all, narrow_low)
    grad_upper = jax.vjp(gelu, upper)[1](grad_act)[0].astype(low)
    grad_widen = left_product(normed_all, grad_upper).astype(low)
    grad_widen = lax.all_to_all(
        grad_widen.reshape(group_dp, -1, hidden), "dp", split_axis=0, concat_axis=0, tiled=True
    )
    grad_normed_two = sum_parts(8, right_product(grad_upper, widen_low))
    grad_middle, grad_gain_two = jax.vjp(rms_scale, middle, gain_two)[1](grad_normed_two)
    grad_middle = grad_middle + incoming.astype(jnp.float32)

    branch_grad = grad_middle.astype(low)
    grad_output = lax.psum_scatter(
        left_product(heads_out, branch_grad).astype(low), "dp", scatter_dimension=0, tiled=True
    ).astype(jnp.float32)
    grad_heads = right_product(branch_grad, output_low).astype(low)
    (grad_mixed,) = attention_call(
        attention_back_kernel,
        length,
        (flat_spots, mixed, grad_heads),
        tables,
        [jax.ShapeDtypeStruct(mixed.shape, low)],
        "attention_back",
        12,
    )
    grad_widen, grad_mixed = lax.optimization_barrier((grad_widen, grad_mixed))
    grad_attend = left_product(normed_one, grad_mixed)
    grad_normed = right_product(grad_mixed, attend_low)
    grad_inputs, grad_gain_one = jax.vjp(rms_scale, inputs_wide, gain_one)[1](grad_normed)
    here = spots[:, :, None] == jnp.arange(length, dtype=jnp.int32)
    grad_skip = jnp.sum(
        jnp.where(
            here[..., None], grad_middle.reshape(slots_local, spots_seq, 1, width), 0.0
        ),
        axis=1,
    ).reshape(-1, width)
    leaving = (grad_skip + grad_inputs).astype(low)

    grad_attend = lax.psum_scatter(
        grad_attend.astype(low), "dp", scatter_dimension=0, tiled=True
    ).astype(jnp.float32)

    def other_grads(state):
        turn, total = state
        spread, pick = other_plan(turn)
        sent = left_product(spread, leaving).astype(low).reshape(sources, cap, width)
        got = lax.all_to_all(sent, everyone, split_axis=0, concat_axis=0, tiled=True)
        return turn + 1, total + left_product(pick, got.reshape(-1, width))

    given = left_product(spread, leaving).astype(low).reshape(sources, cap, width)
    gain_grads = jnp.concatenate([grad_gain_one, grad_gain_two, grad_final])
    gain_grads = jnp.pad(gain_grads.reshape(-1, 128), ((0, -gain_grads.shape[0] // 128 % 8), (0, 0)))
    given, gain_grads = exchange(
        9, (everyone, given, False), (("dp",), gain_grads, True)
    )
    given, scored = lax.optimization_barrier((given, scored))
    table_grad = product(grad_logits, scored)
    table_grad = table_grad + left_product(pick, given.reshape(-1, width))
    table_grad = lax.while_loop(
        lambda state: state[0] < rounds, other_grads, (jnp.int32(1), table_grad)
    )[1]
    gain_grads = jnp.sum(gain_grads, axis=0).reshape(-1)
    own_gain_grads = gain_grads[: 2 * width]
    final_rows = gain_grads[2 * width : 3 * width].reshape(-1, 128)
    gain_part = gains.shape[1]
    grad_gains = lax.dynamic_slice_in_dim(own_gain_grads, dp_place * gain_part, gain_part)
    widen_squares = square_sum(grad_widen.astype(jnp.float32).reshape(-1, hidden))
    grad_widen = side_by_side(grad_widen)
    matrix_grads = (grad_attend[None], grad_output[None], grad_widen[None], grad_narrow[None])
    squares = sum(square_sum(g) for g in (grad_attend, grad_output, grad_narrow, table_grad))
    squares = squares + widen_squares
    squares = squares + jnp.sum(grad_gains * grad_gains)
    last = jnp.concatenate(
        [final_rows, jnp.broadcast_to(squares, (16 - final_rows.shape[0] % 8 - 8, 128))], axis=0
    )
    final_count = final_rows.shape[0]
    last = norm_call(11, last, final_count)
    grad_final = last[:final_count].reshape(-1)
    squares = last[final_count, 0]
    final_part = final_gain.shape[0]
    grad_final = lax.dynamic_slice_in_dim(grad_final, mod_place * final_part, final_part)
    gradient_norm = jnp.sqrt(squares) / count_total
    factor = CLIP_LIMIT / jnp.maximum(gradient_norm, CLIP_LIMIT) / count_total
    params = (attend, output, widen, narrow, gains, table, final_gain)
    grads = matrix_grads + (grad_gains[None], table_grad, grad_final)
    firsts = (
        first_attend,
        first_output,
        first_widen,
        first_narrow,
        first_gains,
        first_table,
        first_final,
    )
    seconds = (
        second_attend,
        second_output,
        second_widen,
        second_narrow,
        second_gains,
        second_table,
        second_final,
    )
    rates = (RATE_MATRIX, RATE_MATRIX, RATE_MATRIX, RATE_MATRIX, RATE_GAIN, RATE_MATRIX, RATE_GAIN)
    decays = (DECAY_MATRIX, DECAY_MATRIX, DECAY_MATRIX, DECAY_MATRIX, 0.0, DECAY_MATRIX, 0.0)
    updated = [
        adam_step(w, g * factor, f, s, r, c)
        for w, g, f, s, r, c in zip(params, grads, firsts, seconds, rates, decays)
    ]
    return (
        loss_total / count_total,
        gradient_norm,
        *(entry[0] for entry in updated),
        *(entry[1] for entry in updated),
        *(entry[2] for entry in updated),
    )


def solution(mesh):
    placed = (
        P(None, "mod", None),
        P(None, "mod", None),
        P(None, "mod", None),
        P(None, "mod", None),
        P(None, "mod"),
        P("mod", "dp", None),
        P("mod", "dp", None),
        P("mod", "dp", None),
        P("mod", "dp", None),
        P("mod", "dp"),
        P(("mod", "dp"), None),
        P("mod"),
        P("mod", "dp", None),
        P("mod", "dp", None),
        P("mod", "dp", None),
        P("mod", "dp", None),
        P("mod", "dp"),
        P(("mod", "dp"), None),
        P("mod"),
        P("mod", "dp", None),
        P("mod", "dp", None),
        P("mod", "dp", None),
        P("mod", "dp", None),
        P("mod", "dp"),
        P(("mod", "dp"), None),
        P("mod"),
    )
    return jax.shard_map(
        on_device,
        mesh=mesh,
        in_specs=placed,
        out_specs=(
            P(),
            P(),
            P("mod", "dp", None),
            P("mod", "dp", None),
            P("mod", "dp", None),
            P("mod", "dp", None),
            P("mod", "dp"),
            P(("mod", "dp"), None),
            P("mod"),
            P("mod", "dp", None),
            P("mod", "dp", None),
            P("mod", "dp", None),
            P("mod", "dp", None),
            P("mod", "dp"),
            P(("mod", "dp"), None),
            P("mod"),
            P("mod", "dp", None),
            P("mod", "dp", None),
            P("mod", "dp", None),
            P("mod", "dp", None),
            P("mod", "dp"),
            P(("mod", "dp"), None),
            P("mod"),
        ),
        check_vma=False,
    )
```

```python
import functools
import math

import jax
import jax.numpy as jnp
import numpy as np
from jax import lax
from jax.experimental import pallas as pl
from jax.experimental.pallas import tpu as pltpu
from jax.sharding import PartitionSpec as P

HEAD_DIM = 64


NORM_EPS = 1e-05
CLIP_LIMIT = 0.05
BETA_ONE = 0.5
BETA_TWO = 0.5
ADAM_STEP = 10.0
ADAM_EPS = 1e-08
RATE_MATRIX = 0.03
RATE_GAIN = 0.3
DECAY_MATRIX = 0.1


def rms_scale(values, gain):
    return values * lax.rsqrt(jnp.mean(values * values, axis=-1, keepdims=True) + NORM_EPS) * gain


def rotary_tables(length):
    half = HEAD_DIM // 2
    inverse = 10000.0 ** (-np.arange(half, dtype=np.float32) / half)
    angle = np.arange(length, dtype=np.float32)[:, None] * inverse[None, :]
    cosine, sine = np.cos(angle), np.sin(angle)
    cosine = np.concatenate([cosine] * 4, axis=1).astype(np.float32)
    sine = np.concatenate([-sine, sine] * 2, axis=1).astype(np.float32)
    return jnp.asarray(cosine), jnp.asarray(sine)


def product(left, right):
    return jnp.dot(left, right, preferred_element_type=jnp.float32)


def left_product(left, right):
    return lax.dot_general(
        left, right, (((0,), (0,)), ((), ())), preferred_element_type=jnp.float32
    )


def right_product(left, right):
    return lax.dot_general(
        left, right, (((1,), (1,)), ((), ())), preferred_element_type=jnp.float32
    )


def adam_step(weight, grad, first, second, rate, decay):
    mean = BETA_ONE * first + (1.0 - BETA_ONE) * grad
    square = BETA_TWO * second + (1.0 - BETA_TWO) * grad * grad
    mean_hat = mean / (1.0 - BETA_ONE**ADAM_STEP)
    square_hat = square / (1.0 - BETA_TWO**ADAM_STEP)
    return (
        weight - rate * (mean_hat / (jnp.sqrt(square_hat) + ADAM_EPS) + decay * weight),
        mean,
        square,
    )


def one_hot(index, extent):
    return (index[..., None] == jnp.arange(extent, dtype=jnp.int32)).astype(jnp.bfloat16)


def exchange_kernel(groups, plan, *refs):
    count = len(plan)
    ins, outs = refs[:count], refs[count : 2 * count]
    sends, recvs = refs[2 * count : 3 * count], refs[3 * count : 4 * count]
    local = refs[4 * count]
    sizes = [math.prod(lax.axis_size(axis) for axis in axes) for axes in groups]
    places = []
    for axes in groups:
        place = lax.axis_index(axes[0])
        for axis in axes[1:]:
            place = place * lax.axis_size(axis) + lax.axis_index(axis)
        places.append(place)

    def device(group, index):
        axes = groups[group]
        if len(axes) == 1:
            return {axes[0]: index}
        inner = lax.axis_size(axes[1])
        return {axes[0]: index // inner, axes[1]: lax.rem(index, inner)}

    barrier = pltpu.get_barrier_semaphore()
    for group, size in enumerate(sizes):

        def greet(step, carry, group=group, size=size):
            peer = lax.rem(places[group] + step, size)
            pl.semaphore_signal(
                barrier,
                inc=1,
                device_id=device(group, peer),
                device_id_type=pl.DeviceIdType.MESH,
            )
            return carry

        lax.fori_loop(1, size, greet, 0)
    pl.semaphore_wait(barrier, sum(sizes) - len(sizes))

    def copy(item, step, arriving):
        group, shared = plan[item]
        size, place = sizes[group], places[group]
        peer = lax.rem(place + step, size)
        source = ins[item] if shared else ins[item].at[peer]
        slot = lax.rem(place + size - step, size) if arriving else place
        return pltpu.make_async_remote_copy(
            src_ref=source,
            dst_ref=outs[item].at[slot],
            send_sem=sends[item].at[step],
            recv_sem=recvs[item].at[step],
            device_id=device(group, peer),
            device_id_type=pl.DeviceIdType.MESH,
        )

    for item in range(count):

        def begin(step, carry, item=item):
            copy(item, step, False).start()
            return carry

        lax.fori_loop(1, sizes[plan[item][0]], begin, 0)
    own = []
    for item in range(count):
        group, shared = plan[item]
        source = ins[item] if shared else ins[item].at[places[group]]
        own.append(
            pltpu.make_async_copy(source, outs[item].at[places[group]], local.at[item])
        )
        own[-1].start()
    for item in range(count):
        own[item].wait()

        def finish(step, carry, item=item):
            copy(item, step, False).wait_send()
            copy(item, step, True).wait_recv()
            return carry

        lax.fori_loop(1, sizes[plan[item][0]], finish, 0)


def exchange(ident, *items):
    groups, plan, shapes, scratch = [], [], [], []
    for axes, array, shared in items:
        if axes not in groups:
            groups.append(axes)
        plan.append((groups.index(axes), shared))
        size = math.prod(lax.axis_size(axis) for axis in axes)
        shape = (size,) + array.shape if shared else array.shape
        shapes.append(jax.ShapeDtypeStruct(shape, array.dtype))
        scratch.append(pltpu.SemaphoreType.DMA((size,)))
    result = pl.pallas_call(
        functools.partial(exchange_kernel, groups, plan),
        out_shape=shapes,
        in_specs=[pl.BlockSpec(memory_space=pltpu.VMEM)] * len(items),
        out_specs=[pl.BlockSpec(memory_space=pltpu.VMEM)] * len(items),
        scratch_shapes=scratch + scratch + [pltpu.SemaphoreType.DMA((len(items),))],
        compiler_params=pltpu.CompilerParams(collective_id=ident, has_side_effects=True),
        name="exchange_%d" % ident,
    )(*(array for _, array, _ in items))
    return result[0] if len(items) == 1 else result


GATHER_ORDERS = ((0, 1, 2), (2, 0, 1), (1, 2, 0))


def chip_grid():
    group_mod, group_dp = lax.axis_size("mod"), lax.axis_size("dp")
    deep = math.gcd(group_mod, 4)
    return deep, group_mod // deep, group_dp // 2


def row_pieces(rows):
    part = rows // 64 * 16
    return (0, rows - 2 * part), (rows - 2 * part, part), (rows - part, part)


def chip_place(sizes):
    mod, dp = lax.axis_index("mod"), lax.axis_index("dp")
    return [mod // sizes[1], lax.rem(mod, sizes[1]), dp // 2], lax.rem(dp, 2)


def chip_device(sizes, at, core):
    return {"mod": at[0] * sizes[1] + at[1], "dp": at[2] * 2 + core}


def shifted(sizes, at, axis, step):
    at = list(at)
    at[axis] = lax.rem(at[axis] + step, sizes[axis])
    return at


def greet_lines(sizes, at, core):
    barrier = pltpu.get_barrier_semaphore()
    targets = [chip_device(sizes, at, 1 - core)]
    for axis in range(3):
        for step in range(1, sizes[axis]):
            targets.append(chip_device(sizes, shifted(sizes, at, axis, step), core))
    for target in targets:
        pl.semaphore_signal(
            barrier, inc=1, device_id=target, device_id_type=pl.DeviceIdType.MESH
        )
    pl.semaphore_wait(barrier, len(targets))


def line_copies(sizes):
    return sum(len(GATHER_ORDERS) * (size - 1) for size in sizes)


def gather_kernel(sizes, rows, in_ref, out_ref, send, recv, pair_send, pair_recv, local):
    at, core = chip_place(sizes)
    greet_lines(sizes, at, core)
    pieces = row_pieces(rows)
    keys = {}
    for piece, order in enumerate(GATHER_ORDERS):
        for stage, axis in enumerate(order):
            for step in range(1, sizes[axis]):
                keys[piece, stage, step] = len(keys)

    def region(at, done, core, piece):
        start, count = pieces[piece]
        index = tuple(slice(None) if axis in done else at[axis] for axis in range(3))
        return out_ref.at[index + (core, pl.ds(start, count))]

    def remote(source, target, sems, index, at, core):
        return pltpu.make_async_remote_copy(
            src_ref=source,
            dst_ref=target,
            send_sem=sems[0].at[index],
            recv_sem=sems[1].at[index],
            device_id=chip_device(sizes, at, core),
            device_id_type=pl.DeviceIdType.MESH,
        )

    def line(piece, stage, step, arriving):
        order = GATHER_ORDERS[piece]
        axis, done = order[stage], order[:stage]
        peer = shifted(sizes, at, axis, step)
        origin = shifted(sizes, at, axis, sizes[axis] - step)
        target = region(origin if arriving else at, done, core, piece)
        source = region(at, done, core, piece)
        if stage == 0:
            source = in_ref.at[pl.ds(*pieces[piece])]
        return remote(source, target, (send, recv), keys[piece, stage, step], peer, core)

    def pair(piece, stage, step, arriving):
        order = GATHER_ORDERS[piece]
        axis, done = order[stage], order[:stage]
        origin = shifted(sizes, at, axis, sizes[axis] - step)
        source = region(origin, done, core, piece)
        target = region(origin, done, 1 - core if arriving else core, piece)
        index = keys[piece, stage, step]
        return remote(source, target, (pair_send, pair_recv), index, at, 1 - core)

    def pair_own(arriving):
        target = out_ref.at[at[0], at[1], at[2], 1 - core if arriving else core]
        return remote(in_ref, target, (pair_send, pair_recv), len(keys), at, 1 - core)

    own = pltpu.make_async_copy(in_ref, out_ref.at[at[0], at[1], at[2], core], local)
    own.start()
    pair_own(False).start()
    for stage in range(4):
        for piece, order in enumerate(GATHER_ORDERS):
            if stage > 0:
                for step in range(1, sizes[order[stage - 1]]):
                    line(piece, stage - 1, step, True).wait_recv()
                if stage == 1 and piece == 0:
                    own.wait()
            if stage < 3:
                for step in range(1, sizes[order[stage]]):
                    line(piece, stage, step, False).start()
            if stage > 0:
                for step in range(1, sizes[order[stage - 1]]):
                    pair(piece, stage - 1, step, False).start()
    for piece, stage, step in keys:
        line(piece, stage, step, False).wait_send()
        pair(piece, stage, step, False).wait_send()
        pair(piece, stage, step, True).wait_recv()
    pair_own(False).wait_send()
    pair_own(True).wait_recv()


def gather_rows(ident, rows):
    sizes = chip_grid()
    count, width = rows.shape
    copies = line_copies(sizes)
    dma = pltpu.SemaphoreType.DMA
    gathered = pl.pallas_call(
        functools.partial(gather_kernel, sizes, count),
        out_shape=jax.ShapeDtypeStruct(sizes + (2, count, width), rows.dtype),
        in_specs=[pl.BlockSpec(memory_space=pltpu.VMEM)],
        out_specs=pl.BlockSpec(memory_space=pltpu.VMEM),
        scratch_shapes=[dma((copies,)), dma((copies,)), dma((copies + 1,)), dma((copies + 1,)), dma],
        compiler_params=pltpu.CompilerParams(collective_id=ident, has_side_effects=True),
        name="gather_rows",
    )(rows)
    return gathered.reshape(-1, width)


def scatter_kernel(sizes, rows, in_ref, out_ref, acc, arrived, *rest):
    slots, (send, recv, pair_send, pair_recv, local) = rest[:-5], rest[-5:]
    at, core = chip_place(sizes)
    greet_lines(sizes, at, core)
    pieces = row_pieces(rows)
    orders = [order[::-1] for order in GATHER_ORDERS]
    keys = {}
    for piece, order in enumerate(orders):
        for stage, axis in enumerate(order):
            for step in range(1, sizes[axis]):
                keys[piece, stage, step] = len(keys)

    def line(piece, stage, step):
        order = orders[piece]
        axis, done = order[stage], order[:stage]
        peer = shifted(sizes, at, axis, step)
        index = tuple(
            peer[a] if a == axis else at[a] if a in done else slice(None) for a in range(3)
        )
        key = keys[piece, stage, step]
        return pltpu.make_async_remote_copy(
            src_ref=acc.at[index + (pl.ds(*pieces[piece]),)],
            dst_ref=slots[3 * piece + stage].at[step - 1],
            send_sem=send.at[key],
            recv_sem=recv.at[key],
            device_id=chip_device(sizes, peer, core),
            device_id_type=pl.DeviceIdType.MESH,
        )

    loads, pairs = [], []
    for piece in range(3):
        part = pl.ds(*pieces[piece])
        pairs.append(
            pltpu.make_async_remote_copy(
                src_ref=in_ref.at[:, :, :, 1 - core, part],
                dst_ref=arrived.at[:, :, :, part],
                send_sem=pair_send.at[piece],
                recv_sem=pair_recv.at[piece],
                device_id=chip_device(sizes, at, 1 - core),
                device_id_type=pl.DeviceIdType.MESH,
            )
        )
        pairs[-1].start()
        loads.append(
            pltpu.make_async_copy(
                in_ref.at[:, :, :, core, part], acc.at[:, :, :, part], local.at[piece]
            )
        )
        loads[-1].start()

    def add(piece, stage):
        order = orders[piece]
        done = order[:stage]
        left = [axis for axis in range(3) if axis not in done]
        part = pl.ds(*pieces[piece])

        def one(index, carry):
            where, inner = list(at), []
            for axis in reversed(left):
                where[axis] = lax.rem(index, sizes[axis])
                index = index // sizes[axis]
                inner.insert(0, where[axis])
            spot = tuple(where) + (part,)
            total = acc[spot].astype(jnp.float32)
            if stage == 0:
                total = total + arrived[spot].astype(jnp.float32)
            else:
                taken = slots[3 * piece + stage - 1]
                for step in range(taken.shape[0]):
                    total = total + taken[(step,) + tuple(inner)].astype(jnp.float32)
            if stage == 3:
                out_ref[part] = total
            else:
                acc[spot] = total.astype(acc.dtype)
            return carry

        lax.fori_loop(0, math.prod(sizes[axis] for axis in left), one, 0)

    for stage in range(4):
        for piece, order in enumerate(orders):
            if stage == 0:
                loads[piece].wait()
                pairs[piece].wait_recv()
            else:
                for step in range(1, sizes[order[stage - 1]]):
                    line(piece, stage - 1, step).wait_recv()
            add(piece, stage)
            if stage < 3:
                for step in range(1, sizes[order[stage]]):
                    line(piece, stage, step).start()
    for piece in range(3):
        pairs[piece].wait_send()
    for piece, stage, step in keys:
        line(piece, stage, step).wait_send()


def scatter_rows(ident, parts):
    sizes = chip_grid()
    width = parts.shape[1]
    count = parts.shape[0] // (2 * math.prod(sizes))
    copies = line_copies(sizes)
    dma = pltpu.SemaphoreType.DMA
    slots = []
    for piece, order in enumerate(GATHER_ORDERS):
        order = order[::-1]
        for stage, axis in enumerate(order):
            left = tuple(sizes[a] for a in range(3) if a not in order[: stage + 1])
            shape = (sizes[axis] - 1,) + left + (row_pieces(count)[piece][1], width)
            slots.append(pltpu.VMEM(shape, parts.dtype))
    return pl.pallas_call(
        functools.partial(scatter_kernel, sizes, count),
        out_shape=jax.ShapeDtypeStruct((count, width), jnp.float32),
        in_specs=[pl.BlockSpec(memory_space=pl.ANY)],
        out_specs=pl.BlockSpec(memory_space=pltpu.VMEM),
        scratch_shapes=[
            pltpu.VMEM(sizes + (count, width), parts.dtype),
            pltpu.VMEM(sizes + (count, width), parts.dtype),
            *slots,
            dma((copies,)),
            dma((copies,)),
            dma((3,)),
            dma((3,)),
            dma((3,)),
        ],
        compiler_params=pltpu.CompilerParams(collective_id=ident, has_side_effects=True),
        name="scatter_rows",
    )(parts.reshape(sizes + (2, count, width)))


def totals_kernel(in_ref, out_ref, arrived, mine, send, recv, back_send, back_recv):
    group_mod, group_dp = lax.axis_size("mod"), lax.axis_size("dp")
    size = group_mod * group_dp
    place = lax.axis_index("mod") * group_dp + lax.axis_index("dp")

    def device(index):
        return {"mod": index // group_dp, "dp": lax.rem(index, group_dp)}

    barrier = pltpu.get_barrier_semaphore()

    def greet(step, carry):
        pl.semaphore_signal(
            barrier,
            inc=1,
            device_id=device(lax.rem(place + step, size)),
            device_id_type=pl.DeviceIdType.MESH,
        )
        return carry

    def ahead(step, slot):
        peer = lax.rem(place + step, size)
        return pltpu.make_async_remote_copy(
            src_ref=in_ref.at[peer],
            dst_ref=arrived.at[slot],
            send_sem=send.at[step],
            recv_sem=recv.at[step],
            device_id=device(peer),
            device_id_type=pl.DeviceIdType.MESH,
        )

    def back(step, slot):
        return pltpu.make_async_remote_copy(
            src_ref=mine,
            dst_ref=out_ref.at[slot],
            send_sem=back_send.at[step],
            recv_sem=back_recv.at[step],
            device_id=device(lax.rem(place + step, size)),
            device_id_type=pl.DeviceIdType.MESH,
        )

    def begin(copy):
        def one(step, carry):
            copy(step, place).start()
            return carry

        lax.fori_loop(1, size, one, 0)

    def finish(copy):
        def one(step, carry):
            copy(step, place).wait_send()
            copy(step, lax.rem(place + size - step, size)).wait_recv()
            return carry

        lax.fori_loop(1, size, one, 0)

    lax.fori_loop(1, size, greet, 0)
    pl.semaphore_wait(barrier, size - 1)
    begin(ahead)
    arrived[place] = in_ref[place]
    finish(ahead)
    tops = arrived[:, 0:1]
    top = jnp.max(tops, axis=0)
    total = jnp.sum(arrived[:, 1:2] * jnp.exp(tops - top[None]), axis=0)
    hit = jnp.sum(arrived[:, 2:3], axis=0)
    line = lax.broadcasted_iota(jnp.int32, mine.shape, 0)
    mine[...] = jnp.where(line == 0, top + jnp.log(total), jnp.where(line == 1, hit, 0.0))
    out_ref[place] = mine[...]
    begin(back)
    finish(back)


def totals_call(ident, stats):
    dma = pltpu.SemaphoreType.DMA((stats.shape[0],))
    return pl.pallas_call(
        totals_kernel,
        out_shape=jax.ShapeDtypeStruct(stats.shape, stats.dtype),
        in_specs=[pl.BlockSpec(memory_space=pltpu.VMEM)],
        out_specs=pl.BlockSpec(memory_space=pltpu.VMEM),
        scratch_shapes=[
            pltpu.VMEM(stats.shape, stats.dtype),
            pltpu.VMEM(stats.shape[1:], stats.dtype),
            dma,
            dma,
            dma,
            dma,
        ],
        compiler_params=pltpu.CompilerParams(collective_id=ident, has_side_effects=True),
        name="totals",
    )(stats)


def side_by_side(blocks):
    count, rows, columns = blocks.shape
    if columns % 128:
        return jnp.concatenate(list(blocks.astype(jnp.float32)), axis=1)

    def place(in_ref, out_ref):
        out_ref[...] = in_ref[0].astype(jnp.float32)

    return pl.pallas_call(
        place,
        grid=(count,),
        out_shape=jax.ShapeDtypeStruct((rows, count * columns), jnp.float32),
        in_specs=[pl.BlockSpec((1, rows, columns), lambda i: (i, 0, 0))],
        out_specs=pl.BlockSpec((rows, columns), lambda i: (0, i)),
        name="side_by_side",
    )(blocks)


HEAD_ROWS = 256


def scores_kernel(rows_ref, table_ref, wanted_ref, out_ref, logits_ref):
    logits = right_product(table_ref[...], rows_ref[...])
    logits_ref[...] = logits
    hits = lax.broadcasted_iota(jnp.int32, logits.shape, 0) == wanted_ref[...]
    top = jnp.max(logits, axis=0, keepdims=True)
    total = jnp.sum(jnp.exp(logits - top), axis=0, keepdims=True)
    hit = jnp.sum(jnp.where(hits, logits, 0.0), axis=0, keepdims=True)
    count, lines, part = out_ref.shape
    line = lax.broadcasted_iota(jnp.int32, (lines, part), 0)
    for block in range(count):
        at = slice(block * part, (block + 1) * part)
        out_ref[block] = jnp.where(
            line == 0, top[:, at], jnp.where(line == 1, total[:, at], hit[:, at])
        )


def scores_call(rows, table, wanted, part):
    step = math.gcd(HEAD_ROWS, rows.shape[0])
    return pl.pallas_call(
        scores_kernel,
        grid=(rows.shape[0] // step,),
        out_shape=[
            jax.ShapeDtypeStruct((rows.shape[0] // part, 8, part), jnp.float32),
            jax.ShapeDtypeStruct((table.shape[0], rows.shape[0]), jnp.float32),
        ],
        in_specs=[
            pl.BlockSpec((step, rows.shape[1]), lambda i: (i, 0)),
            pl.BlockSpec(table.shape, lambda i: (0, 0)),
            pl.BlockSpec((1, step), lambda i: (0, i)),
        ],
        out_specs=[
            pl.BlockSpec((step // part, 8, part), lambda i: (i, 0, 0)),
            pl.BlockSpec((table.shape[0], step), lambda i: (0, i)),
        ],
        name="scores",
    )(rows, table, wanted[None])


def norm_kernel(group_mod, group_dp, final_lines, in_ref, out_ref, gathered, send, recv, local):
    exchange_kernel([("mod", "dp")], [(0, True)], in_ref, gathered, send, recv, local)
    final = gathered[0]
    for mod in range(1, group_mod):
        final = final + gathered[mod * group_dp]
    line = lax.broadcasted_iota(jnp.int32, final.shape, 0)
    final = jnp.where(line < final_lines, final, 0.0)
    squares = jnp.sum(jnp.sum(final * final, axis=1, keepdims=True), axis=0, keepdims=True)
    total = jnp.sum(gathered[...], axis=0) + squares
    out_ref[...] = jnp.where(line < final_lines, final, total)


def norm_call(ident, last, final_lines):
    group_mod, group_dp = lax.axis_size("mod"), lax.axis_size("dp")
    size = group_mod * group_dp
    dma = pltpu.SemaphoreType.DMA
    return pl.pallas_call(
        functools.partial(norm_kernel, group_mod, group_dp, final_lines),
        out_shape=jax.ShapeDtypeStruct(last.shape, last.dtype),
        in_specs=[pl.BlockSpec(memory_space=pltpu.VMEM)],
        out_specs=pl.BlockSpec(memory_space=pltpu.VMEM),
        scratch_shapes=[
            pltpu.VMEM((size,) + last.shape, last.dtype),
            dma((size,)),
            dma((size,)),
            dma((1,)),
        ],
        compiler_params=pltpu.CompilerParams(collective_id=ident, has_side_effects=True),
        name="norm",
    )(last)


GROUP_SEQS = 4


def wide_table(table_ref, tokens, width):
    table = table_ref[...]
    table = jnp.concatenate([table] * (tokens // table.shape[0]), axis=0)
    return jnp.concatenate([table] * (width // table.shape[1]), axis=1)


def turned(values, cosine, sine):
    width = values.shape[-1]
    half = HEAD_DIM // 2
    lane = lax.broadcasted_iota(jnp.int32, values.shape, 1)
    other = jnp.where(
        lane % HEAD_DIM < half,
        pltpu.roll(values, width - half, 1),
        pltpu.roll(values, half, 1),
    )
    return values * cosine + other * sine


def head_spread(values, heads):
    rows, width = values.shape
    lane = lax.broadcasted_iota(jnp.int32, (heads, rows, width), 2)
    head = lax.broadcasted_iota(jnp.int32, (heads, rows, width), 0)
    return jnp.where(lane // HEAD_DIM == head, values[None], jnp.zeros((), values.dtype))


def head_fold(values, heads):
    rows, width = values.shape
    values = values.reshape(heads, rows // heads, width)
    lane = lax.broadcasted_iota(jnp.int32, values.shape, 2)
    head = lax.broadcasted_iota(jnp.int32, values.shape, 0)
    return jnp.sum(jnp.where(lane // HEAD_DIM == head, values, 0.0), axis=0)


def attention_parts(length, spots_ref, mixed_ref, cosine_ref, sine_ref):
    tokens, width = mixed_ref.shape[0], mixed_ref.shape[1] // 3
    heads = width // HEAD_DIM
    cosine = wide_table(cosine_ref, tokens, width)
    sine = wide_table(sine_ref, tokens, width)
    spot = spots_ref[...]
    key = lax.broadcasted_iota(jnp.int32, (spot.shape[0], tokens), 1)
    chosen = key == spot
    seen = (key <= spot) & (key >= spot - spot % length)
    queries = turned(mixed_ref[:, :width], cosine, sine).astype(jnp.bfloat16)
    queries = product(chosen.astype(jnp.bfloat16), queries)
    queries = head_spread(queries, heads).reshape(-1, width).astype(jnp.bfloat16)
    keys_in = turned(mixed_ref[:, width : 2 * width], cosine, sine).astype(jnp.bfloat16)
    values = mixed_ref[:, 2 * width :].astype(jnp.bfloat16)
    raw = right_product(queries, keys_in).reshape(heads, -1, tokens)
    scores = jnp.where(seen[None], raw * HEAD_DIM ** (-0.5), -1e30).reshape(-1, tokens)
    top = jnp.max(scores, axis=1, keepdims=True)
    terms = jnp.exp(scores - top)
    chances = terms / jnp.sum(terms, axis=1, keepdims=True)
    return chosen, queries, keys_in, values, chances, cosine, sine


def attention_kernel(
    length, spots_ref, mixed_ref, inputs_ref, cosine_ref, sine_ref, heads_ref, picked_ref
):
    heads = inputs_ref.shape[1] // HEAD_DIM
    chosen, _, _, values, chances, _, _ = attention_parts(
        length, spots_ref, mixed_ref, cosine_ref, sine_ref
    )
    spread = product(chances.astype(jnp.bfloat16), values)
    heads_ref[...] = head_fold(spread, heads).astype(jnp.bfloat16)
    picked_ref[...] = product(chosen.astype(jnp.bfloat16), inputs_ref[...])


def attention_back_kernel(
    length, spots_ref, mixed_ref, grad_ref, cosine_ref, sine_ref, out_ref
):
    width = grad_ref.shape[1]
    heads = width // HEAD_DIM
    chosen, queries, keys_in, values, chances, cosine, sine = attention_parts(
        length, spots_ref, mixed_ref, cosine_ref, sine_ref
    )
    grad_heads = head_spread(grad_ref[...].astype(jnp.float32), heads)
    grad_heads = grad_heads.reshape(-1, width).astype(jnp.bfloat16)
    grad_values = left_product(chances.astype(jnp.bfloat16), grad_heads)
    grad_chances = right_product(grad_heads, values)
    delta = jnp.sum(chances * grad_chances, axis=1, keepdims=True)
    grad_raw = (chances * (grad_chances - delta) * HEAD_DIM ** (-0.5)).astype(jnp.bfloat16)
    grad_queries = head_fold(product(grad_raw, keys_in), heads)
    grad_queries = lax.dot_general(
        chosen.astype(jnp.float32),
        grad_queries,
        (((0,), (0,)), ((), ())),
        precision=lax.Precision.HIGHEST,
        preferred_element_type=jnp.float32,
    )
    grad_keys = left_product(grad_raw, queries)
    out_ref[:, :width] = turned(grad_queries, cosine, -sine).astype(jnp.bfloat16)
    out_ref[:, width : 2 * width] = turned(grad_keys, cosine, -sine).astype(jnp.bfloat16)
    out_ref[:, 2 * width :] = grad_values.astype(jnp.bfloat16)


def attention_call(body, length, operands, tables, outs, name, microseconds):
    sequences = operands[1].shape[0] // length
    steps = sequences // math.gcd(GROUP_SEQS, sequences)

    def block(array):
        return pl.BlockSpec((array.shape[0] // steps, array.shape[1]), lambda i: (i, 0))

    fixed = [pl.BlockSpec(table.shape, lambda i: (0, 0)) for table in tables]
    return pl.pallas_call(
        functools.partial(body, length),
        grid=(steps,),
        out_shape=outs,
        in_specs=[block(array) for array in operands] + fixed,
        out_specs=[block(array) for array in outs],
        cost_estimate=pl.CostEstimate(
            flops=0, bytes_accessed=microseconds * 3_000_000, transcendentals=0
        ),
        name=name,
    )(*operands, *tables)


def square_sum(values):
    return jnp.sum(lax.optimization_barrier(jnp.sum(values * values, axis=0)))


def on_device(
    token_ids,
    targets,
    positions,
    loss_mask,
    paths,
    attend,
    output,
    widen,
    narrow,
    gains,
    table,
    final_gain,
    first_attend,
    first_output,
    first_widen,
    first_narrow,
    first_gains,
    first_table,
    first_final,
    second_attend,
    second_output,
    second_widen,
    second_narrow,
    second_gains,
    second_table,
    second_final,
):
    group_dp = lax.axis_size("dp")
    group_mod = lax.axis_size("mod")
    dp_place = lax.axis_index("dp")
    mod_place = lax.axis_index("mod")
    everyone = ("mod", "dp")
    place = mod_place * group_dp + dp_place
    sources = group_mod * group_dp
    micro, per_mod, length = token_ids.shape
    spots_seq = positions.shape[2]
    seq_dev = per_mod // group_dp
    shard_rows, width = table.shape
    heads = width // HEAD_DIM
    slots = micro * sources
    slots_local = slots // group_dp
    low = jnp.bfloat16

    mixing = lax.all_gather(
        jnp.concatenate([attend[0], output[0]], axis=1).astype(low), "dp", axis=0, tiled=True
    )
    attend_low, output_low = mixing[:, : 3 * width], mixing[:, 3 * width :]
    hidden = narrow.shape[1]
    widen_low = jnp.stack(
        [widen[0, :, i * hidden : (i + 1) * hidden].astype(low) for i in range(group_dp)]
    )
    widen_low = lax.all_to_all(widen_low, "dp", split_axis=0, concat_axis=0, tiled=True)
    widen_low = widen_low.reshape(width, hidden)
    narrow_low = narrow[0].astype(low)
    table_low = table.astype(low)

    fields = jnp.concatenate(
        [token_ids, positions, targets, loss_mask, paths[..., None]], axis=-1
    )
    fields, gain_parts, final_parts = exchange(
        0,
        (("mod",), fields.reshape(micro * per_mod, -1), True),
        (("dp",), jnp.broadcast_to(gains.astype(low), (16, gains.shape[1])), True),
        (("mod",), jnp.broadcast_to(final_gain.astype(low)[None], (16, final_gain.shape[0])), True),
    )
    own_gains = gain_parts[:, 0].reshape(-1).astype(jnp.float32)
    gain_one, gain_two = own_gains[:width], own_gains[width:]
    gain_final = final_parts[:, 0].reshape(-1).astype(jnp.float32)
    fields = fields.reshape(group_mod, micro, per_mod, -1).transpose(1, 0, 2, 3)
    fields = fields.reshape(slots, seq_dev, -1)
    own = lax.dynamic_slice_in_dim(fields, dp_place * slots_local, slots_local)
    own_match = own[..., -1] == mod_place
    own = jnp.sum(jnp.where(own_match[..., None], own[..., : length + spots_seq], 0), axis=1)
    own_tokens = own[:, :length].reshape(-1)
    spots = own[:, length:]
    held = jnp.repeat(jnp.any(own_match, axis=1), length)
    match = fields[None, ..., -1] == jnp.arange(group_mod, dtype=jnp.int32)[:, None, None]
    scoring = jnp.sum(
        jnp.where(match[..., None], fields[None, ..., length + spots_seq : -1], 0), axis=2
    )
    wanted = scoring[..., :spots_seq].reshape(-1)
    counted = scoring[..., spots_seq:].reshape(-1).astype(jnp.float32)
    count_total = jnp.sum(counted)

    shard = own_tokens // shard_rows
    row = own_tokens % shard_rows
    key = jnp.where(held, own_tokens, -1)
    order = jnp.arange(key.shape[0], dtype=jnp.int32)
    repeated = jnp.any((key[:, None] == key[None, :]) & (order[None, :] < order[:, None]), axis=1)
    leading = held & ~repeated
    rank = jnp.sum(
        (
            leading[None, :] & (shard[None, :] == shard[:, None]) & (key[None, :] < key[:, None])
        ).astype(jnp.int32),
        axis=1,
    )
    expected = -(-slots_local * length // sources)
    cap = -(-3 * expected // 16) * 8
    cap = min(max(cap, 16), -(-shard_rows // 8) * 8, 112)
    own_rounds = jnp.max(jnp.where(leading, rank // cap, 0)) + 1

    def ask(turn):
        slot = rank - turn * cap
        inside = held & (slot >= 0) & (slot < cap)
        slot = jnp.where(inside, shard * cap + slot, -1)
        asked = jnp.sum(
            jnp.where(
                leading[None, :]
                & (slot[None, :] == jnp.arange(sources * cap, dtype=jnp.int32)[:, None]),
                row[None, :] + 1,
                0,
            ),
            axis=1,
        ).reshape(sources, cap)
        return slot, asked

    slot, asked = ask(0)
    message = jnp.concatenate(
        [asked, jnp.broadcast_to(own_rounds, (sources, 128 - cap))], axis=1
    )
    message = exchange(
        1, (everyone, jnp.broadcast_to(message[:, None], (sources, 8, 128)), False)
    )
    rounds = jnp.max(message[:, 0, cap])
    spread = one_hot(slot, sources * cap)
    pick = one_hot(message[:, 0, :cap].reshape(-1) - 1, shard_rows)

    def other_plan(turn):
        slot, asked = ask(turn)
        asked = lax.all_to_all(asked, everyone, split_axis=0, concat_axis=0, tiled=True)
        return one_hot(slot, sources * cap), one_hot(asked.reshape(-1) - 1, shard_rows)

    def other_rows(state):
        turn, rows = state
        spread, pick = other_plan(turn)
        sent = product(pick, table_low).astype(low).reshape(sources, cap, width)
        got = lax.all_to_all(sent, everyone, split_axis=0, concat_axis=0, tiled=True)
        return turn + 1, rows + product(spread, got.reshape(-1, width)).astype(low)

    sent = product(pick, table_low).astype(low).reshape(sources, cap, width)
    got = exchange(2, (everyone, sent, False))
    inputs = product(spread, got.reshape(-1, width)).astype(low)
    inputs = lax.while_loop(
        lambda state: state[0] < rounds, other_rows, (jnp.int32(1), inputs)
    )[1]

    group = math.gcd(GROUP_SEQS, slots_local)
    tables = rotary_tables(length)
    flat_spots = spots + (jnp.arange(slots_local, dtype=jnp.int32) % group)[:, None] * length
    flat_spots = flat_spots.reshape(-1, 1)
    inputs_wide = inputs.astype(jnp.float32)
    normed_one = lax.optimization_barrier(rms_scale(inputs_wide, gain_one).astype(low))
    mixed = product(normed_one, attend_low)
    picked_rows = slots_local * spots_seq
    heads_out, picked_inputs = attention_call(
        attention_kernel,
        length,
        (flat_spots, mixed, inputs),
        tables,
        [
            jax.ShapeDtypeStruct((picked_rows, width), low),
            jax.ShapeDtypeStruct((picked_rows, width), jnp.float32),
        ],
        "attention",
        7,
    )
    middle = picked_inputs + product(heads_out, output_low)

    def sum_parts(ident, parts):
        parts = parts.astype(low).reshape(group_dp, picked_rows, width)
        return jnp.sum(exchange(ident, (("dp",), parts, False)).astype(jnp.float32), axis=0)

    normed_two = rms_scale(middle, gain_two).astype(low)
    normed_all = exchange(3, (("dp",), normed_two, True)).reshape(-1, width)
    upper = product(normed_all, widen_low)
    gelu = lambda value: jax.nn.gelu(value, approximate=True)
    activated = gelu(upper).astype(low)
    lifted = sum_parts(4, product(activated, narrow_low))
    returned = (middle + lifted).astype(low).astype(jnp.float32)

    final, final_back = jax.vjp(rms_scale, returned, gain_final)
    scored = gather_rows(12, final.astype(low))
    target_row = wanted - place * shard_rows
    stats, logits = scores_call(scored, table_low, target_row, picked_rows)
    totals = totals_call(5, stats)
    log_total = totals[:, 0].reshape(-1)
    loss_total = jnp.sum(counted * (log_total - totals[:, 1].reshape(-1)))
    hits = target_row[None, :] == jnp.arange(shard_rows, dtype=jnp.int32)[:, None]
    grad_logits = (
        counted[None] * (jnp.exp(logits - log_total[None]) - hits.astype(jnp.float32))
    ).astype(low)
    grad_logits = lax.optimization_barrier(grad_logits)
    grad_picked = scatter_rows(13, left_product(grad_logits, table_low).astype(low))

    grad_returned, grad_final = final_back(grad_picked)
    incoming = grad_returned.astype(low)
    incoming_all = exchange(7, (("dp",), incoming, True)).reshape(-1, width)
    grad_narrow = left_product(activated, incoming_all)
    grad_act = right_product(incoming_all, narrow_low)
    grad_upper = jax.vjp(gelu, upper)[1](grad_act)[0].astype(low)
    grad_widen = left_product(normed_all, grad_upper).astype(low)
    grad_widen = lax.all_to_all(
        grad_widen.reshape(group_dp, -1, hidden), "dp", split_axis=0, concat_axis=0, tiled=True
    )
    grad_normed_two = sum_parts(8, right_product(grad_upper, widen_low))
    grad_middle, grad_gain_two = jax.vjp(rms_scale, middle, gain_two)[1](grad_normed_two)
    grad_middle = grad_middle + incoming.astype(jnp.float32)

    branch_grad = grad_middle.astype(low)
    grad_output = lax.psum_scatter(
        left_product(heads_out, branch_grad).astype(low), "dp", scatter_dimension=0, tiled=True
    ).astype(jnp.float32)
    grad_heads = right_product(branch_grad, output_low).astype(low)
    (grad_mixed,) = attention_call(
        attention_back_kernel,
        length,
        (flat_spots, mixed, grad_heads),
        tables,
        [jax.ShapeDtypeStruct(mixed.shape, low)],
        "attention_back",
        12,
    )
    grad_widen, grad_mixed = lax.optimization_barrier((grad_widen, grad_mixed))
    grad_attend = left_product(normed_one, grad_mixed)
    grad_normed = right_product(grad_mixed, attend_low)
    grad_inputs, grad_gain_one = jax.vjp(rms_scale, inputs_wide, gain_one)[1](grad_normed)
    here = spots[:, :, None] == jnp.arange(length, dtype=jnp.int32)
    grad_skip = jnp.sum(
        jnp.where(
            here[..., None], grad_middle.reshape(slots_local, spots_seq, 1, width), 0.0
        ),
        axis=1,
    ).reshape(-1, width)
    leaving = (grad_skip + grad_inputs).astype(low)

    grad_attend = lax.psum_scatter(
        grad_attend.astype(low), "dp", scatter_dimension=0, tiled=True
    ).astype(jnp.float32)

    def other_grads(state):
        turn, total = state
        spread, pick = other_plan(turn)
        sent = left_product(spread, leaving).astype(low).reshape(sources, cap, width)
        got = lax.all_to_all(sent, everyone, split_axis=0, concat_axis=0, tiled=True)
        return turn + 1, total + left_product(pick, got.reshape(-1, width))

    given = left_product(spread, leaving).astype(low).reshape(sources, cap, width)
    gain_grads = jnp.concatenate([grad_gain_one, grad_gain_two, grad_final])
    gain_grads = jnp.pad(gain_grads.reshape(-1, 128), ((0, -gain_grads.shape[0] // 128 % 8), (0, 0)))
    given, gain_grads = exchange(
        9, (everyone, given, False), (("dp",), gain_grads, True)
    )
    given, scored = lax.optimization_barrier((given, scored))
    table_grad = product(grad_logits, scored)
    table_grad = table_grad + left_product(pick, given.reshape(-1, width))
    table_grad = lax.while_loop(
        lambda state: state[0] < rounds, other_grads, (jnp.int32(1), table_grad)
    )[1]
    gain_grads = jnp.sum(gain_grads, axis=0).reshape(-1)
    own_gain_grads = gain_grads[: 2 * width]
    final_rows = gain_grads[2 * width : 3 * width].reshape(-1, 128)
    gain_part = gains.shape[1]
    grad_gains = lax.dynamic_slice_in_dim(own_gain_grads, dp_place * gain_part, gain_part)
    widen_squares = square_sum(grad_widen.astype(jnp.float32).reshape(-1, hidden))
    grad_widen = side_by_side(grad_widen)
    matrix_grads = (grad_attend[None], grad_output[None], grad_widen[None], grad_narrow[None])
    squares = sum(square_sum(g) for g in (grad_attend, grad_output, grad_narrow, table_grad))
    squares = squares + widen_squares
    squares = squares + jnp.sum(grad_gains * grad_gains)
    last = jnp.concatenate(
        [final_rows, jnp.broadcast_to(squares, (16 - final_rows.shape[0] % 8 - 8, 128))], axis=0
    )
    final_count = final_rows.shape[0]
    last = norm_call(11, last, final_count)
    grad_final = last[:final_count].reshape(-1)
    squares = last[final_count, 0]
    final_part = final_gain.shape[0]
    grad_final = lax.dynamic_slice_in_dim(grad_final, mod_place * final_part, final_part)
    gradient_norm = jnp.sqrt(squares) / count_total
    factor = CLIP_LIMIT / jnp.maximum(gradient_norm, CLIP_LIMIT) / count_total
    params = (attend, output, widen, narrow, gains, table, final_gain)
    grads = matrix_grads + (grad_gains[None], table_grad, grad_final)
    firsts = (
        first_attend,
        first_output,
        first_widen,
        first_narrow,
        first_gains,
        first_table,
        first_final,
    )
    seconds = (
        second_attend,
        second_output,
        second_widen,
        second_narrow,
        second_gains,
        second_table,
        second_final,
    )
    rates = (RATE_MATRIX, RATE_MATRIX, RATE_MATRIX, RATE_MATRIX, RATE_GAIN, RATE_MATRIX, RATE_GAIN)
    decays = (DECAY_MATRIX, DECAY_MATRIX, DECAY_MATRIX, DECAY_MATRIX, 0.0, DECAY_MATRIX, 0.0)
    updated = [
        adam_step(w, g * factor, f, s, r, c)
        for w, g, f, s, r, c in zip(params, grads, firsts, seconds, rates, decays)
    ]
    return (
        loss_total / count_total,
        gradient_norm,
        *(entry[0] for entry in updated),
        *(entry[1] for entry in updated),
        *(entry[2] for entry in updated),
    )


def solution(mesh):
    placed = (
        P(None, "mod", None),
        P(None, "mod", None),
        P(None, "mod", None),
        P(None, "mod", None),
        P(None, "mod"),
        P("mod", "dp", None),
        P("mod", "dp", None),
        P("mod", "dp", None),
        P("mod", "dp", None),
        P("mod", "dp"),
        P(("mod", "dp"), None),
        P("mod"),
        P("mod", "dp", None),
        P("mod", "dp", None),
        P("mod", "dp", None),
        P("mod", "dp", None),
        P("mod", "dp"),
        P(("mod", "dp"), None),
        P("mod"),
        P("mod", "dp", None),
        P("mod", "dp", None),
        P("mod", "dp", None),
        P("mod", "dp", None),
        P("mod", "dp"),
        P(("mod", "dp"), None),
        P("mod"),
    )
    return jax.shard_map(
        on_device,
        mesh=mesh,
        in_specs=placed,
        out_specs=(
            P(),
            P(),
            P("mod", "dp", None),
            P("mod", "dp", None),
            P("mod", "dp", None),
            P("mod", "dp", None),
            P("mod", "dp"),
            P(("mod", "dp"), None),
            P("mod"),
            P("mod", "dp", None),
            P("mod", "dp", None),
            P("mod", "dp", None),
            P("mod", "dp", None),
            P("mod", "dp"),
            P(("mod", "dp"), None),
            P("mod"),
            P("mod", "dp", None),
            P("mod", "dp", None),
            P("mod", "dp", None),
            P("mod", "dp", None),
            P("mod", "dp"),
            P(("mod", "dp"), None),
            P("mod"),
        ),
        check_vma=False,
    )
```
